32 devices in a mesh: dp: 4 (over z), row: 2 (over core), col: 4 (over y, x).
Axes of the slice: x: 2, y: 2, z: 4, core: 2. Of those that a mesh axis runs over, the one named last changes fastest.
Arguments:
- hidden: float32 [16384, 768], P(('dp', 'col'), 'row'), may hold values from -6 to 6
- lengths: int32 [8], P('dp'), may hold values from 512 to 2048, as said below
- inner_project: float32 [768, 2304], P(('row', 'dp'), 'col'), may hold values from -0.21875 to 0.21875
- inner_merge: float32 [768, 768], P(('col', 'dp'), 'row'), may hold values from -2 to 2
- inner_expand: float32 [768, 3072], P(('row', 'dp'), 'col'), may hold values from -0.21875 to 0.21875
- inner_shrink: float32 [3072, 768], P(('col', 'dp'), 'row'), may hold values from -0.109375 to 0.109375
- inner_norms: float32 [768, 4], P(('row', 'dp', 'col')), may hold values from 0.1 to 1.9
- outer_places: float32 [768, 16], P(('row', 'dp', 'col')), may hold values from -6 to 6
- outer_project: float32 [768, 2304], P(('row', 'dp'), 'col'), may hold values from -0.21875 to 0.21875
- outer_merge: float32 [768, 768], P(('col', 'dp'), 'row'), may hold values from -1.5 to 1.5
- outer_expand: float32 [768, 3072], P(('row', 'dp'), 'col'), may hold values from -0.21875 to 0.21875
- outer_shrink: float32 [3072, 768], P(('col', 'dp'), 'row'), may hold values from -0.109375 to 0.109375
- outer_norms: float32 [768, 4], P(('row', 'dp', 'col')), may hold values from 0.1 to 1.9
- out_grad: float32 [16384, 768], P(('dp', 'col'), 'row'), may hold values from -6 to 6
Outputs:
- layer_out: float32 [16384, 768], P(('dp', 'col'), 'row')
- input_grad: float32 [16384, 768], P(('dp', 'col'), 'row')
- inner_project_grad: float32 [768, 2304], P(('row', 'dp'), 'col')
- inner_merge_grad: float32 [768, 768], P(('col', 'dp'), 'row')
- inner_expand_grad: float32 [768, 3072], P(('row', 'dp'), 'col')
- inner_shrink_grad: float32 [3072, 768], P(('col', 'dp'), 'row')
- inner_norms_grad: float32 [768, 4], P(('row', 'dp', 'col'))
- outer_places_grad: float32 [768, 16], P(('row', 'dp', 'col'))
- outer_project_grad: float32 [768, 2304], P(('row', 'dp'), 'col')
- outer_merge_grad: float32 [768, 768], P(('col', 'dp'), 'row')
- outer_expand_grad: float32 [768, 3072], P(('row', 'dp'), 'col')
- outer_shrink_grad: float32 [3072, 768], P(('col', 'dp'), 'row')
- outer_norms_grad: float32 [768, 4], P(('row', 'dp', 'col'))
The draws below stay inside these ranges and needn't reach their ends.
Inputs may be any that keep to these rules, and one draw needn't show every extreme that they name: A sequence's valid slots are its first lengths slots; in every draw some sequence is full (2048) and some has 512.
All inputs are finite; a program needn't handle non-finite values.
Results may differ from the reference program's by a relative error of at most 0.04.
Values may be sent and summed in bfloat16 or wider, within the bound.
No kernel may reach another device: no remote copies, remote signals or barrier semaphores. Data moves between devices by JAX's collectives and lax.ppermute only.
A program may use at most 192 MiB of HBM per device.

```python
import jax
import jax.numpy as jnp
from jax import lax

D = 768
HEADS = 12
HDIM = 64
FF = 3072
SEG = 128
SEQ_LEN = 2048
NSEG = 16
SEQS = 8
TOKENS = 16384


def draw_lengths(key, part):
    first, second, third = jax.random.split(key, 3)
    base = jax.random.randint(first, (SEQS,), SEQ_LEN // 4, SEQ_LEN + 1)
    full_at = jax.random.randint(second, (), 0, SEQS)
    short_at = (full_at + 1 + jax.random.randint(third, (), 0, SEQS - 1)) % SEQS
    spots = jnp.arange(SEQS)
    base = jnp.where(spots == full_at, SEQ_LEN, base)
    return jnp.where(spots == short_at, SEQ_LEN // 4, base).astype(jnp.int32)


def levels(stream_key, dims, pieces, smallest, high):
    def one(axis_at, shards_of):
        draws = jax.random.uniform(jax.random.fold_in(jax.random.fold_in(stream_key, 6), axis_at), (shards_of,), jnp.float32, smallest / len(pieces), high / len(pieces))
        return jnp.repeat(jnp.exp(draws), dims[axis_at] // shards_of).reshape((-1,) + (1,) * (len(dims) - axis_at - 1))

    factor_of = one(*pieces[0])
    for cut in pieces[1:]:
        factor_of = factor_of * one(*cut)
    return factor_of


def normal_values(stream_key, dims, scale, most, shards=(), kind=jnp.bfloat16):
    values = scale * jax.random.normal(stream_key, dims, jnp.float32)
    if shards:
        values = values * levels(stream_key, dims, shards, -0.22, 0.18)
    return jnp.clip(values, -most, most).astype(kind)


def setup_inputs(seed: int = 0) -> dict:
    key_of = jax.random.split(jax.random.key(seed), 15)
    return {
        "hidden": normal_values(key_of[0], (TOKENS, D), 1.0, 6.0, ((0, 16), (1, 2)), jnp.float32),
        "lengths": draw_lengths(jax.random.fold_in(key_of[14], 71), 0),
        "inner_project": normal_values(key_of[2], (D, 3 * D), D ** -0.5, 0.21875, ((0, 8), (1, 4)), jnp.float32),
        "inner_merge": normal_values(key_of[3], (D, D), (HDIM // 8) ** -0.5, 2.0, ((0, 16), (1, 2)), jnp.float32),
        "inner_expand": normal_values(key_of[4], (D, FF), D ** -0.5, 0.21875, ((0, 8), (1, 4)), jnp.float32),
        "inner_shrink": normal_values(key_of[5], (FF, D), FF ** -0.5, 0.109375, ((0, 16), (1, 2)), jnp.float32),
        "inner_norms": jnp.clip(1.0 + 0.18 * jax.random.normal(key_of[6], (D, 4), jnp.float32), 0.1, 1.9),
        "outer_places": normal_values(key_of[7], (D, NSEG), 1.0, 6.0, ((0, 32),), jnp.float32),
        "outer_project": normal_values(key_of[8], (D, 3 * D), D ** -0.5, 0.21875, ((0, 8), (1, 4)), jnp.float32),
        "outer_merge": normal_values(key_of[9], (D, D), (HDIM // 4) ** -0.5, 1.5, ((0, 16), (1, 2)), jnp.float32),
        "outer_expand": normal_values(key_of[10], (D, FF), D ** -0.5, 0.21875, ((0, 8), (1, 4)), jnp.float32),
        "outer_shrink": normal_values(key_of[11], (FF, D), FF ** -0.5, 0.109375, ((0, 16), (1, 2)), jnp.float32),
        "outer_norms": jnp.clip(1.0 + 0.18 * jax.random.normal(key_of[12], (D, 4), jnp.float32), 0.1, 1.9),
        "out_grad": normal_values(key_of[13], (TOKENS, D), 1.0, 6.0, ((0, 16), (1, 2)), jnp.float32),
    }


@jax.custom_vjp
def low(v):
    return lax.optimization_barrier(v.astype(jnp.bfloat16)).astype(jnp.float32)

@jax.custom_vjp
def low_back(v):
    return v

def low_keep(v):
    return (low(v), None)

def low_pass(kept, grad):
    return (grad,)

def back_keep(v):
    return (v, None)

def back_low(kept, grad):
    return (low(grad),)
low.defvjp(low_keep, low_pass)
low_back.defvjp(back_keep, back_low)
highest = lax.Precision.HIGHEST
epsilon = 1e-06

def product(left, right):
    return jnp.dot(left, right, precision=highest, preferred_element_type=jnp.float32)

def normalize(value, gain, shift):
    average = lax.optimization_barrier(jnp.mean(value, axis=-1, keepdims=True))
    centred = value - average
    spread = lax.optimization_barrier(jnp.mean(centred * centred, axis=-1, keepdims=True))
    return centred * lax.rsqrt(spread + epsilon) * gain + shift

def attention(qkv, group, keep):
    count = qkv.shape[0]
    parts = qkv.reshape(count // group, group, HEADS, 3, HDIM)
    query = parts[:, :, :, 0]
    key_part = parts[:, :, :, 1]
    value_part = parts[:, :, :, 2]
    scores = low_back(jnp.einsum('gqhd,gkhd->ghqk', query, key_part, precision=highest) * HDIM ** (-0.5))
    allowed = keep.reshape(count // group, 1, 1, group) > 0.5
    scores = jnp.where(allowed, scores, -1000000000.0)
    topmost = lax.optimization_barrier(jnp.max(scores, axis=-1, keepdims=True))
    expo = jnp.exp(scores - topmost)
    probs = low(expo / lax.optimization_barrier(jnp.sum(expo, axis=-1, keepdims=True)))
    mixed = jnp.einsum('ghqk,gkhd->gqhd', probs, value_part, precision=highest)
    return mixed.reshape(count, D)

def block(value, weights, norms, group, keep):
    project, merge, expand, shrink = weights
    qkv = low(low_back(product(low(value), low(project))))
    mixed = low(low_back(attention(qkv, group, keep)))
    attended = low_back(product(mixed, low(merge)))
    hid = normalize(value + attended, norms[:, 0], norms[:, 1])
    pre = low_back(product(low(hid), low(expand)))
    active = low(jax.nn.gelu(pre, approximate=False))
    ffn = low_back(product(active, low(shrink)))
    return normalize(hid + ffn, norms[:, 2], norms[:, 3])

def layer(hidden, params, valid, keep_tok, keep_seg):
    inner_project, inner_merge, inner_expand, inner_shrink, inner_norms, outer_places, outer_project, outer_merge, outer_expand, outer_shrink, outer_norms = params
    count = hidden.shape[0]
    inner = block(hidden, (inner_project, inner_merge, inner_expand, inner_shrink), inner_norms, SEG, keep_tok)
    grid = inner.reshape(count // SEG, SEG, D)
    heads_in = grid[:, 0] + jnp.tile(outer_places.T, (count // SEQ_LEN, 1))
    outer = block(heads_in, (outer_project, outer_merge, outer_expand, outer_shrink), outer_norms, NSEG, keep_seg)
    joined = jnp.concatenate([outer[:, None], grid[:, 1:]], axis=1).reshape(count, D)
    return joined * valid[:, None]

def reference(hidden, lengths, inner_project, inner_merge, inner_expand, inner_shrink, inner_norms, outer_places, outer_project, outer_merge, outer_expand, outer_shrink, outer_norms, out_grad):
    params = (inner_project, inner_merge, inner_expand, inner_shrink, inner_norms, outer_places, outer_project, outer_merge, outer_expand, outer_shrink, outer_norms)
    width = 2 * SEQ_LEN
    turns = SEQS // 2
    items = (hidden.reshape(turns, width, D), out_grad.reshape(turns, width, D), lengths.reshape(turns, 2))

    def step(totals, item):
        block_in, block_grad, lens = item
        place = jnp.arange(SEQ_LEN, dtype=jnp.int32)
        inside = place[None, :] < lens[:, None]
        valid = inside.reshape(width).astype(jnp.float32)
        keep_tok = (inside | (place[None, :] % SEG == 0)).reshape(width).astype(jnp.float32)
        starts = jnp.arange(NSEG, dtype=jnp.int32) * SEG
        keep_seg = (starts[None, :] < lens[:, None]).reshape(2 * NSEG).astype(jnp.float32)

        def forward(value, *weights):
            return layer(value, weights, valid, keep_tok, keep_seg)
        result, pull = jax.vjp(forward, block_in, *params)
        grads = pull(block_grad)
        totals = tuple((total + grad for total, grad in zip(totals, grads[1:])))
        return (totals, (result, grads[0]))
    start = tuple((jnp.zeros_like(param) for param in params))
    totals, (results, ingrads) = lax.scan(step, start, items)
    return (results.reshape(TOKENS, D), ingrads.reshape(TOKENS, D), totals[0], totals[1], totals[2], totals[3], totals[4], totals[5], totals[6], totals[7], totals[8], totals[9], totals[10])
```

```python
import jax
import jax.numpy as jnp
from jax import lax
from jax.sharding import PartitionSpec as P

HDIM = 64
SEG = 128
SEQ_LEN = 2048
NSEG = 16
epsilon = 1e-06
highest = lax.Precision.HIGHEST
low_type = jnp.bfloat16


def dot(left, right):
    return jnp.dot(left, right, preferred_element_type=jnp.float32)


def dot_t(left, right):
    return lax.dot_general(
        left, right, (((1,), (1,)), ((), ())), preferred_element_type=jnp.float32
    )


def dot_rows(left, right):
    return lax.dot_general(
        left, right, (((0,), (0,)), ((), ())), preferred_element_type=jnp.float32
    )


def row_swap(value):
    return lax.ppermute(value, "row", [(0, 1), (1, 0)])


def col_swap(value, mask):
    return lax.ppermute(value, "col", [(i, i ^ mask) for i in range(lax.axis_size("col"))])


def dp_shift(value, step):
    count = lax.axis_size("dp")
    return lax.ppermute(value, "dp", [(i, (i + step) % count) for i in range(count)])


def dp_gather(value):
    count = lax.axis_size("dp")
    if count > 4:
        return lax.all_gather(value, "dp", axis=0, tiled=True)
    place = lax.axis_index("dp")
    whole = jnp.zeros((count,) + value.shape, value.dtype)
    whole = lax.dynamic_update_index_in_dim(whole, value, place, 0)
    for step in range(1, count):
        whole = lax.dynamic_update_index_in_dim(
            whole, dp_shift(value, step), (place - step) % count, 0
        )
    return whole.reshape((-1,) + value.shape[1:])


def dp_scatter_sum(value):
    count = lax.axis_size("dp")
    if count > 4:
        return lax.psum_scatter(value, "dp", scatter_dimension=0, tiled=True)
    place = lax.axis_index("dp")
    parts = value.reshape((count, -1) + value.shape[1:])
    total = lax.dynamic_index_in_dim(parts, place, 0, False)
    for step in range(1, count):
        piece = lax.dynamic_index_in_dim(parts, (place + step) % count, 0, False)
        total = total + dp_shift(piece.astype(low_type), step).astype(jnp.float32)
    return total


def gather_plane(shard, through):
    own = dp_gather(shard.astype(low_type))
    side = col_swap(own, 1)
    over = col_swap(own, 2)
    far = col_swap(over, 1) if through == 1 else col_swap(side, 2)
    mine = (own, side, over, far)
    return (mine, tuple(row_swap(block) for block in mine))


def gather_pair(shard):
    own = dp_gather(shard.astype(low_type))
    mine = (own, col_swap(own, 2))
    return (mine, tuple(row_swap(block) for block in mine))


def first_matrix(blocks):
    return jnp.concatenate([jnp.concatenate(half, axis=1) for half in blocks], axis=0)


def second_matrix(blocks):
    return jnp.concatenate([jnp.concatenate(half, axis=0) for half in blocks], axis=1)


def plane_sum(sums, through):
    other = 3 - through
    own = sums[0] + col_swap(sums[through].astype(low_type), through).astype(jnp.float32)
    onward = sums[other] + col_swap(sums[3].astype(low_type), through).astype(jnp.float32)
    return own + col_swap(onward.astype(low_type), other).astype(jnp.float32)


def scatter_grad(mine, theirs, through):
    sums = [
        block.astype(jnp.float32) + row_swap(sent).astype(jnp.float32)
        for block, sent in zip(mine, theirs)
    ]
    return dp_scatter_sum(plane_sum(sums, through))


def normalize(value, gain, shift):
    average = jnp.mean(value, axis=-1, keepdims=True)
    centred = value - average
    inverse = lax.rsqrt(jnp.mean(centred * centred, axis=-1, keepdims=True) + epsilon)
    unit = centred * inverse
    return (unit * gain + shift, unit, inverse)


def norm_backward(upstream, unit, inverse, gain):
    scaled = upstream * gain
    centre = jnp.mean(scaled, axis=-1, keepdims=True)
    slope = jnp.mean(scaled * unit, axis=-1, keepdims=True)
    result = inverse * (scaled - centre - unit * slope)
    return (result, jnp.sum(upstream * unit, 0), jnp.sum(upstream, 0))


def split_heads(qkv_low, group):
    count = qkv_low.shape[0]
    heads = qkv_low.shape[1] // (3 * HDIM)
    parts = qkv_low.reshape(count // group, group, heads, 3, HDIM)
    return (parts[:, :, :, 0], parts[:, :, :, 1], parts[:, :, :, 2])


def masked_scores(query, key_part, group, keep):
    scores = jnp.einsum(
        "gqhd,gkhd->ghqk", query, key_part, preferred_element_type=jnp.float32
    ) * HDIM ** (-0.5)
    allowed = keep.reshape(-1, 1, 1, group) > 0.5
    return jnp.where(allowed, scores, -1000000000.0)


def attend(qkv_low, group, keep):
    query, key_part, value_part = split_heads(qkv_low, group)
    scores = masked_scores(query, key_part, group, keep)
    topmost = jnp.max(scores, axis=-1, keepdims=True)
    expo = jnp.exp(scores - topmost)
    total = jnp.sum(expo, axis=-1, keepdims=True)
    probs = (expo / total).astype(low_type)
    mixed = jnp.einsum("ghqk,gkhd->gqhd", probs, value_part, preferred_element_type=jnp.float32)
    return (mixed.reshape(qkv_low.shape[0], -1), topmost + jnp.log(total))


def attend_backward(upstream, qkv_low, logsum, group, keep):
    query, key_part, value_part = split_heads(qkv_low, group)
    count = qkv_low.shape[0]
    incoming = upstream.reshape(query.shape)
    probs = jnp.exp(masked_scores(query, key_part, group, keep) - logsum)
    probs_low = probs.astype(low_type)
    dprobs = jnp.einsum("gqhd,gkhd->ghqk", incoming, value_part, preferred_element_type=jnp.float32)
    dvalue = jnp.einsum("ghqk,gqhd->gkhd", probs_low, incoming, preferred_element_type=jnp.float32)
    centre = jnp.sum(dprobs * probs, axis=-1, keepdims=True)
    dscore = (probs * (dprobs - centre)).astype(low_type)
    dquery = jnp.einsum(
        "ghqk,gkhd->gqhd", dscore, key_part, preferred_element_type=jnp.float32
    ) * HDIM ** (-0.5)
    dkey = jnp.einsum(
        "ghqk,gqhd->gkhd", dscore, query, preferred_element_type=jnp.float32
    ) * HDIM ** (-0.5)
    return jnp.stack([dquery, dkey, dvalue], axis=3).reshape(count, -1)


def exact_gelu(value):
    return jax.nn.gelu(value, approximate=False)


def block_forward(value, weights, norms, group, keep, join):
    project, merge, expand, shrink = weights
    value_low = value.astype(low_type)
    qkv_low = dot(value_low, project).astype(low_type)
    mixed, logsum = attend(qkv_low, group, keep)
    mixed = mixed.astype(low_type)
    attended = join(dot(mixed, merge))
    hid, unit_one, inverse_one = normalize(value + attended, norms[0], norms[1])
    hid_low = hid.astype(low_type)
    pre = dot(hid_low, expand)
    active = exact_gelu(pre).astype(low_type)
    ffn = join(dot(active, shrink))
    result, unit_two, inverse_two = normalize(hid + ffn, norms[2], norms[3])
    saved = (
        value_low,
        qkv_low,
        logsum,
        mixed,
        unit_one,
        inverse_one,
        hid_low,
        pre,
        active,
        unit_two,
        inverse_two,
    )
    return (result, saved)


def block_backward(upstream, saved, weights, norms, group, keep, join):
    project, merge, expand, shrink = weights
    value_low, qkv_low, logsum, mixed, unit_one, inverse_one = saved[:6]
    hid_low, pre, active, unit_two, inverse_two = saved[6:]
    dsecond, gain_two, shift_two = norm_backward(upstream, unit_two, inverse_two, norms[2])
    dffn = dsecond.astype(low_type)
    dactive = dot_t(dffn, shrink)
    dpre = jax.vjp(exact_gelu, pre)[1](dactive)[0].astype(low_type)
    dhid = dsecond + join(dot_t(dpre, expand))
    dfirst, gain_one, shift_one = norm_backward(dhid, unit_one, inverse_one, norms[0])
    datt = dfirst.astype(low_type)
    dmixed = dot_t(datt, merge).astype(low_type)
    dqkv = attend_backward(dmixed, qkv_low, logsum, group, keep).astype(low_type)
    dvalue = dfirst + join(dot_t(dqkv, project))
    pairs = ((value_low, dqkv), (mixed, datt), (hid_low, dpre), (active, dffn))
    return (dvalue, pairs, jnp.stack([gain_one, shift_one, gain_two, shift_two], axis=1))


def halves(value, axis):
    return jnp.split(value, 2, axis=axis)


def first_grad(pair, through):
    left, right = pair
    blocks = jnp.split(right, lax.axis_size("col"), axis=1)
    whole = [dot_rows(left, block).astype(low_type) for block in blocks]
    split = [halves(block, 0) for block in whole]
    return scatter_grad([s[0] for s in split], [s[1] for s in split], through)


def second_grad(pair, through):
    left, right = pair
    sides = [dot_rows(left, part).astype(low_type) for part in halves(right, 1)]
    count = lax.axis_size("col")
    return scatter_grad(jnp.split(sides[0], count, 0), jnp.split(sides[1], count, 0), through)


def to_tokens(value, row):
    parts = value.reshape((2, -1) + value.shape[1:])
    mine = lax.dynamic_index_in_dim(parts, row, 0, False)
    theirs = lax.dynamic_index_in_dim(parts, 1 - row, 0, False)
    return jnp.concatenate([mine, row_swap(theirs)], axis=1)


def to_features(value, row):
    mine, theirs = halves(value, 1)
    got = row_swap(theirs)
    first = jnp.where(row == 0, mine, got)
    second = jnp.where(row == 0, got, mine)
    return jnp.concatenate([first, second], axis=0)


def swap_features(value):
    first, second = halves(value, 1)
    return jnp.concatenate([second, first], axis=1)


def swap_rows(value):
    first, second = halves(value, 0)
    return jnp.concatenate([second, first], axis=0)


def local(
    hidden,
    lengths,
    inner_project,
    inner_merge,
    inner_expand,
    inner_shrink,
    inner_norms,
    outer_places,
    outer_project,
    outer_merge,
    outer_expand,
    outer_shrink,
    outer_norms,
    out_grad,
):
    dp_count, row_count, col_count = (lax.axis_size(name) for name in ("dp", "row", "col"))
    dp, row, col = (lax.axis_index(name) for name in ("dp", "row", "col"))
    everyone = ("dp", "row", "col")
    device_count = dp_count * row_count * col_count
    value = to_tokens(hidden, row)
    grad_in = to_tokens(out_grad, row)
    tokens, width = value.shape
    segs = tokens // SEG

    inner = (
        first_matrix(gather_plane(inner_project, 1)),
        second_matrix(gather_plane(inner_merge, 2)),
        first_matrix(gather_plane(inner_expand, 1)),
        second_matrix(gather_plane(inner_shrink, 2)),
    )
    outer = (
        first_matrix(gather_pair(outer_project)),
        second_matrix(gather_pair(outer_merge)),
        first_matrix(gather_pair(outer_expand)),
        second_matrix(gather_pair(outer_shrink)),
    )

    small = jnp.concatenate([inner_norms, outer_norms, outer_places], axis=1)
    small = lax.all_to_all(
        jnp.broadcast_to(small[None], (device_count,) + small.shape), everyone, 0, 0, tiled=True
    )
    small = small.reshape((dp_count, row_count, -1) + small.shape[2:])
    small = jnp.concatenate(
        [
            lax.dynamic_index_in_dim(small, row, 1, False).reshape(-1, small.shape[-1]),
            lax.dynamic_index_in_dim(small, 1 - row, 1, False).reshape(-1, small.shape[-1]),
        ],
        axis=0,
    )
    vectors = small.T
    inner_gains = vectors[0:4]
    outer_gains = vectors[4:8]
    places = vectors[8:]

    length = lax.dynamic_index_in_dim(lengths, col // 2, 0, False)
    half = col % 2
    seg_own = (half * 2 + row) * segs + jnp.arange(segs, dtype=jnp.int32)
    spot = (seg_own[:, None] * SEG + jnp.arange(SEG, dtype=jnp.int32)[None]).reshape(tokens)
    valid = (spot < length).astype(jnp.float32)
    keep_tok = ((spot < length) | (spot % SEG == 0)).astype(jnp.float32)
    seg_all = jnp.concatenate(
        [
            (h * 2 + r) * segs + jnp.arange(segs, dtype=jnp.int32)
            for h in (half, 1 - half)
            for r in (row, 1 - row)
        ]
    )
    keep_seg = (seg_all * SEG < length).astype(jnp.float32)
    one_hot = (seg_own[:, None] == jnp.arange(NSEG, dtype=jnp.int32)[None]).astype(jnp.float32)

    inner_out, inner_saved = block_forward(
        value, inner, inner_gains, SEG, keep_tok, lambda partial_sum: partial_sum
    )
    grid = inner_out.reshape(segs, SEG, width)
    masked_grad = (grad_in * valid[:, None]).reshape(segs, SEG, width)
    heads_in = grid[:, 0] + jnp.dot(
        one_hot, places, precision=highest, preferred_element_type=jnp.float32
    )
    rows = jnp.concatenate([heads_in, masked_grad[:, 0]], axis=0)
    rows = jnp.stack([rows, swap_features(row_swap(rows))]).reshape(2, 2, segs, width)
    rows = jnp.stack([rows, col_swap(rows, 1)])
    rows = rows.transpose(2, 0, 1, 3, 4).reshape(2, NSEG, width)

    def join(partial_sum):
        return partial_sum + swap_rows(col_swap(partial_sum, 1))

    outer_out, outer_saved = block_forward(rows[0], outer, outer_gains, NSEG, keep_seg, join)
    dheads, outer_pairs, outer_norm_grad = block_backward(
        rows[1], outer_saved, outer, outer_gains, NSEG, keep_seg, join
    )
    dheads = dheads[:segs]
    layer_out = (
        jnp.concatenate([outer_out[:segs, None], grid[:, 1:]], axis=1).reshape(tokens, width)
        * valid[:, None]
    )
    places_grad = jnp.dot(dheads.T, one_hot, precision=highest, preferred_element_type=jnp.float32)
    dinner = jnp.concatenate([dheads[:, None], masked_grad[:, 1:]], axis=1).reshape(tokens, width)
    input_grad, inner_pairs, inner_norm_grad = block_backward(
        dinner, inner_saved, inner, inner_gains, SEG, keep_tok, lambda partial_sum: partial_sum
    )
    inner_grads = (
        first_grad(inner_pairs[0], 1),
        second_grad(inner_pairs[1], 2),
        first_grad(inner_pairs[2], 1),
        second_grad(inner_pairs[3], 2),
    )

    (x_low, dqkv), (mixed, datt), (hid_low, dpre), (active, dffn) = outer_pairs
    shared = [halves(part, 1)[0] for part in (x_low, hid_low, datt, dffn)]
    own, over = zip(*(halves(part, 1) for part in (active, dpre, mixed, dqkv)))
    packed = jnp.concatenate(
        [
            jnp.concatenate(shared + list(own), axis=1),
            col_swap(jnp.concatenate(shared + list(over), axis=1), 2),
        ],
        axis=0,
    )
    if dp_count > 4:
        packed = lax.all_gather(packed, "dp", axis=0, tiled=True)
    else:
        packed = jnp.concatenate(
            [packed] + [dp_shift(packed, step) for step in range(1, dp_count)], axis=0
        )
    ends = []
    for part in shared + list(own):
        ends.append((ends[-1] if ends else 0) + part.shape[1])
    x_all, hid_all, datt_all, dffn_all, active_all, dpre_all, mixed_all, dqkv_all = jnp.split(
        packed, ends[:-1], axis=1
    )

    def own_rows(product):
        return lax.dynamic_index_in_dim(
            product.reshape((dp_count, -1) + product.shape[1:]), dp, 0, False
        )

    outer_grads = (
        own_rows(dot_rows(x_all, dqkv_all)),
        own_rows(dot_rows(mixed_all, datt_all)),
        own_rows(dot_rows(hid_all, dpre_all)),
        own_rows(dot_rows(active_all, dffn_all)),
    )

    small_grad = jnp.concatenate([inner_norm_grad, 0.25 * outer_norm_grad, places_grad], axis=1)
    columns = small_grad.shape[1]
    blocks = small_grad.reshape(2, dp_count, col_count, -1, columns)
    blocks = jnp.where(row == 0, blocks, blocks[::-1]).transpose(1, 0, 2, 3, 4)
    blocks = lax.all_to_all(
        blocks.reshape(device_count, -1, columns), everyone, 0, 0, tiled=True
    )
    small_sum = jnp.sum(blocks, axis=0)
    return (
        to_features(layer_out, row),
        to_features(input_grad, row),
        inner_grads[0],
        inner_grads[1],
        inner_grads[2],
        inner_grads[3],
        small_sum[:, 0:4],
        small_sum[:, 8:],
        outer_grads[0],
        outer_grads[1],
        outer_grads[2],
        outer_grads[3],
        small_sum[:, 4:8],
    )


def solution(mesh):
    tokens = P(("dp", "col"), "row")
    first = P(("row", "dp"), "col")
    second = P(("col", "dp"), "row")
    small = P(("row", "dp", "col"), None)
    weights = (first, second, first, second)
    return jax.shard_map(
        local,
        mesh=mesh,
        in_specs=(tokens, P("dp")) + weights + (small, small) + weights + (small, tokens),
        out_specs=(tokens, tokens) + weights + (small, small) + weights + (small,),
        check_vma=False,
    )
```

```python
import jax
import jax.numpy as jnp
from jax import lax
from jax.experimental import pallas as pl
from jax.experimental.pallas import tpu as pltpu
from jax.sharding import PartitionSpec as P

HDIM = 64
SEG = 128
SEQ_LEN = 2048
NSEG = 16
epsilon = 1e-06
highest = lax.Precision.HIGHEST
low_type = jnp.bfloat16


def dot(left, right):
    return jnp.dot(left, right, preferred_element_type=jnp.float32)


def dot_t(left, right):
    return lax.dot_general(
        left, right, (((1,), (1,)), ((), ())), preferred_element_type=jnp.float32
    )


def dot_rows(left, right):
    return lax.dot_general(
        left, right, (((0,), (0,)), ((), ())), preferred_element_type=jnp.float32
    )


def row_swap(value):
    return lax.ppermute(value, "row", [(0, 1), (1, 0)])


def col_swap(value, mask):
    return lax.ppermute(value, "col", [(i, i ^ mask) for i in range(lax.axis_size("col"))])


def dp_shift(value, step):
    count = lax.axis_size("dp")
    return lax.ppermute(value, "dp", [(i, (i + step) % count) for i in range(count)])


def after(value, earlier):
    return lax.optimization_barrier((value, earlier))[0]


def dp_pieces(value):
    count = lax.axis_size("dp")
    return [value] + [dp_shift(value, step) for step in range(1, count)]


def place_pieces(pieces):
    count = len(pieces)
    height, width = pieces[0].shape

    def kernel(place_ref, *refs):
        for step in range(count):
            at = lax.rem(place_ref[0] - step + count, count)
            refs[count][pl.ds(pl.multiple_of(at * height, 16), height), :] = refs[step][...]

    whole = pl.BlockSpec(memory_space=pltpu.VMEM)
    return pl.pallas_call(
        kernel,
        out_shape=jax.ShapeDtypeStruct((count * height, width), pieces[0].dtype),
        grid_spec=pltpu.PrefetchScalarGridSpec(
            num_scalar_prefetch=1, grid=(), in_specs=[whole] * count, out_specs=whole
        ),
        cost_estimate=pl.CostEstimate(
            flops=0, bytes_accessed=4 * count * height * width, transcendentals=0
        ),
        name="place_pieces",
    )(lax.axis_index("dp").reshape(1), *pieces)


def dp_scatter_sum(value):
    count = lax.axis_size("dp")
    if count > 4:
        return lax.psum_scatter(value, "dp", scatter_dimension=0, tiled=True)
    place = lax.axis_index("dp")
    parts = value.reshape((count, -1) + value.shape[1:])
    total = lax.dynamic_index_in_dim(parts, place, 0, False)
    for step in range(1, count):
        piece = lax.dynamic_index_in_dim(parts, (place + step) % count, 0, False)
        total = total + dp_shift(piece.astype(low_type), step).astype(jnp.float32)
    return total


def plane_blocks(own, through):
    side = col_swap(own, 1)
    over = col_swap(own, 2)
    far = col_swap(over, 1) if through == 1 else col_swap(side, 2)
    mine = (own, side, over, far)
    return (mine, tuple(row_swap(block) for block in mine))


def pair_blocks(own):
    mine = (own, col_swap(own, 2))
    return (mine, tuple(row_swap(block) for block in mine))


def gather_weights(inner_shards, outer_shards):
    inner_shards = [shard.astype(low_type) for shard in inner_shards]
    outer_shards = [shard.astype(low_type) for shard in outer_shards]
    throughs = (1, 2, 1, 2)
    if lax.axis_size("dp") > 4:
        inner_own = [lax.all_gather(s, "dp", axis=0, tiled=True) for s in inner_shards]
        outer_own = [lax.all_gather(s, "dp", axis=0, tiled=True) for s in outer_shards]
    else:
        inner_own = []
        gate = None
        for shard in inner_shards:
            pieces = dp_pieces(shard if gate is None else after(shard, gate))
            gate = pieces[1]
            inner_own.append(place_pieces(pieces))
        columns = jnp.concatenate([outer_shards[2], outer_shards[0]], axis=1)
        rows = jnp.concatenate([outer_shards[3], outer_shards[1]], axis=0)
        pieces = dp_pieces(after(columns, pieces))
        columns = place_pieces(pieces)
        split = outer_shards[2].shape[1]
        height = outer_shards[3].shape[0]
        pieces = dp_pieces(after(rows, pieces[1]))
        outer_own = [
            columns[:, split:],
            place_pieces([piece[height:] for piece in pieces]),
            columns[:, :split],
            place_pieces([piece[:height] for piece in pieces]),
        ]
    inner = [plane_blocks(own, through) for own, through in zip(inner_own, throughs)]
    last = inner[3][0][3]
    outer = [pair_blocks(after(own, last)) for own in outer_own]
    return tuple(
        tuple(
            matrix(blocks)
            for matrix, blocks in zip(
                (first_matrix, second_matrix, first_matrix, second_matrix), group
            )
        )
        for group in (inner, outer)
    )


def first_matrix(blocks):
    return jnp.concatenate([jnp.concatenate(half, axis=1) for half in blocks], axis=0)


def second_matrix(blocks):
    return jnp.concatenate([jnp.concatenate(half, axis=0) for half in blocks], axis=1)


def plane_sum(sums, through):
    other = 3 - through
    own = sums[0] + col_swap(sums[through].astype(low_type), through).astype(jnp.float32)
    onward = sums[other] + col_swap(sums[3].astype(low_type), through).astype(jnp.float32)
    return own + col_swap(onward.astype(low_type), other).astype(jnp.float32)


def scatter_grad(mine, theirs, through):
    sums = [
        block.astype(jnp.float32) + row_swap(sent).astype(jnp.float32)
        for block, sent in zip(mine, theirs)
    ]
    return dp_scatter_sum(plane_sum(sums, through))


def normalize(value, gain, shift):
    average = jnp.mean(value, axis=-1, keepdims=True)
    centred = value - average
    inverse = lax.rsqrt(jnp.mean(centred * centred, axis=-1, keepdims=True) + epsilon)
    unit = centred * inverse
    return (unit * gain + shift, unit, inverse)


def norm_backward(upstream, unit, inverse, gain):
    scaled = upstream * gain
    centre = jnp.mean(scaled, axis=-1, keepdims=True)
    slope = jnp.mean(scaled * unit, axis=-1, keepdims=True)
    result = inverse * (scaled - centre - unit * slope)
    return (result, jnp.sum(upstream * unit, 0), jnp.sum(upstream, 0))


def split_heads(qkv_low, group):
    count = qkv_low.shape[0]
    heads = qkv_low.shape[1] // (3 * HDIM)
    parts = qkv_low.reshape(count // group, group, heads, 3, HDIM)
    return (parts[:, :, :, 0], parts[:, :, :, 1], parts[:, :, :, 2])


def masked_scores(query, key_part, group, keep):
    scores = jnp.einsum(
        "gqhd,gkhd->ghqk", query, key_part, preferred_element_type=jnp.float32
    ) * HDIM ** (-0.5)
    allowed = keep.reshape(-1, 1, 1, group) > 0.5
    return jnp.where(allowed, scores, -1000000000.0)


def attend(qkv_low, group, keep):
    query, key_part, value_part = split_heads(qkv_low, group)
    scores = masked_scores(query, key_part, group, keep)
    topmost = jnp.max(scores, axis=-1, keepdims=True)
    expo = jnp.exp(scores - topmost)
    total = jnp.sum(expo, axis=-1, keepdims=True)
    probs = (expo / total).astype(low_type)
    mixed = jnp.einsum("ghqk,gkhd->gqhd", probs, value_part, preferred_element_type=jnp.float32)
    return (mixed.reshape(qkv_low.shape[0], -1), topmost + jnp.log(total))


def attend_backward(upstream, qkv_low, logsum, group, keep):
    query, key_part, value_part = split_heads(qkv_low, group)
    count = qkv_low.shape[0]
    incoming = upstream.reshape(query.shape)
    probs = jnp.exp(masked_scores(query, key_part, group, keep) - logsum)
    probs_low = probs.astype(low_type)
    dprobs = jnp.einsum("gqhd,gkhd->ghqk", incoming, value_part, preferred_element_type=jnp.float32)
    dvalue = jnp.einsum("ghqk,gqhd->gkhd", probs_low, incoming, preferred_element_type=jnp.float32)
    centre = jnp.sum(dprobs * probs, axis=-1, keepdims=True)
    dscore = (probs * (dprobs - centre)).astype(low_type)
    dquery = jnp.einsum(
        "ghqk,gkhd->gqhd", dscore, key_part, preferred_element_type=jnp.float32
    ) * HDIM ** (-0.5)
    dkey = jnp.einsum(
        "ghqk,gqhd->gkhd", dscore, query, preferred_element_type=jnp.float32
    ) * HDIM ** (-0.5)
    return jnp.stack([dquery, dkey, dvalue], axis=3).reshape(count, -1)


def gelu_and_slope(value):
    share = 0.5 + 0.5 * lax.erf(value * 0.7071067811865476)
    density = 0.3989422804014327 * jnp.exp(-0.5 * value * value)
    return ((value * share).astype(low_type), (share + value * density).astype(low_type))


def block_forward(value, weights, norms, group, keep, join):
    project, merge, expand, shrink = weights
    value_low = value.astype(low_type)
    qkv_low = dot(value_low, project).astype(low_type)
    mixed, logsum = attend(qkv_low, group, keep)
    mixed = mixed.astype(low_type)
    attended = join(dot(mixed, merge))
    hid, unit_one, inverse_one = normalize(value + attended, norms[0], norms[1])
    hid_low = hid.astype(low_type)
    pre = dot(hid_low, expand)
    active, slope = gelu_and_slope(pre)
    ffn = join(dot(active, shrink))
    result, unit_two, inverse_two = normalize(hid + ffn, norms[2], norms[3])
    saved = (
        value_low,
        qkv_low,
        logsum,
        mixed,
        unit_one,
        inverse_one,
        hid_low,
        slope,
        active,
        unit_two,
        inverse_two,
    )
    return (result, saved)


def ffn_backward(upstream, unit, inverse, slope, weights, norms, join):
    dsecond, gain_two, shift_two = norm_backward(upstream, unit, inverse, norms[2])
    dffn = dsecond.astype(low_type)
    dpre = (dot_t(dffn, weights[3]) * slope.astype(jnp.float32)).astype(low_type)
    dhid = dsecond + join(dot_t(dpre, weights[2]))
    return (dffn, dpre, dhid, gain_two, shift_two)


def attention_backward(dhid, saved, weights, norms, group, keep, join):
    qkv_low, logsum, _, unit_one, inverse_one = saved[1:6]
    dfirst, gain_one, shift_one = norm_backward(dhid, unit_one, inverse_one, norms[0])
    datt = dfirst.astype(low_type)
    dmixed = dot_t(datt, weights[1]).astype(low_type)
    dqkv = attend_backward(dmixed, qkv_low, logsum, group, keep).astype(low_type)
    dvalue = dfirst + join(dot_t(dqkv, weights[0]))
    return (datt, dqkv, dvalue, gain_one, shift_one)


def ffn_grads(hid_low, dpre, active, dffn, col):
    dp_count, col_count = lax.axis_size("dp"), lax.axis_size("col")
    half = hid_low.shape[1] // 2
    theirs_first = dot_rows(hid_low[:, half:], dpre).astype(low_type)
    theirs_second = dot_rows(active, dffn[:, half:]).astype(low_type)
    mine_first = dot_rows(hid_low[:, :half], dpre).astype(low_type)
    mine_second = dot_rows(active, dffn[:, :half]).astype(low_type)
    if dp_count > 4:
        return (
            scatter_grad(
                jnp.split(mine_first, col_count, 1), jnp.split(theirs_first, col_count, 1), 1
            ),
            scatter_grad(
                jnp.split(mine_second, col_count, 0), jnp.split(theirs_second, col_count, 0), 2
            ),
        )
    wide = mine_first.shape[1] // col_count
    tall = mine_second.shape[0] // col_count
    low, high = half // dp_count, tall // dp_count
    rows = 2 * low + high

    def kernel(col_ref, mine_a, got_a, mine_b, got_b, out):
        first = mine_a[...].astype(jnp.float32) + got_a[...].astype(jnp.float32)
        second = mine_b[...].astype(jnp.float32) + got_b[...].astype(jnp.float32)
        first = first.astype(low_type)
        second = second.astype(low_type)
        for place in range(dp_count):
            part = first[place * low : (place + 1) * low]
            out[0, place, :low] = part[:, :half]
            out[0, place, low : 2 * low] = part[:, half:]
            out[0, place, 2 * low :] = second[place * high : (place + 1) * high]

    first_spec = pl.BlockSpec((half, wide), lambda j, c: (0, j ^ c[0]))
    second_spec = pl.BlockSpec((tall, half), lambda j, c: (j ^ c[0], 0))
    packed = pl.pallas_call(
        kernel,
        out_shape=jax.ShapeDtypeStruct((col_count, dp_count, rows, half), low_type),
        grid_spec=pltpu.PrefetchScalarGridSpec(
            num_scalar_prefetch=1,
            grid=(col_count,),
            in_specs=[first_spec, first_spec, second_spec, second_spec],
            out_specs=pl.BlockSpec((1, dp_count, rows, half), lambda j, c: (j, 0, 0, 0)),
        ),
        cost_estimate=pl.CostEstimate(
            flops=0, bytes_accessed=6 * col_count * dp_count * rows * half, transcendentals=0
        ),
        name="pack_grads",
    )(col.reshape(1), mine_first, row_swap(theirs_first), mine_second, row_swap(theirs_second))
    packed = packed.reshape(col_count * dp_count, rows, half)
    packed = lax.psum_scatter(packed, "col", scatter_dimension=0, tiled=True)
    packed = lax.psum_scatter(packed, "dp", scatter_dimension=0, tiled=True)[0]
    packed = packed.astype(jnp.float32)
    return (
        jnp.concatenate([packed[:low], packed[low : 2 * low]], axis=1),
        packed[2 * low :],
    )


def halves(value, axis):
    return jnp.split(value, 2, axis=axis)


def first_grad(pair, through):
    left, right = pair
    mine_left, theirs_left = halves(left, 1)
    blocks = jnp.split(right, lax.axis_size("col"), axis=1)
    theirs = [dot_rows(theirs_left, block).astype(low_type) for block in blocks]
    mine = [dot_rows(mine_left, block).astype(low_type) for block in blocks]
    return scatter_grad(mine, theirs, through)


def second_grad(pair, through):
    left, right = pair
    mine_right, theirs_right = halves(right, 1)
    count = lax.axis_size("col")
    theirs = dot_rows(left, theirs_right).astype(low_type)
    mine = dot_rows(left, mine_right).astype(low_type)
    got = row_swap(theirs)
    total = mine.astype(jnp.float32) + got.astype(jnp.float32)
    return dp_scatter_sum(plane_sum(jnp.split(total, count, 0), through))


def to_tokens(value, row):
    parts = value.reshape((2, -1) + value.shape[1:])
    mine = lax.dynamic_index_in_dim(parts, row, 0, False)
    theirs = lax.dynamic_index_in_dim(parts, 1 - row, 0, False)
    return jnp.concatenate([mine, row_swap(theirs)], axis=1)


def to_features(value, row):
    mine, theirs = halves(value, 1)
    got = row_swap(theirs)
    first = jnp.where(row == 0, mine, got)
    second = jnp.where(row == 0, got, mine)
    return jnp.concatenate([first, second], axis=0)


def swap_features(value):
    first, second = halves(value, 1)
    return jnp.concatenate([second, first], axis=1)


def swap_rows(value):
    first, second = halves(value, 0)
    return jnp.concatenate([second, first], axis=0)


def local(
    hidden,
    lengths,
    inner_project,
    inner_merge,
    inner_expand,
    inner_shrink,
    inner_norms,
    outer_places,
    outer_project,
    outer_merge,
    outer_expand,
    outer_shrink,
    outer_norms,
    out_grad,
):
    dp_count, row_count, col_count = (lax.axis_size(name) for name in ("dp", "row", "col"))
    dp, row, col = (lax.axis_index(name) for name in ("dp", "row", "col"))
    everyone = ("dp", "row", "col")
    device_count = dp_count * row_count * col_count
    value = to_tokens(hidden, row)
    grad_in = to_tokens(out_grad, row)
    tokens, width = value.shape
    segs = tokens // SEG

    inner, outer = gather_weights(
        (inner_project, inner_merge, inner_expand, inner_shrink),
        (outer_project, outer_merge, outer_expand, outer_shrink),
    )
    small = jnp.concatenate([inner_norms, outer_norms, outer_places], axis=1)
    small = lax.all_to_all(
        jnp.broadcast_to(small[None], (device_count,) + small.shape), everyone, 0, 0, tiled=True
    )
    small = small.reshape((dp_count, row_count, -1) + small.shape[2:])
    small = jnp.concatenate(
        [
            lax.dynamic_index_in_dim(small, row, 1, False).reshape(-1, small.shape[-1]),
            lax.dynamic_index_in_dim(small, 1 - row, 1, False).reshape(-1, small.shape[-1]),
        ],
        axis=0,
    )
    vectors = small.T
    inner_gains = vectors[0:4]
    outer_gains = vectors[4:8]
    places = vectors[8:]

    length = lax.dynamic_index_in_dim(lengths, col // 2, 0, False)
    half = col % 2
    seg_own = (half * 2 + row) * segs + jnp.arange(segs, dtype=jnp.int32)
    spot = (seg_own[:, None] * SEG + jnp.arange(SEG, dtype=jnp.int32)[None]).reshape(tokens)
    valid = (spot < length).astype(jnp.float32)
    keep_tok = ((spot < length) | (spot % SEG == 0)).astype(jnp.float32)
    seg_all = jnp.concatenate(
        [
            (h * 2 + r) * segs + jnp.arange(segs, dtype=jnp.int32)
            for h in (half, 1 - half)
            for r in (row, 1 - row)
        ]
    )
    keep_seg = (seg_all * SEG < length).astype(jnp.float32)
    one_hot = (seg_own[:, None] == jnp.arange(NSEG, dtype=jnp.int32)[None]).astype(jnp.float32)

    inner_out, inner_saved = block_forward(
        value, inner, inner_gains, SEG, keep_tok, lambda partial_sum: partial_sum
    )
    grid = inner_out.reshape(segs, SEG, width)
    masked_grad = (grad_in * valid[:, None]).reshape(segs, SEG, width)
    heads_in = grid[:, 0] + jnp.dot(
        one_hot, places, precision=highest, preferred_element_type=jnp.float32
    )
    rows = jnp.concatenate([heads_in, masked_grad[:, 0]], axis=0)
    rows = jnp.stack([rows, swap_features(row_swap(rows))]).reshape(2, 2, segs, width)
    rows = jnp.stack([rows, col_swap(rows, 1)])
    rows = rows.transpose(2, 0, 1, 3, 4).reshape(2, NSEG, width)

    def join(partial_sum):
        return partial_sum + swap_rows(col_swap(partial_sum, 1))

    def alone(partial_sum):
        return partial_sum

    is_first = (jnp.arange(tokens, dtype=jnp.int32) % SEG == 0)[:, None]
    main = ffn_backward(
        jnp.where(is_first, 0.0, masked_grad.reshape(tokens, width)),
        inner_saved[9],
        inner_saved[10],
        inner_saved[7],
        inner,
        inner_gains,
        alone,
    )
    outer_out, outer_saved = block_forward(rows[0], outer, outer_gains, NSEG, keep_seg, join)
    o_dffn, o_dpre, o_dhid, *o_second = ffn_backward(
        rows[1], outer_saved[9], outer_saved[10], outer_saved[7], outer, outer_gains, join
    )
    o_datt, o_dqkv, dheads, *o_first = attention_backward(
        o_dhid, outer_saved, outer, outer_gains, NSEG, keep_seg, join
    )
    outer_norm_grad = jnp.stack(o_first + o_second, axis=1)
    outer_pairs = (
        (outer_saved[0], o_dqkv),
        (outer_saved[3], o_datt),
        (outer_saved[6], o_dpre),
        (outer_saved[8], o_dffn),
    )
    dheads = dheads[:segs]
    layer_out = (
        jnp.concatenate([outer_out[:segs, None], grid[:, 1:]], axis=1).reshape(tokens, width)
        * valid[:, None]
    )
    places_grad = jnp.dot(dheads.T, one_hot, precision=highest, preferred_element_type=jnp.float32)

    def firsts(array):
        return array.reshape((segs, SEG) + array.shape[1:])[:, 0]

    few = ffn_backward(
        dheads,
        firsts(inner_saved[9]),
        firsts(inner_saved[10]),
        firsts(inner_saved[7]),
        inner,
        inner_gains,
        alone,
    )
    dffn, dpre, dhid = (
        jnp.where(is_first, jnp.repeat(some, SEG, axis=0), rest)
        for some, rest in zip(few[:3], main[:3])
    )
    expand_grad, shrink_grad = ffn_grads(inner_saved[6], dpre, inner_saved[8], dffn, col)
    datt, dqkv, input_grad, *i_first = attention_backward(
        dhid, inner_saved, inner, inner_gains, SEG, keep_tok, alone
    )
    inner_norm_grad = jnp.stack(i_first + [few[3] + main[3], few[4] + main[4]], axis=1)
    inner_grads = (
        first_grad((inner_saved[0], dqkv), 1),
        second_grad((inner_saved[3], datt), 2),
        expand_grad,
        shrink_grad,
    )

    (x_low, dqkv), (mixed, datt), (hid_low, dpre), (active, dffn) = outer_pairs
    shared = [halves(part, 1)[0] for part in (x_low, hid_low, datt, dffn)]
    own, over = zip(*(halves(part, 1) for part in (active, dpre, mixed, dqkv)))
    packed = jnp.concatenate(
        [
            jnp.concatenate(shared + list(own), axis=1),
            col_swap(jnp.concatenate(shared + list(over), axis=1), 2),
        ],
        axis=0,
    )
    if dp_count > 4:
        packed = lax.all_gather(packed, "dp", axis=0, tiled=True)
    else:
        packed = jnp.concatenate(
            [packed] + [dp_shift(packed, step) for step in range(1, dp_count)], axis=0
        )
    ends = []
    for part in shared + list(own):
        ends.append((ends[-1] if ends else 0) + part.shape[1])
    x_all, hid_all, datt_all, dffn_all, active_all, dpre_all, mixed_all, dqkv_all = jnp.split(
        packed, ends[:-1], axis=1
    )

    def own_rows(product):
        return lax.dynamic_index_in_dim(
            product.reshape((dp_count, -1) + product.shape[1:]), dp, 0, False
        )

    outer_grads = (
        own_rows(dot_rows(x_all, dqkv_all)),
        own_rows(dot_rows(mixed_all, datt_all)),
        own_rows(dot_rows(hid_all, dpre_all)),
        own_rows(dot_rows(active_all, dffn_all)),
    )

    small_grad = jnp.concatenate([inner_norm_grad, 0.25 * outer_norm_grad, places_grad], axis=1)
    columns = small_grad.shape[1]
    blocks = small_grad.reshape(2, dp_count, col_count, -1, columns)
    blocks = jnp.where(row == 0, blocks, blocks[::-1]).transpose(1, 0, 2, 3, 4)
    blocks = lax.all_to_all(
        blocks.reshape(device_count, -1, columns), everyone, 0, 0, tiled=True
    )
    small_sum = jnp.sum(blocks, axis=0)
    return (
        to_features(layer_out, row),
        to_features(input_grad, row),
        inner_grads[0],
        inner_grads[1],
        inner_grads[2],
        inner_grads[3],
        small_sum[:, 0:4],
        small_sum[:, 8:],
        outer_grads[0],
        outer_grads[1],
        outer_grads[2],
        outer_grads[3],
        small_sum[:, 4:8],
    )


def solution(mesh):
    tokens = P(("dp", "col"), "row")
    first = P(("row", "dp"), "col")
    second = P(("col", "dp"), "row")
    small = P(("row", "dp", "col"), None)
    weights = (first, second, first, second)
    return jax.shard_map(
        local,
        mesh=mesh,
        in_specs=(tokens, P("dp")) + weights + (small, small) + weights + (small, tokens),
        out_specs=(tokens, tokens) + weights + (small, small) + weights + (small,),
        check_vma=False,
    )
```

```python
import jax
import jax.numpy as jnp
from jax import lax
from jax.experimental import pallas as pl
from jax.experimental.pallas import tpu as pltpu
from jax.sharding import PartitionSpec as P

HDIM = 64
SEG = 128
SEQ_LEN = 2048
NSEG = 16
epsilon = 1e-06
highest = lax.Precision.HIGHEST
low_type = jnp.bfloat16


def dot(left, right):
    return jnp.dot(left, right, preferred_element_type=jnp.float32)


def dot_t(left, right):
    return lax.dot_general(
        left, right, (((1,), (1,)), ((), ())), preferred_element_type=jnp.float32
    )


def dot_rows(left, right):
    return lax.dot_general(
        left, right, (((0,), (0,)), ((), ())), preferred_element_type=jnp.float32
    )


def row_swap(value):
    return lax.ppermute(value, "row", [(0, 1), (1, 0)])


def col_swap(value, mask):
    return lax.ppermute(value, "col", [(i, i ^ mask) for i in range(lax.axis_size("col"))])


def dp_shift(value, step):
    count = lax.axis_size("dp")
    return lax.ppermute(value, "dp", [(i, (i + step) % count) for i in range(count)])


def after(value, earlier):
    return lax.optimization_barrier((value, earlier))[0]


def dp_pieces(value):
    count = lax.axis_size("dp")
    return [value] + [dp_shift(value, step) for step in range(1, count)]


def place_pieces(pieces):
    count = len(pieces)
    height, width = pieces[0].shape

    def kernel(place_ref, *refs):
        for step in range(count):
            at = lax.rem(place_ref[0] - step + count, count)
            refs[count][pl.ds(pl.multiple_of(at * height, 16), height), :] = refs[step][...]

    whole = pl.BlockSpec(memory_space=pltpu.VMEM)
    return pl.pallas_call(
        kernel,
        out_shape=jax.ShapeDtypeStruct((count * height, width), pieces[0].dtype),
        grid_spec=pltpu.PrefetchScalarGridSpec(
            num_scalar_prefetch=1, grid=(), in_specs=[whole] * count, out_specs=whole
        ),
        cost_estimate=pl.CostEstimate(
            flops=0, bytes_accessed=4 * count * height * width, transcendentals=0
        ),
        name="place_pieces",
    )(lax.axis_index("dp").reshape(1), *pieces)


def dp_scatter_sum(value):
    count = lax.axis_size("dp")
    if count > 4:
        return lax.psum_scatter(value, "dp", scatter_dimension=0, tiled=True)
    place = lax.axis_index("dp")
    parts = value.reshape((count, -1) + value.shape[1:])
    total = lax.dynamic_index_in_dim(parts, place, 0, False)
    for step in range(1, count):
        piece = lax.dynamic_index_in_dim(parts, (place + step) % count, 0, False)
        total = total + dp_shift(piece.astype(low_type), step).astype(jnp.float32)
    return total


def plane_blocks(own, through):
    side = col_swap(own, 1)
    over = col_swap(own, 2)
    far = col_swap(over, 1) if through == 1 else col_swap(side, 2)
    mine = (own, side, over, far)
    return (mine, tuple(row_swap(block) for block in mine))


def pair_blocks(own):
    mine = (own, col_swap(own, 2))
    return (mine, tuple(row_swap(block) for block in mine))


def gather_weights(inner_shards, outer_shards):
    inner_shards = [shard.astype(low_type) for shard in inner_shards]
    outer_shards = [shard.astype(low_type) for shard in outer_shards]
    throughs = (1, 2, 1, 2)
    if lax.axis_size("dp") > 4:
        inner_own = [lax.all_gather(s, "dp", axis=0, tiled=True) for s in inner_shards]
        outer_own = [lax.all_gather(s, "dp", axis=0, tiled=True) for s in outer_shards]
    else:
        inner_own = []
        gate = None
        for shard in inner_shards:
            pieces = dp_pieces(shard if gate is None else after(shard, gate))
            gate = pieces[1]
            inner_own.append(place_pieces(pieces))
        columns = jnp.concatenate([outer_shards[2], outer_shards[0]], axis=1)
        rows = jnp.concatenate([outer_shards[3], outer_shards[1]], axis=0)
        pieces = dp_pieces(after(columns, pieces))
        columns = place_pieces(pieces)
        split = outer_shards[2].shape[1]
        height = outer_shards[3].shape[0]
        pieces = dp_pieces(after(rows, pieces[1]))
        outer_own = [
            columns[:, split:],
            place_pieces([piece[height:] for piece in pieces]),
            columns[:, :split],
            place_pieces([piece[:height] for piece in pieces]),
        ]
    inner = [plane_blocks(own, through) for own, through in zip(inner_own, throughs)]
    last = inner[3][0][3]
    outer = [pair_blocks(after(own, last)) for own in outer_own]
    return inner, outer


def plane_sum(sums, through):
    other = 3 - through
    own = sums[0] + col_swap(sums[through].astype(low_type), through).astype(jnp.float32)
    onward = sums[other] + col_swap(sums[3].astype(low_type), through).astype(jnp.float32)
    return own + col_swap(onward.astype(low_type), other).astype(jnp.float32)


def scatter_grad(mine, theirs, through):
    sums = [
        block.astype(jnp.float32) + row_swap(sent).astype(jnp.float32)
        for block, sent in zip(mine, theirs)
    ]
    return dp_scatter_sum(plane_sum(sums, through))


def whole_spec(array):
    return pl.BlockSpec(
        array.shape, lambda i: (0,) * array.ndim, pipeline_mode=pl.Buffered(1)
    )


def flat(blocks):
    return [block for half in blocks for block in half]


def grouped(refs, cols):
    return (refs[:cols], refs[cols : 2 * cols])


def down(refs, cols):
    return lambda c: jnp.concatenate([refs[c][...], refs[cols + c][...]], axis=0)


def across(refs, cols):
    return lambda c: jnp.concatenate([refs[c][...], refs[cols + c][...]], axis=1)


def kernel_norm(value, gain, shift):
    average = jnp.mean(value, axis=1, keepdims=True)
    centred = value - average
    inverse = lax.rsqrt(jnp.mean(centred * centred, axis=1, keepdims=True) + epsilon)
    unit = centred * inverse
    return unit * gain + shift, unit, inverse


def kernel_norm_backward(upstream, unit, inverse, gain):
    scaled = upstream * gain
    centre = jnp.mean(scaled, axis=1, keepdims=True)
    slope = jnp.mean(scaled * unit, axis=1, keepdims=True)
    return inverse * (scaled - centre - unit * slope)


def gelu_and_slope(value):
    share = 0.5 + 0.5 * lax.erf(value * 0.7071067811865476)
    density = 0.3989422804014327 * jnp.exp(-0.5 * value * value)
    return (value * share).astype(low_type), (share + value * density).astype(low_type)


def softmax(query, key_part, allowed):
    scores = dot_t(query, key_part) * HDIM ** (-0.5)
    scores = jnp.where(allowed, scores, -1000000000.0)
    expo = jnp.exp(scores - jnp.max(scores, axis=1, keepdims=True))
    return expo / jnp.sum(expo, axis=1, keepdims=True)


def head_parts(qkv, head):
    start = head * 3 * HDIM
    return [qkv[:, start + k * HDIM : start + (k + 1) * HDIM] for k in range(3)]


def run(kernel, name, grid, ins, in_specs, outs, out_specs, flops, aliases=None):
    moved = sum(x.size * x.dtype.itemsize for x in list(ins) + list(outs))
    return pl.pallas_call(
        kernel,
        out_shape=outs,
        grid=grid,
        in_specs=in_specs,
        out_specs=out_specs,
        input_output_aliases=aliases or {},
        cost_estimate=pl.CostEstimate(flops=flops, bytes_accessed=moved, transcendentals=0),
        name=name,
    )(*ins)


def shape(*dims, kind=low_type):
    return jax.ShapeDtypeStruct(dims, kind)


def tile(rows, width):
    return pl.BlockSpec((rows, width), lambda i: (i, 0))


def stack_tile(cols, rows, width):
    return pl.BlockSpec((cols, rows, width), lambda i: (0, i, 0))


def project_attend(value, keep, project, merge, group, rows):
    tokens, width = value.shape
    cols = len(project[0])
    wide = project[0][0].shape[1]
    heads = wide // (3 * HDIM)
    out_width = cols * heads * HDIM
    merge_in = flat(merge) if merge else []

    def kernel(value_ref, keep_ref, *refs):
        weight = down(refs, cols)
        merge_refs = refs[2 * cols : 2 * cols + len(merge_in)]
        low_ref, qkv_ref, mixed_ref = refs[2 * cols + len(merge_in) :][:3]
        low = value_ref[...].astype(low_type)
        low_ref[...] = low
        qkvs = []
        for c in range(cols):
            qkvs.append(dot(low, weight(c)).astype(low_type))
            qkv_ref[c] = qkvs[c]
        for g in range(rows // group):
            span = slice(g * group, (g + 1) * group)
            allowed = keep_ref[:, span] > 0.5
            outs = []
            for c in range(cols):
                for head in range(heads):
                    query, key_part, content = head_parts(qkvs[c][span], head)
                    probs = softmax(query, key_part, allowed).astype(low_type)
                    outs.append(dot(probs, content))
            mixed_ref[span] = jnp.concatenate(outs, axis=1).astype(low_type)
        if merge_in:
            mixed = mixed_ref[...]
            for r, half in enumerate(grouped(merge_refs, cols)):
                joined = jnp.concatenate([ref[...] for ref in half], axis=0)
                size = joined.shape[1]
                refs[-1][:, r * size : (r + 1) * size] = dot(mixed, joined)

    ins = [value, keep] + flat(project) + merge_in
    outs = [
        shape(tokens, width),
        shape(cols, tokens, wide),
        shape(tokens, out_width),
    ]
    out_specs = [tile(rows, width), stack_tile(cols, rows, wide), tile(rows, out_width)]
    if merge_in:
        outs.append(shape(tokens, width, kind=jnp.float32))
        out_specs.append(tile(rows, width))
    return run(
        kernel,
        "project_attend",
        (tokens // rows,),
        ins,
        [tile(rows, width), pl.BlockSpec((1, rows), lambda i: (0, i))]
        + [whole_spec(x) for x in ins[2:]],
        outs,
        out_specs,
        2 * tokens * width * cols * wide + 4 * tokens * group * out_width,
    )


def merge_values(mixed, merge_refs, cols):
    parts = [
        dot(mixed, jnp.concatenate([ref[...] for ref in half], axis=0))
        for half in grouped(merge_refs, cols)
    ]
    return jnp.concatenate(parts, axis=1)


def merge_expand(value, mixed, merge, expand, norms, rows):
    tokens, width = value.shape
    cols = len(expand[0])
    wide = expand[0][0].shape[1]

    def kernel(value_ref, mixed_ref, norm_ref, *refs):
        merge_refs, expand_refs = refs[: 2 * cols], refs[2 * cols : 4 * cols]
        unit_ref, inverse_ref, low_ref, active_ref, slope_ref = refs[4 * cols :]
        attended = merge_values(mixed_ref[...], merge_refs, cols)
        hid, unit, inverse = kernel_norm(
            value_ref[...] + attended, norm_ref[0:1], norm_ref[1:2]
        )
        low = hid.astype(low_type)
        unit_ref[...] = unit
        inverse_ref[...] = inverse
        low_ref[...] = low
        weight = down(expand_refs, cols)
        for c in range(cols):
            span = slice(c * wide, (c + 1) * wide)
            active_ref[:, span], slope_ref[:, span] = gelu_and_slope(dot(low, weight(c)))

    ins = [value, mixed, norms] + flat(merge) + flat(expand)
    return run(
        kernel,
        "merge_expand",
        (tokens // rows,),
        ins,
        [tile(rows, width), tile(rows, width)] + [whole_spec(x) for x in ins[2:]],
        [
            shape(tokens, width, kind=jnp.float32),
            shape(tokens, 1, kind=jnp.float32),
            shape(tokens, width),
            shape(tokens, cols * wide),
            shape(tokens, cols * wide),
        ],
        [tile(rows, width), tile(rows, 1), tile(rows, width)] + [tile(rows, cols * wide)] * 2,
        2 * tokens * width * (width + cols * wide),
    )


def shrink_values(active, shrink_refs, cols):
    parts = [
        dot(active, jnp.concatenate([ref[...] for ref in half], axis=0))
        for half in grouped(shrink_refs, cols)
    ]
    return jnp.concatenate(parts, axis=1)


def shrink_norm(unit, active, shrink, norms, rows):
    tokens, width = unit.shape
    cols = len(shrink[0])

    def kernel(unit_ref, active_ref, norm_ref, *refs):
        out_ref, second_ref, inverse_ref = refs[2 * cols :]
        hid = unit_ref[...] * norm_ref[0:1] + norm_ref[1:2]
        ffn = shrink_values(active_ref[...], refs[: 2 * cols], cols)
        out_ref[...], second_ref[...], inverse_ref[...] = kernel_norm(
            hid + ffn, norm_ref[2:3], norm_ref[3:4]
        )

    ins = [unit, active, norms] + flat(shrink)
    return run(
        kernel,
        "shrink_norm",
        (tokens // rows,),
        ins,
        [tile(rows, width), tile(rows, active.shape[1])] + [whole_spec(x) for x in ins[2:]],
        [
            shape(tokens, width, kind=jnp.float32),
            shape(tokens, width, kind=jnp.float32),
            shape(tokens, 1, kind=jnp.float32),
        ],
        [tile(rows, width), tile(rows, width), tile(rows, 1)],
        2 * tokens * width * active.shape[1],
    )


def ffn_backward_values(upstream, unit, inverse, slope, gain, shrink_refs, expand_refs, cols, put):
    dsecond = kernel_norm_backward(upstream, unit, inverse, gain)
    dffn = dsecond.astype(low_type)
    back = None
    for c in range(cols):
        dactive = dot_t(dffn, across(shrink_refs, cols)(c))
        dpre = (dactive * slope(c).astype(jnp.float32)).astype(low_type)
        put(c, dpre)
        part = dot_t(dpre, down(expand_refs, cols)(c))
        back = part if back is None else back + part
    return dffn, dsecond, back


def put_sums(ref, first, second, width):
    ref[0] = jnp.concatenate([first, second, jnp.zeros((6, width), jnp.float32)], axis=0)


def column_sum(value):
    return jnp.sum(value, axis=0, keepdims=True)


def ffn_backward(grad, unit, inverse, slope, shrink, expand, norms, rows):
    tokens, width = grad.shape
    cols = len(shrink[0])
    wide = shrink[0][0].shape[0]

    def kernel(grad_ref, unit_ref, inverse_ref, slope_ref, norm_ref, *refs):
        dffn_ref, dpre_ref, dhid_ref, sum_ref = refs[4 * cols :]
        place = lax.broadcasted_iota(jnp.int32, (rows, 1), 0)
        upstream = jnp.where(place % SEG == 0, 0.0, grad_ref[...])
        unit = unit_ref[...]

        def put(c, value):
            dpre_ref[:, c * wide : (c + 1) * wide] = value

        dffn, dsecond, back = ffn_backward_values(
            upstream,
            unit,
            inverse_ref[...],
            lambda c: slope_ref[:, c * wide : (c + 1) * wide],
            norm_ref[2:3],
            refs[: 2 * cols],
            refs[2 * cols : 4 * cols],
            cols,
            put,
        )
        dffn_ref[...] = dffn
        dhid_ref[...] = dsecond + back
        put_sums(sum_ref, column_sum(upstream * unit), column_sum(upstream), width)

    ins = [grad, unit, inverse, slope, norms] + flat(shrink) + flat(expand)
    return run(
        kernel,
        "ffn_backward",
        (tokens // rows,),
        ins,
        [tile(rows, width), tile(rows, width), tile(rows, 1), tile(rows, cols * wide)]
        + [whole_spec(x) for x in ins[4:]],
        [
            shape(tokens, width),
            shape(tokens, cols * wide),
            shape(tokens, width, kind=jnp.float32),
            shape(tokens // rows, 8, width, kind=jnp.float32),
        ],
        [
            tile(rows, width),
            tile(rows, cols * wide),
            tile(rows, width),
            pl.BlockSpec((1, 8, width), lambda i: (i, 0, 0)),
        ],
        4 * tokens * width * cols * wide,
    )


def ffn_backward_firsts(grad, dheads, unit, inverse, slope, shrink, expand, norms, outs):
    tokens, width = grad.shape
    segs = tokens // SEG
    few = 16
    cols = len(shrink[0])
    wide = shrink[0][0].shape[0]
    by_seg = [x.reshape(segs, SEG, -1) for x in (grad, unit, inverse, slope)]
    outs = [x.reshape(segs, SEG, -1) for x in outs]
    upstream = jnp.concatenate([dheads[:, None], by_seg[0][:, 1:few]], axis=1)

    def kernel(up_ref, unit_ref, inverse_ref, slope_ref, norm_ref, *refs):
        dffn_ref, dpre_ref, dhid_ref, sum_ref = refs[4 * cols + 3 :]
        count = segs * few
        upstream = up_ref[...].reshape(count, width)
        unit = unit_ref[...].reshape(count, width)

        def put(c, value):
            dpre_ref[:, :, c * wide : (c + 1) * wide] = value.reshape(segs, few, wide)

        dffn, dsecond, back = ffn_backward_values(
            upstream,
            unit,
            inverse_ref[...].reshape(count, 1),
            lambda c: slope_ref[:, :, c * wide : (c + 1) * wide].reshape(count, wide),
            norm_ref[2:3],
            refs[: 2 * cols],
            refs[2 * cols : 4 * cols],
            cols,
            put,
        )
        dffn_ref[...] = dffn.reshape(segs, few, width)
        dhid_ref[...] = (dsecond + back).reshape(segs, few, width)
        place = lax.broadcasted_iota(jnp.int32, (count, 1), 0)
        only = jnp.where(place % few == 0, upstream, 0.0)
        put_sums(sum_ref, column_sum(only * unit), column_sum(only), width)

    ins = [upstream] + by_seg[1:] + [norms] + flat(shrink) + flat(expand) + outs
    front = [
        pl.BlockSpec((segs, few, x.shape[2]), lambda i: (0, 0, 0)) for x in [upstream] + by_seg[1:]
    ]
    back_specs = [pl.BlockSpec((segs, few, x.shape[2]), lambda i: (0, 0, 0)) for x in outs]
    first_out = len(ins) - 3
    dffn, dpre, dhid, sums = run(
        kernel,
        "ffn_backward_firsts",
        (1,),
        ins,
        front
        + [whole_spec(x) for x in ins[4:first_out]]
        + [pl.BlockSpec(memory_space=pl.ANY)] * 3,
        [shape(*x.shape, kind=x.dtype) for x in outs] + [shape(1, 8, width, kind=jnp.float32)],
        back_specs + [pl.BlockSpec((1, 8, width), lambda i: (0, 0, 0))],
        4 * segs * few * width * cols * wide,
        {first_out + k: k for k in range(3)},
    )
    return [x.reshape(tokens, -1) for x in (dffn, dpre, dhid)] + [sums]


def attention_backward(dhid, unit, inverse, qkv, keep, project, merge, norms, group, rows, whole):
    tokens, width = dhid.shape
    cols = len(project[0])
    wide = project[0][0].shape[1]
    heads = wide // (3 * HDIM)

    def kernel(dhid_ref, unit_ref, inverse_ref, qkv_ref, keep_ref, norm_ref, *refs):
        project_refs, merge_refs = refs[: 2 * cols], refs[2 * cols : 4 * cols]
        datt_ref, dqkv_ref, dx_ref, sum_ref = refs[4 * cols : 4 * cols + 4]
        upstream = dhid_ref[...]
        unit = unit_ref[...]
        dfirst = kernel_norm_backward(upstream, unit, inverse_ref[...], norm_ref[0:1])
        put_sums(sum_ref, column_sum(upstream * unit), column_sum(upstream), width)
        datt = dfirst.astype(low_type)
        datt_ref[...] = datt
        back = dfirst if whole else None
        if not whole:
            refs[-1][...] = dfirst
        for c in range(cols):
            dmixed = dot_t(datt, across(merge_refs, cols)(c)).astype(low_type)
            blocks = []
            for g in range(rows // group):
                span = slice(g * group, (g + 1) * group)
                allowed = keep_ref[:, span] > 0.5
                pieces = []
                for head in range(heads):
                    query, key_part, content = head_parts(qkv_ref[c, span], head)
                    incoming = dmixed[span, head * HDIM : (head + 1) * HDIM]
                    probs = softmax(query, key_part, allowed)
                    dprobs = dot_t(incoming, content)
                    centre = jnp.sum(dprobs * probs, axis=1, keepdims=True)
                    dscore = (probs * (dprobs - centre)).astype(low_type)
                    pieces.append(dot(dscore, key_part) * HDIM ** (-0.5))
                    pieces.append(dot_rows(dscore, query) * HDIM ** (-0.5))
                    pieces.append(dot_rows(probs.astype(low_type), incoming))
                blocks.append(jnp.concatenate(pieces, axis=1).astype(low_type))
            dqkv = blocks[0] if len(blocks) == 1 else jnp.concatenate(blocks, axis=0)
            dqkv_ref[c] = dqkv
            part = dot_t(dqkv, down(project_refs, cols)(c))
            back = part if back is None else back + part
        dx_ref[...] = back

    ins = [dhid, unit, inverse, qkv, keep, norms] + flat(project) + flat(merge)
    outs = [
        shape(tokens, width),
        shape(cols, tokens, wide),
        shape(tokens, width, kind=jnp.float32),
        shape(tokens // rows, 8, width, kind=jnp.float32),
    ]
    out_specs = [
        tile(rows, width),
        stack_tile(cols, rows, wide),
        tile(rows, width),
        pl.BlockSpec((1, 8, width), lambda i: (i, 0, 0)),
    ]
    if not whole:
        outs.append(shape(tokens, width, kind=jnp.float32))
        out_specs.append(tile(rows, width))
    return run(
        kernel,
        "attention_backward",
        (tokens // rows,),
        ins,
        [
            tile(rows, width),
            tile(rows, width),
            tile(rows, 1),
            stack_tile(cols, rows, wide),
            pl.BlockSpec((1, rows), lambda i: (0, i)),
        ]
        + [whole_spec(x) for x in ins[5:]],
        outs,
        out_specs,
        2 * tokens * width * cols * wide + 10 * tokens * group * cols * heads * HDIM,
    )


def outer_middle(value, attended, expand, shrink, norms):
    tokens, width = value.shape
    cols = len(expand[0])
    wide = expand[0][0].shape[1]

    def kernel(value_ref, attended_ref, norm_ref, *refs):
        unit_ref, inverse_ref, low_ref, active_ref, slope_ref, ffn_ref = refs[4 * cols :]
        hid, unit, inverse = kernel_norm(
            value_ref[...] + attended_ref[...], norm_ref[0:1], norm_ref[1:2]
        )
        low = hid.astype(low_type)
        unit_ref[...] = unit
        inverse_ref[...] = inverse
        low_ref[...] = low
        for c in range(cols):
            span = slice(c * wide, (c + 1) * wide)
            active_ref[:, span], slope_ref[:, span] = gelu_and_slope(
                dot(low, down(refs[: 2 * cols], cols)(c))
            )
        ffn_ref[...] = shrink_values(active_ref[...], refs[2 * cols : 4 * cols], cols)

    ins = [value, attended, norms] + flat(expand) + flat(shrink)
    outs = [
        shape(tokens, width, kind=jnp.float32),
        shape(tokens, 1, kind=jnp.float32),
        shape(tokens, width),
        shape(tokens, cols * wide),
        shape(tokens, cols * wide),
        shape(tokens, width, kind=jnp.float32),
    ]
    return run(
        kernel,
        "outer_middle",
        (1,),
        ins,
        [whole_spec(x) for x in ins],
        outs,
        [whole_spec(x) for x in outs],
        4 * tokens * width * cols * wide,
    )


def outer_turn(unit, ffn, grad, slope, shrink, expand, norms):
    tokens, width = unit.shape
    cols = len(expand[0])
    wide = expand[0][0].shape[1]

    def kernel(unit_ref, ffn_ref, grad_ref, slope_ref, norm_ref, *refs):
        out_ref, dffn_ref, dpre_ref, dsecond_ref, back_ref, sum_ref = refs[4 * cols :]
        hid = unit_ref[...] * norm_ref[0:1] + norm_ref[1:2]
        result, second, inverse = kernel_norm(hid + ffn_ref[...], norm_ref[2:3], norm_ref[3:4])
        out_ref[...] = result
        upstream = grad_ref[...]

        def put(c, value):
            dpre_ref[:, c * wide : (c + 1) * wide] = value

        dffn_ref[...], dsecond_ref[...], back_ref[...] = ffn_backward_values(
            upstream,
            second,
            inverse,
            lambda c: slope_ref[:, c * wide : (c + 1) * wide],
            norm_ref[2:3],
            refs[: 2 * cols],
            refs[2 * cols : 4 * cols],
            cols,
            put,
        )
        put_sums(sum_ref, column_sum(upstream * second), column_sum(upstream), width)

    ins = [unit, ffn, grad, slope, norms] + flat(shrink) + flat(expand)
    outs = [
        shape(tokens, width, kind=jnp.float32),
        shape(tokens, width),
        shape(tokens, cols * wide),
        shape(tokens, width, kind=jnp.float32),
        shape(tokens, width, kind=jnp.float32),
        shape(1, 8, width, kind=jnp.float32),
    ]
    return run(
        kernel,
        "outer_turn",
        (1,),
        ins,
        [whole_spec(x) for x in ins],
        outs,
        [whole_spec(x) for x in outs],
        4 * tokens * width * cols * wide,
    )


def ffn_grads(hid_low, dpre, active, dffn, col):
    dp_count, col_count = lax.axis_size("dp"), lax.axis_size("col")
    half = hid_low.shape[1] // 2
    theirs_first = dot_rows(hid_low[:, half:], dpre).astype(low_type)
    theirs_second = dot_rows(active, dffn[:, half:]).astype(low_type)
    mine_first = dot_rows(hid_low[:, :half], dpre).astype(low_type)
    mine_second = dot_rows(active, dffn[:, :half]).astype(low_type)
    if dp_count > 4:
        return (
            scatter_grad(
                jnp.split(mine_first, col_count, 1), jnp.split(theirs_first, col_count, 1), 1
            ),
            scatter_grad(
                jnp.split(mine_second, col_count, 0), jnp.split(theirs_second, col_count, 0), 2
            ),
        )
    wide = mine_first.shape[1] // col_count
    tall = mine_second.shape[0] // col_count
    low, high = half // dp_count, tall // dp_count
    rows = 2 * low + high

    def kernel(col_ref, mine_a, got_a, mine_b, got_b, out):
        first = mine_a[...].astype(jnp.float32) + got_a[...].astype(jnp.float32)
        second = mine_b[...].astype(jnp.float32) + got_b[...].astype(jnp.float32)
        first = first.astype(low_type)
        second = second.astype(low_type)
        for place in range(dp_count):
            part = first[place * low : (place + 1) * low]
            out[0, place, :low] = part[:, :half]
            out[0, place, low : 2 * low] = part[:, half:]
            out[0, place, 2 * low :] = second[place * high : (place + 1) * high]

    first_spec = pl.BlockSpec((half, wide), lambda j, c: (0, j ^ c[0]))
    second_spec = pl.BlockSpec((tall, half), lambda j, c: (j ^ c[0], 0))
    packed = pl.pallas_call(
        kernel,
        out_shape=jax.ShapeDtypeStruct((col_count, dp_count, rows, half), low_type),
        grid_spec=pltpu.PrefetchScalarGridSpec(
            num_scalar_prefetch=1,
            grid=(col_count,),
            in_specs=[first_spec, first_spec, second_spec, second_spec],
            out_specs=pl.BlockSpec((1, dp_count, rows, half), lambda j, c: (j, 0, 0, 0)),
        ),
        cost_estimate=pl.CostEstimate(
            flops=0, bytes_accessed=6 * col_count * dp_count * rows * half, transcendentals=0
        ),
        name="pack_grads",
    )(col.reshape(1), mine_first, row_swap(theirs_first), mine_second, row_swap(theirs_second))
    packed = packed.reshape(col_count * dp_count, rows, half)
    packed = lax.psum_scatter(packed, "col", scatter_dimension=0, tiled=True)
    packed = lax.psum_scatter(packed, "dp", scatter_dimension=0, tiled=True)[0]
    packed = packed.astype(jnp.float32)
    return (
        jnp.concatenate([packed[:low], packed[low : 2 * low]], axis=1),
        packed[2 * low :],
    )


def halves(value, axis):
    return jnp.split(value, 2, axis=axis)


def first_grad(left, right, through):
    mine_left, theirs_left = halves(left, 1)
    theirs = [dot_rows(theirs_left, block).astype(low_type) for block in right]
    mine = [dot_rows(mine_left, block).astype(low_type) for block in right]
    return scatter_grad(mine, theirs, through)


def second_grad(pair, through):
    left, right = pair
    mine_right, theirs_right = halves(right, 1)
    count = lax.axis_size("col")
    theirs = dot_rows(left, theirs_right).astype(low_type)
    mine = dot_rows(left, mine_right).astype(low_type)
    got = row_swap(theirs)
    total = mine.astype(jnp.float32) + got.astype(jnp.float32)
    return dp_scatter_sum(plane_sum(jnp.split(total, count, 0), through))


def to_tokens(value, row):
    parts = value.reshape((2, -1) + value.shape[1:])
    mine = lax.dynamic_index_in_dim(parts, row, 0, False)
    theirs = lax.dynamic_index_in_dim(parts, 1 - row, 0, False)
    return jnp.concatenate([mine, row_swap(theirs)], axis=1)


def to_features(value, row):
    mine, theirs = halves(value, 1)
    got = row_swap(theirs)
    first = jnp.where(row == 0, mine, got)
    second = jnp.where(row == 0, got, mine)
    return jnp.concatenate([first, second], axis=0)


def swap_features(value):
    first, second = halves(value, 1)
    return jnp.concatenate([second, first], axis=1)


def swap_rows(value):
    first, second = halves(value, 0)
    return jnp.concatenate([second, first], axis=0)


def local(
    hidden,
    lengths,
    inner_project,
    inner_merge,
    inner_expand,
    inner_shrink,
    inner_norms,
    outer_places,
    outer_project,
    outer_merge,
    outer_expand,
    outer_shrink,
    outer_norms,
    out_grad,
):
    dp_count, row_count, col_count = (lax.axis_size(name) for name in ("dp", "row", "col"))
    dp, row, col = (lax.axis_index(name) for name in ("dp", "row", "col"))
    everyone = ("dp", "row", "col")
    device_count = dp_count * row_count * col_count
    value = to_tokens(hidden, row)
    grad_in = to_tokens(out_grad, row)
    tokens, width = value.shape
    segs = tokens // SEG

    inner, outer = gather_weights(
        (inner_project, inner_merge, inner_expand, inner_shrink),
        (outer_project, outer_merge, outer_expand, outer_shrink),
    )
    small = jnp.concatenate([inner_norms, outer_norms, outer_places], axis=1)
    small = lax.all_to_all(
        jnp.broadcast_to(small[None], (device_count,) + small.shape), everyone, 0, 0, tiled=True
    )
    small = small.reshape((dp_count, row_count, -1) + small.shape[2:])
    small = jnp.concatenate(
        [
            lax.dynamic_index_in_dim(small, row, 1, False).reshape(-1, small.shape[-1]),
            lax.dynamic_index_in_dim(small, 1 - row, 1, False).reshape(-1, small.shape[-1]),
        ],
        axis=0,
    )
    vectors = small.T
    inner_gains = vectors[0:4]
    outer_gains = vectors[4:8]
    places = vectors[8:]

    length = lax.dynamic_index_in_dim(lengths, col // 2, 0, False)
    half = col % 2
    seg_own = (half * 2 + row) * segs + jnp.arange(segs, dtype=jnp.int32)
    spot = (seg_own[:, None] * SEG + jnp.arange(SEG, dtype=jnp.int32)[None]).reshape(tokens)
    valid = (spot < length).astype(jnp.float32)
    keep_tok = ((spot < length) | (spot % SEG == 0)).astype(jnp.float32)
    seg_all = jnp.concatenate(
        [
            (h * 2 + r) * segs + jnp.arange(segs, dtype=jnp.int32)
            for h in (half, 1 - half)
            for r in (row, 1 - row)
        ]
    )
    keep_seg = (seg_all * SEG < length).astype(jnp.float32)
    one_hot = (seg_own[:, None] == jnp.arange(NSEG, dtype=jnp.int32)[None]).astype(jnp.float32)

    keep_row = keep_tok[None]
    rows_tile = 2 * SEG
    x_in, qkv, mixed_in = project_attend(value, keep_row, inner[0], None, SEG, rows_tile)
    unit_one, inverse_one, hid_in, active_in, slope = merge_expand(
        value, mixed_in, inner[1], inner[2], inner_gains, rows_tile
    )
    inner_out, unit_two, inverse_two = shrink_norm(
        unit_one, active_in, inner[3], inner_gains, rows_tile
    )
    grid = inner_out.reshape(segs, SEG, width)
    masked_grad = (grad_in * valid[:, None]).reshape(segs, SEG, width)
    heads_in = grid[:, 0] + jnp.dot(
        one_hot, places, precision=highest, preferred_element_type=jnp.float32
    )
    rows = jnp.concatenate([heads_in, masked_grad[:, 0]], axis=0)
    rows = jnp.stack([rows, swap_features(row_swap(rows))]).reshape(2, 2, segs, width)
    rows = jnp.stack([rows, col_swap(rows, 1)])
    rows = rows.transpose(2, 0, 1, 3, 4).reshape(2, NSEG, width)

    def join(partial_sum):
        return partial_sum + swap_rows(col_swap(partial_sum, 1))

    flat_grad = masked_grad.reshape(tokens, width)
    main = ffn_backward(
        flat_grad, unit_two, inverse_two, slope, inner[3], inner[2], inner_gains, rows_tile
    )
    x_low, o_qkv, mixed, attended = project_attend(
        rows[0], keep_seg[None], outer[0], outer[1], NSEG, NSEG
    )
    o_unit, o_inverse, hid_low, active, o_slope, ffn = outer_middle(
        rows[0], join(attended), outer[2], outer[3], outer_gains
    )
    outer_out, dffn, dpre, dsecond, back, o_second = outer_turn(
        o_unit, join(ffn), rows[1], o_slope, outer[3], outer[2], outer_gains
    )
    datt, dqkv, back, o_first, dfirst = attention_backward(
        dsecond + join(back),
        o_unit,
        o_inverse,
        o_qkv,
        keep_seg[None],
        outer[0],
        outer[1],
        outer_gains,
        NSEG,
        NSEG,
        False,
    )
    dheads = dfirst + join(back)
    outer_norm_grad = jnp.concatenate([o_first[0, :2], o_second[0, :2]], axis=0).T
    dheads = dheads[:segs]
    layer_out = (
        jnp.concatenate([outer_out[:segs, None], grid[:, 1:]], axis=1).reshape(tokens, width)
        * valid[:, None]
    )
    places_grad = jnp.dot(dheads.T, one_hot, precision=highest, preferred_element_type=jnp.float32)

    dffn_in, dpre_in, dhid_in, few_sums = ffn_backward_firsts(
        flat_grad,
        dheads,
        unit_two,
        inverse_two,
        slope,
        inner[3],
        inner[2],
        inner_gains,
        main[:3],
    )
    expand_grad, shrink_grad = ffn_grads(hid_in, dpre_in, active_in, dffn_in, col)
    datt_in, dqkv_in, input_grad, first_sums = attention_backward(
        dhid_in,
        unit_one,
        inverse_one,
        qkv,
        keep_row,
        inner[0],
        inner[1],
        inner_gains,
        SEG,
        rows_tile,
        True,
    )
    inner_norm_grad = jnp.concatenate(
        [jnp.sum(first_sums, 0)[:2], jnp.sum(main[3], 0)[:2] + few_sums[0, :2]], axis=0
    ).T
    inner_grads = (
        first_grad(x_in, dqkv_in, 1),
        second_grad((mixed_in, datt_in), 2),
        expand_grad,
        shrink_grad,
    )

    shared = [halves(part, 1)[0] for part in (x_low, hid_low, datt, dffn)]
    own, over = zip(*([halves(part, 1) for part in (active, dpre, mixed)] + [tuple(dqkv)]))
    packed = jnp.concatenate(
        [
            jnp.concatenate(shared + list(own), axis=1),
            col_swap(jnp.concatenate(shared + list(over), axis=1), 2),
        ],
        axis=0,
    )
    if dp_count > 4:
        packed = lax.all_gather(packed, "dp", axis=0, tiled=True)
    else:
        packed = jnp.concatenate(
            [packed] + [dp_shift(packed, step) for step in range(1, dp_count)], axis=0
        )
    ends = []
    for part in shared + list(own):
        ends.append((ends[-1] if ends else 0) + part.shape[1])
    x_all, hid_all, datt_all, dffn_all, active_all, dpre_all, mixed_all, dqkv_all = jnp.split(
        packed, ends[:-1], axis=1
    )

    def own_rows(product):
        return lax.dynamic_index_in_dim(
            product.reshape((dp_count, -1) + product.shape[1:]), dp, 0, False
        )

    outer_grads = (
        own_rows(dot_rows(x_all, dqkv_all)),
        own_rows(dot_rows(mixed_all, datt_all)),
        own_rows(dot_rows(hid_all, dpre_all)),
        own_rows(dot_rows(active_all, dffn_all)),
    )

    small_grad = jnp.concatenate([inner_norm_grad, 0.25 * outer_norm_grad, places_grad], axis=1)
    columns = small_grad.shape[1]
    blocks = small_grad.reshape(2, dp_count, col_count, -1, columns)
    blocks = jnp.where(row == 0, blocks, blocks[::-1]).transpose(1, 0, 2, 3, 4)
    blocks = lax.all_to_all(
        blocks.reshape(device_count, -1, columns), everyone, 0, 0, tiled=True
    )
    small_sum = jnp.sum(blocks, axis=0)
    return (
        to_features(layer_out, row),
        to_features(input_grad, row),
        inner_grads[0],
        inner_grads[1],
        inner_grads[2],
        inner_grads[3],
        small_sum[:, 0:4],
        small_sum[:, 8:],
        outer_grads[0],
        outer_grads[1],
        outer_grads[2],
        outer_grads[3],
        small_sum[:, 4:8],
    )


def solution(mesh):
    tokens = P(("dp", "col"), "row")
    first = P(("row", "dp"), "col")
    second = P(("col", "dp"), "row")
    small = P(("row", "dp", "col"), None)
    weights = (first, second, first, second)
    return jax.shard_map(
        local,
        mesh=mesh,
        in_specs=(tokens, P("dp")) + weights + (small, small) + weights + (small, tokens),
        out_specs=(tokens, tokens) + weights + (small, small) + weights + (small,),
        check_vma=False,
    )
```

```python
import jax
import jax.numpy as jnp
from jax import lax
from jax.experimental import pallas as pl
from jax.experimental.pallas import tpu as pltpu
from jax.sharding import PartitionSpec as P

HDIM = 64
SEG = 128
SEQ_LEN = 2048
NSEG = 16
epsilon = 1e-06
highest = lax.Precision.HIGHEST
low_type = jnp.bfloat16


def dot(left, right):
    return jnp.dot(left, right, preferred_element_type=jnp.float32)


def dot_t(left, right):
    return lax.dot_general(
        left, right, (((1,), (1,)), ((), ())), preferred_element_type=jnp.float32
    )


def dot_rows(left, right):
    return lax.dot_general(
        left, right, (((0,), (0,)), ((), ())), preferred_element_type=jnp.float32
    )


def row_swap(value):
    return lax.ppermute(value, "row", [(0, 1), (1, 0)])


def col_swap(value, mask):
    return lax.ppermute(value, "col", [(i, i ^ mask) for i in range(lax.axis_size("col"))])


def dp_shift(value, step):
    count = lax.axis_size("dp")
    return lax.ppermute(value, "dp", [(i, (i + step) % count) for i in range(count)])


def after(value, earlier):
    return lax.optimization_barrier((value, earlier))[0]


def dp_pieces(value):
    count = lax.axis_size("dp")
    return [value] + [dp_shift(value, step) for step in range(1, count)]


def place_pieces(pieces, cut=None):
    count = len(pieces)
    height, width = pieces[0].shape
    bounds = (0, height) if cut is None else (0, cut, height)
    spans = list(zip(bounds[:-1], bounds[1:]))

    def kernel(place_ref, *refs):
        for step in range(count):
            at = lax.rem(place_ref[0] - step + count, count)
            for (low, high), out in zip(spans, refs[count:]):
                size = high - low
                out[pl.ds(pl.multiple_of(at * size, 16), size), :] = refs[step][low:high]

    whole = pl.BlockSpec(memory_space=pltpu.VMEM)
    outs = [
        jax.ShapeDtypeStruct((count * (high - low), width), pieces[0].dtype) for low, high in spans
    ]
    placed = pl.pallas_call(
        kernel,
        out_shape=outs,
        grid_spec=pltpu.PrefetchScalarGridSpec(
            num_scalar_prefetch=1,
            grid=(),
            in_specs=[whole] * count,
            out_specs=[whole] * len(outs),
        ),
        cost_estimate=pl.CostEstimate(
            flops=0, bytes_accessed=4 * count * height * width, transcendentals=0
        ),
        name="place_pieces",
    )(lax.axis_index("dp").reshape(1), *pieces)
    return placed[0] if cut is None else placed


def dp_scatter_sum(value):
    count = lax.axis_size("dp")
    if count > 4:
        return lax.psum_scatter(value, "dp", scatter_dimension=0, tiled=True)
    place = lax.axis_index("dp")
    parts = value.reshape((count, -1) + value.shape[1:])
    total = lax.dynamic_index_in_dim(parts, place, 0, False)
    for step in range(1, count):
        piece = lax.dynamic_index_in_dim(parts, (place + step) % count, 0, False)
        total = total + dp_shift(piece.astype(low_type), step).astype(jnp.float32)
    return total


def plane_blocks(own, through):
    side = col_swap(own, 1)
    over = col_swap(own, 2)
    far = col_swap(over, 1) if through == 1 else col_swap(side, 2)
    mine = (own, side, over, far)
    return (mine, tuple(row_swap(block) for block in mine))


def pair_blocks(own):
    mine = (own, col_swap(own, 2))
    return (mine, tuple(row_swap(block) for block in mine))


def gather_wide(inner_shards, outer_shards, first_use):
    inner_own, outer_own = (
        [lax.all_gather(shard, "dp", axis=0, tiled=True) for shard in group]
        for group in (inner_shards, outer_shards)
    )
    inner = [plane_blocks(own, through) for own, through in zip(inner_own, (1, 2, 1, 2))]
    outer = [pair_blocks(own) for own in outer_own]
    return inner, lambda gates: outer, first_use(inner[0])


def gather_weights(inner_shards, outer_shards, first_use):
    inner_shards = [shard.astype(low_type) for shard in inner_shards]
    outer_shards = [shard.astype(low_type) for shard in outer_shards]
    if lax.axis_size("dp") > 4:
        return gather_wide(inner_shards, outer_shards, first_use)
    project = place_pieces(dp_pieces(inner_shards[0]))
    merge_pieces = dp_pieces(inner_shards[1])
    expand_pieces = dp_pieces(after(inner_shards[2], project))
    project = plane_blocks(project, 1)
    shrink_pieces = dp_pieces(after(inner_shards[3], project[0][1]))
    merge = plane_blocks(place_pieces(after(merge_pieces, project[0][2])), 2)
    expand = plane_blocks(place_pieces(after(expand_pieces, (merge[0][1], project[0][3]))), 1)
    used = first_use(after(project, (expand[0][1], expand[0][2])))
    shrink = plane_blocks(place_pieces(after(shrink_pieces, (merge[0][3], expand[0][3]))), 2)
    rows = jnp.concatenate([outer_shards[1], outer_shards[3]], axis=0)
    first = dp_pieces(after(outer_shards[0], shrink_pieces))
    second = dp_pieces(after(rows, first[1]))
    third = dp_pieces(after(outer_shards[2], second[1]))

    def outer(gates):
        project = pair_blocks(place_pieces(after(first, gates[0])))
        merge, shrink = place_pieces(after(second, gates[1]), outer_shards[1].shape[0])
        expand = pair_blocks(place_pieces(after(third, gates[2])))
        return project, pair_blocks(merge), expand, pair_blocks(shrink)

    return (project, merge, expand, shrink), outer, used


def plane_sum(sums, through):
    other = 3 - through
    own = sums[0] + col_swap(sums[through].astype(low_type), through).astype(jnp.float32)
    onward = sums[other] + col_swap(sums[3].astype(low_type), through).astype(jnp.float32)
    return own + col_swap(onward.astype(low_type), other).astype(jnp.float32)


def scatter_grad(mine, theirs, through):
    sums = [
        block.astype(jnp.float32) + row_swap(sent).astype(jnp.float32)
        for block, sent in zip(mine, theirs)
    ]
    return dp_scatter_sum(plane_sum(sums, through))


def whole_spec(array):
    return pl.BlockSpec(
        array.shape, lambda i: (0,) * array.ndim, pipeline_mode=pl.Buffered(1)
    )


def flat(blocks):
    return [block for half in blocks for block in half]


def grouped(refs, cols):
    return (refs[:cols], refs[cols : 2 * cols])


def down(refs, cols):
    return lambda c: jnp.concatenate([refs[c][...], refs[cols + c][...]], axis=0)


def across(refs, cols):
    return lambda c: jnp.concatenate([refs[c][...], refs[cols + c][...]], axis=1)


def kernel_norm(value, gain, shift):
    average = jnp.mean(value, axis=1, keepdims=True)
    centred = value - average
    inverse = lax.rsqrt(jnp.mean(centred * centred, axis=1, keepdims=True) + epsilon)
    unit = centred * inverse
    return unit * gain + shift, unit, inverse


def kernel_norm_backward(upstream, unit, inverse, gain):
    scaled = upstream * gain
    centre = jnp.mean(scaled, axis=1, keepdims=True)
    slope = jnp.mean(scaled * unit, axis=1, keepdims=True)
    return inverse * (scaled - centre - unit * slope)


def gelu_and_slope(value):
    share = 0.5 + 0.5 * lax.erf(value * 0.7071067811865476)
    density = 0.3989422804014327 * jnp.exp(-0.5 * value * value)
    return (value * share).astype(low_type), (share + value * density).astype(low_type)


def softmax(pairs, allowed):
    scores = [dot_t(query, key_part) * HDIM ** (-0.5) for query, key_part in pairs]
    scores = [jnp.where(allowed, one, -1000000000.0) for one in scores]
    tops = [jnp.max(one, axis=1, keepdims=True) for one in scores]
    expos = [jnp.exp(one - top) for one, top in zip(scores, tops)]
    shares = [1.0 / jnp.sum(expo, axis=1, keepdims=True) for expo in expos]
    return [expo * share for expo, share in zip(expos, shares)]


def head_parts(qkv, head):
    start = head * 3 * HDIM
    return [qkv[:, start + k * HDIM : start + (k + 1) * HDIM] for k in range(3)]


def run(kernel, name, grid, ins, in_specs, outs, out_specs, flops, aliases=None):
    moved = sum(x.size * x.dtype.itemsize for x in list(ins) + list(outs))
    return pl.pallas_call(
        kernel,
        out_shape=outs,
        grid=grid,
        in_specs=in_specs,
        out_specs=out_specs,
        input_output_aliases=aliases or {},
        cost_estimate=pl.CostEstimate(flops=flops, bytes_accessed=moved, transcendentals=0),
        name=name,
    )(*ins)


def shape(*dims, kind=low_type):
    return jax.ShapeDtypeStruct(dims, kind)


def tile(rows, width):
    return pl.BlockSpec((rows, width), lambda i: (i, 0))


def stack_tile(cols, rows, width):
    return pl.BlockSpec((cols, rows, width), lambda i: (0, i, 0))


def project_attend(value, keep, project, merge, group, rows):
    tokens, width = value.shape
    cols = len(project[0])
    wide = project[0][0].shape[1]
    heads = wide // (3 * HDIM)
    out_width = cols * heads * HDIM
    merge_in = flat(merge) if merge else []

    def kernel(value_ref, keep_ref, *refs):
        weight = down(refs, cols)
        merge_refs = refs[2 * cols : 2 * cols + len(merge_in)]
        low_ref, qkv_ref, mixed_ref = refs[2 * cols + len(merge_in) :][:3]
        low = value_ref[...].astype(low_type)
        low_ref[...] = low
        qkvs = []
        for c in range(cols):
            qkvs.append(dot(low, weight(c)).astype(low_type))
            qkv_ref[c] = qkvs[c]
        for g in range(rows // group):
            span = slice(g * group, (g + 1) * group)
            allowed = keep_ref[:, span] > 0.5
            outs = []
            for c in range(cols):
                parts = [head_parts(qkvs[c][span], head) for head in range(heads)]
                probs = softmax([part[:2] for part in parts], allowed)
                outs += [
                    dot(some.astype(low_type), part[2]) for some, part in zip(probs, parts)
                ]
            mixed_ref[span] = jnp.concatenate(outs, axis=1).astype(low_type)
        if merge_in:
            mixed = mixed_ref[...]
            for r, half in enumerate(grouped(merge_refs, cols)):
                joined = jnp.concatenate([ref[...] for ref in half], axis=0)
                size = joined.shape[1]
                refs[-1][:, r * size : (r + 1) * size] = dot(mixed, joined)

    ins = [value, keep] + flat(project) + merge_in
    outs = [
        shape(tokens, width),
        shape(cols, tokens, wide),
        shape(tokens, out_width),
    ]
    out_specs = [tile(rows, width), stack_tile(cols, rows, wide), tile(rows, out_width)]
    if merge_in:
        outs.append(shape(tokens, width, kind=jnp.float32))
        out_specs.append(tile(rows, width))
    return run(
        kernel,
        "project_attend",
        (tokens // rows,),
        ins,
        [tile(rows, width), pl.BlockSpec((1, rows), lambda i: (0, i))]
        + [whole_spec(x) for x in ins[2:]],
        outs,
        out_specs,
        2 * tokens * width * cols * wide + 4 * tokens * group * out_width,
    )


def merge_values(mixed, merge_refs, cols):
    parts = [
        dot(mixed, jnp.concatenate([ref[...] for ref in half], axis=0))
        for half in grouped(merge_refs, cols)
    ]
    return jnp.concatenate(parts, axis=1)


def merge_expand(value, mixed, merge, expand, norms, rows):
    tokens, width = value.shape
    cols = len(expand[0])
    wide = expand[0][0].shape[1]

    def kernel(value_ref, mixed_ref, norm_ref, *refs):
        merge_refs, expand_refs = refs[: 2 * cols], refs[2 * cols : 4 * cols]
        unit_ref, inverse_ref, low_ref, active_ref, slope_ref = refs[4 * cols :]
        attended = merge_values(mixed_ref[...], merge_refs, cols)
        hid, unit, inverse = kernel_norm(
            value_ref[...] + attended, norm_ref[0:1], norm_ref[1:2]
        )
        low = hid.astype(low_type)
        unit_ref[...] = unit
        inverse_ref[...] = inverse
        low_ref[...] = low
        weight = down(expand_refs, cols)
        for c in range(cols):
            span = slice(c * wide, (c + 1) * wide)
            active_ref[:, span], slope_ref[:, span] = gelu_and_slope(dot(low, weight(c)))

    ins = [value, mixed, norms] + flat(merge) + flat(expand)
    return run(
        kernel,
        "merge_expand",
        (tokens // rows,),
        ins,
        [tile(rows, width), tile(rows, width)] + [whole_spec(x) for x in ins[2:]],
        [
            shape(tokens, width, kind=jnp.float32),
            shape(tokens, 1, kind=jnp.float32),
            shape(tokens, width),
            shape(tokens, cols * wide),
            shape(tokens, cols * wide),
        ],
        [tile(rows, width), tile(rows, 1), tile(rows, width)] + [tile(rows, cols * wide)] * 2,
        2 * tokens * width * (width + cols * wide),
    )


def shrink_values(active, shrink_refs, cols):
    parts = [
        dot(active, jnp.concatenate([ref[...] for ref in half], axis=0))
        for half in grouped(shrink_refs, cols)
    ]
    return jnp.concatenate(parts, axis=1)


def shrink_norm(unit, active, shrink, norms, rows):
    tokens, width = unit.shape
    cols = len(shrink[0])

    def kernel(unit_ref, active_ref, norm_ref, *refs):
        out_ref, second_ref, inverse_ref = refs[2 * cols :]
        hid = unit_ref[...] * norm_ref[0:1] + norm_ref[1:2]
        ffn = shrink_values(active_ref[...], refs[: 2 * cols], cols)
        out_ref[...], second_ref[...], inverse_ref[...] = kernel_norm(
            hid + ffn, norm_ref[2:3], norm_ref[3:4]
        )

    ins = [unit, active, norms] + flat(shrink)
    return run(
        kernel,
        "shrink_norm",
        (tokens // rows,),
        ins,
        [tile(rows, width), tile(rows, active.shape[1])] + [whole_spec(x) for x in ins[2:]],
        [
            shape(tokens, width, kind=jnp.float32),
            shape(tokens, width, kind=jnp.float32),
            shape(tokens, 1, kind=jnp.float32),
        ],
        [tile(rows, width), tile(rows, width), tile(rows, 1)],
        2 * tokens * width * active.shape[1],
    )


def ffn_backward_values(upstream, unit, inverse, slope, gain, shrink_refs, expand_refs, cols, put):
    dsecond = kernel_norm_backward(upstream, unit, inverse, gain)
    dffn = dsecond.astype(low_type)
    back = None
    for c in range(cols):
        dactive = dot_t(dffn, across(shrink_refs, cols)(c))
        dpre = (dactive * slope(c).astype(jnp.float32)).astype(low_type)
        put(c, dpre)
        part = dot_t(dpre, down(expand_refs, cols)(c))
        back = part if back is None else back + part
    return dffn, dsecond, back


def put_sums(ref, first, second, width):
    ref[0] = jnp.concatenate([first, second, jnp.zeros((6, width), jnp.float32)], axis=0)


def column_sum(value):
    return jnp.sum(value, axis=0, keepdims=True)


def ffn_backward(grad, unit, inverse, slope, shrink, expand, norms, rows):
    tokens, width = grad.shape
    cols = len(shrink[0])
    wide = shrink[0][0].shape[0]

    def kernel(grad_ref, unit_ref, inverse_ref, slope_ref, norm_ref, *refs):
        dffn_ref, dpre_ref, dhid_ref, sum_ref = refs[4 * cols :]
        place = lax.broadcasted_iota(jnp.int32, (rows, 1), 0)
        upstream = jnp.where(place % SEG == 0, 0.0, grad_ref[...])
        unit = unit_ref[...]

        def put(c, value):
            dpre_ref[:, c * wide : (c + 1) * wide] = value

        dffn, dsecond, back = ffn_backward_values(
            upstream,
            unit,
            inverse_ref[...],
            lambda c: slope_ref[:, c * wide : (c + 1) * wide],
            norm_ref[2:3],
            refs[: 2 * cols],
            refs[2 * cols : 4 * cols],
            cols,
            put,
        )
        dffn_ref[...] = dffn
        dhid_ref[...] = dsecond + back
        put_sums(sum_ref, column_sum(upstream * unit), column_sum(upstream), width)

    ins = [grad, unit, inverse, slope, norms] + flat(shrink) + flat(expand)
    return run(
        kernel,
        "ffn_backward",
        (tokens // rows,),
        ins,
        [tile(rows, width), tile(rows, width), tile(rows, 1), tile(rows, cols * wide)]
        + [whole_spec(x) for x in ins[4:]],
        [
            shape(tokens, width),
            shape(tokens, cols * wide),
            shape(tokens, width, kind=jnp.float32),
            shape(tokens // rows, 8, width, kind=jnp.float32),
        ],
        [
            tile(rows, width),
            tile(rows, cols * wide),
            tile(rows, width),
            pl.BlockSpec((1, 8, width), lambda i: (i, 0, 0)),
        ],
        4 * tokens * width * cols * wide,
    )


def ffn_backward_firsts(grad, dheads, unit, inverse, slope, shrink, expand, norms, outs):
    tokens, width = grad.shape
    segs = tokens // SEG
    few = 16
    cols = len(shrink[0])
    wide = shrink[0][0].shape[0]
    by_seg = [x.reshape(segs, SEG, -1) for x in (grad, unit, inverse, slope)]
    outs = [x.reshape(segs, SEG, -1) for x in outs]
    upstream = jnp.concatenate([dheads[:, None], by_seg[0][:, 1:few]], axis=1)

    def kernel(up_ref, unit_ref, inverse_ref, slope_ref, norm_ref, *refs):
        dffn_ref, dpre_ref, dhid_ref, sum_ref = refs[4 * cols + 3 :]
        count = segs * few
        upstream = up_ref[...].reshape(count, width)
        unit = unit_ref[...].reshape(count, width)

        def put(c, value):
            dpre_ref[:, :, c * wide : (c + 1) * wide] = value.reshape(segs, few, wide)

        dffn, dsecond, back = ffn_backward_values(
            upstream,
            unit,
            inverse_ref[...].reshape(count, 1),
            lambda c: slope_ref[:, :, c * wide : (c + 1) * wide].reshape(count, wide),
            norm_ref[2:3],
            refs[: 2 * cols],
            refs[2 * cols : 4 * cols],
            cols,
            put,
        )
        dffn_ref[...] = dffn.reshape(segs, few, width)
        dhid_ref[...] = (dsecond + back).reshape(segs, few, width)
        place = lax.broadcasted_iota(jnp.int32, (count, 1), 0)
        only = jnp.where(place % few == 0, upstream, 0.0)
        put_sums(sum_ref, column_sum(only * unit), column_sum(only), width)

    ins = [upstream] + by_seg[1:] + [norms] + flat(shrink) + flat(expand) + outs
    front = [
        pl.BlockSpec((segs, few, x.shape[2]), lambda i: (0, 0, 0)) for x in [upstream] + by_seg[1:]
    ]
    back_specs = [pl.BlockSpec((segs, few, x.shape[2]), lambda i: (0, 0, 0)) for x in outs]
    first_out = len(ins) - 3
    dffn, dpre, dhid, sums = run(
        kernel,
        "ffn_backward_firsts",
        (1,),
        ins,
        front
        + [whole_spec(x) for x in ins[4:first_out]]
        + [pl.BlockSpec(memory_space=pl.ANY)] * 3,
        [shape(*x.shape, kind=x.dtype) for x in outs] + [shape(1, 8, width, kind=jnp.float32)],
        back_specs + [pl.BlockSpec((1, 8, width), lambda i: (0, 0, 0))],
        4 * segs * few * width * cols * wide,
        {first_out + k: k for k in range(3)},
    )
    return [x.reshape(tokens, -1) for x in (dffn, dpre, dhid)] + [sums]


def attention_backward(dhid, unit, inverse, qkv, keep, project, merge, norms, group, rows, whole):
    tokens, width = dhid.shape
    cols = len(project[0])
    wide = project[0][0].shape[1]
    heads = wide // (3 * HDIM)

    def kernel(dhid_ref, unit_ref, inverse_ref, qkv_ref, keep_ref, norm_ref, *refs):
        project_refs, merge_refs = refs[: 2 * cols], refs[2 * cols : 4 * cols]
        datt_ref, dqkv_ref, dx_ref, sum_ref = refs[4 * cols : 4 * cols + 4]
        upstream = dhid_ref[...]
        unit = unit_ref[...]
        dfirst = kernel_norm_backward(upstream, unit, inverse_ref[...], norm_ref[0:1])
        put_sums(sum_ref, column_sum(upstream * unit), column_sum(upstream), width)
        datt = dfirst.astype(low_type)
        datt_ref[...] = datt
        back = dfirst if whole else None
        if not whole:
            refs[-1][...] = dfirst
        for c in range(cols):
            dmixed = dot_t(datt, across(merge_refs, cols)(c)).astype(low_type)
            blocks = []
            for g in range(rows // group):
                span = slice(g * group, (g + 1) * group)
                allowed = keep_ref[:, span] > 0.5
                parts = [head_parts(qkv_ref[c, span], head) for head in range(heads)]
                incoming = [
                    dmixed[span, head * HDIM : (head + 1) * HDIM] for head in range(heads)
                ]
                dprobs = [dot_t(some, part[2]) for some, part in zip(incoming, parts)]
                probs = softmax([part[:2] for part in parts], allowed)
                centres = [
                    jnp.sum(left * right, axis=1, keepdims=True)
                    for left, right in zip(dprobs, probs)
                ]
                dscores = [
                    (some * (left - centre)).astype(low_type)
                    for some, left, centre in zip(probs, dprobs, centres)
                ]
                pieces = []
                for some, dscore, up, part in zip(probs, dscores, incoming, parts):
                    pieces.append(dot(dscore, part[1]) * HDIM ** (-0.5))
                    pieces.append(dot_rows(dscore, part[0]) * HDIM ** (-0.5))
                    pieces.append(dot_rows(some.astype(low_type), up))
                blocks.append(jnp.concatenate(pieces, axis=1).astype(low_type))
            dqkv = blocks[0] if len(blocks) == 1 else jnp.concatenate(blocks, axis=0)
            dqkv_ref[c] = dqkv
            part = dot_t(dqkv, down(project_refs, cols)(c))
            back = part if back is None else back + part
        dx_ref[...] = back

    ins = [dhid, unit, inverse, qkv, keep, norms] + flat(project) + flat(merge)
    outs = [
        shape(tokens, width),
        shape(cols, tokens, wide),
        shape(tokens, width, kind=jnp.float32),
        shape(tokens // rows, 8, width, kind=jnp.float32),
    ]
    out_specs = [
        tile(rows, width),
        stack_tile(cols, rows, wide),
        tile(rows, width),
        pl.BlockSpec((1, 8, width), lambda i: (i, 0, 0)),
    ]
    if not whole:
        outs.append(shape(tokens, width, kind=jnp.float32))
        out_specs.append(tile(rows, width))
    return run(
        kernel,
        "attention_backward",
        (tokens // rows,),
        ins,
        [
            tile(rows, width),
            tile(rows, width),
            tile(rows, 1),
            stack_tile(cols, rows, wide),
            pl.BlockSpec((1, rows), lambda i: (0, i)),
        ]
        + [whole_spec(x) for x in ins[5:]],
        outs,
        out_specs,
        2 * tokens * width * cols * wide + 10 * tokens * group * cols * heads * HDIM,
    )


def outer_middle(value, attended, expand, shrink, norms):
    tokens, width = value.shape
    cols = len(expand[0])
    wide = expand[0][0].shape[1]

    def kernel(value_ref, attended_ref, norm_ref, *refs):
        unit_ref, inverse_ref, low_ref, active_ref, slope_ref, ffn_ref = refs[4 * cols :]
        hid, unit, inverse = kernel_norm(
            value_ref[...] + attended_ref[...], norm_ref[0:1], norm_ref[1:2]
        )
        low = hid.astype(low_type)
        unit_ref[...] = unit
        inverse_ref[...] = inverse
        low_ref[...] = low
        for c in range(cols):
            span = slice(c * wide, (c + 1) * wide)
            active_ref[:, span], slope_ref[:, span] = gelu_and_slope(
                dot(low, down(refs[: 2 * cols], cols)(c))
            )
        ffn_ref[...] = shrink_values(active_ref[...], refs[2 * cols : 4 * cols], cols)

    ins = [value, attended, norms] + flat(expand) + flat(shrink)
    outs = [
        shape(tokens, width, kind=jnp.float32),
        shape(tokens, 1, kind=jnp.float32),
        shape(tokens, width),
        shape(tokens, cols * wide),
        shape(tokens, cols * wide),
        shape(tokens, width, kind=jnp.float32),
    ]
    return run(
        kernel,
        "outer_middle",
        (1,),
        ins,
        [whole_spec(x) for x in ins],
        outs,
        [whole_spec(x) for x in outs],
        4 * tokens * width * cols * wide,
    )


def outer_turn(unit, ffn, grad, slope, shrink, expand, norms):
    tokens, width = unit.shape
    cols = len(expand[0])
    wide = expand[0][0].shape[1]

    def kernel(unit_ref, ffn_ref, grad_ref, slope_ref, norm_ref, *refs):
        out_ref, dffn_ref, dpre_ref, dsecond_ref, back_ref, sum_ref = refs[4 * cols :]
        hid = unit_ref[...] * norm_ref[0:1] + norm_ref[1:2]
        result, second, inverse = kernel_norm(hid + ffn_ref[...], norm_ref[2:3], norm_ref[3:4])
        out_ref[...] = result
        upstream = grad_ref[...]

        def put(c, value):
            dpre_ref[:, c * wide : (c + 1) * wide] = value

        dffn_ref[...], dsecond_ref[...], back_ref[...] = ffn_backward_values(
            upstream,
            second,
            inverse,
            lambda c: slope_ref[:, c * wide : (c + 1) * wide],
            norm_ref[2:3],
            refs[: 2 * cols],
            refs[2 * cols : 4 * cols],
            cols,
            put,
        )
        put_sums(sum_ref, column_sum(upstream * second), column_sum(upstream), width)

    ins = [unit, ffn, grad, slope, norms] + flat(shrink) + flat(expand)
    outs = [
        shape(tokens, width, kind=jnp.float32),
        shape(tokens, width),
        shape(tokens, cols * wide),
        shape(tokens, width, kind=jnp.float32),
        shape(tokens, width, kind=jnp.float32),
        shape(1, 8, width, kind=jnp.float32),
    ]
    return run(
        kernel,
        "outer_turn",
        (1,),
        ins,
        [whole_spec(x) for x in ins],
        outs,
        [whole_spec(x) for x in outs],
        4 * tokens * width * cols * wide,
    )


def ffn_grads(hid_low, dpre, active, dffn, col):
    dp_count, col_count = lax.axis_size("dp"), lax.axis_size("col")
    half = hid_low.shape[1] // 2
    theirs_first = dot_rows(hid_low[:, half:], dpre).astype(low_type)
    theirs_second = dot_rows(active, dffn[:, half:]).astype(low_type)
    mine_first = dot_rows(hid_low[:, :half], dpre).astype(low_type)
    mine_second = dot_rows(active, dffn[:, :half]).astype(low_type)
    wide = mine_first.shape[1] // col_count
    tall = mine_second.shape[0] // col_count
    low, high = half // dp_count, tall // dp_count
    rows = 2 * low + high

    def kernel(col_ref, mine_a, got_a, mine_b, got_b, out):
        first = mine_a[...].astype(jnp.float32) + got_a[...].astype(jnp.float32)
        second = mine_b[...].astype(jnp.float32) + got_b[...].astype(jnp.float32)
        first = first.astype(low_type)
        second = second.astype(low_type)
        for place in range(dp_count):
            part = first[place * low : (place + 1) * low]
            out[0, place, :low] = part[:, :half]
            out[0, place, low : 2 * low] = part[:, half:]
            out[0, place, 2 * low :] = second[place * high : (place + 1) * high]

    first_spec = pl.BlockSpec((half, wide), lambda j, c: (0, j ^ c[0]))
    second_spec = pl.BlockSpec((tall, half), lambda j, c: (j ^ c[0], 0))
    packed = pl.pallas_call(
        kernel,
        out_shape=jax.ShapeDtypeStruct((col_count, dp_count, rows, half), low_type),
        grid_spec=pltpu.PrefetchScalarGridSpec(
            num_scalar_prefetch=1,
            grid=(col_count,),
            in_specs=[first_spec, first_spec, second_spec, second_spec],
            out_specs=pl.BlockSpec((1, dp_count, rows, half), lambda j, c: (j, 0, 0, 0)),
        ),
        cost_estimate=pl.CostEstimate(
            flops=0, bytes_accessed=6 * col_count * dp_count * rows * half, transcendentals=0
        ),
        name="pack_grads",
    )(col.reshape(1), mine_first, row_swap(theirs_first), mine_second, row_swap(theirs_second))
    return packed, lax.psum_scatter(
        packed.reshape(col_count * dp_count, rows, half), "col", scatter_dimension=0, tiled=True
    )


def row_products(left, right, part):
    cols, tokens, wide = right.shape
    half = left.shape[1] // 2

    def kernel(left_ref, right_ref, out_ref):
        out_ref[0] = dot_rows(left_ref[...], right_ref[0]).astype(low_type)

    return run(
        kernel,
        "row_products",
        (cols,),
        [left, right],
        [
            pl.BlockSpec((tokens, half), lambda c: (0, part)),
            pl.BlockSpec((1, tokens, wide), lambda c: (c, 0, 0)),
        ],
        [shape(cols, half, wide)],
        [pl.BlockSpec((1, half, wide), lambda c: (c, 0, 0))],
        2 * tokens * half * cols * wide,
    )[0]


def attention_grads(x_low, dqkv, mixed, datt, col):
    dp_count, col_count = lax.axis_size("dp"), lax.axis_size("col")
    half = x_low.shape[1] // 2
    wide = dqkv.shape[2]
    got_first = row_swap(row_products(x_low, dqkv, 1))
    got_second = row_swap(dot_rows(mixed, datt[:, half:]).astype(low_type))
    mine_first = row_products(x_low, dqkv, 0)
    mine_second = dot_rows(mixed, datt[:, :half]).astype(low_type)
    tall = mine_second.shape[0] // col_count
    low, high = half // dp_count, tall // dp_count
    rest = wide - half
    rows = low + low // 2 + high

    def kernel(col_ref, mine_a, got_a, mine_b, got_b, out):
        first = mine_a[0].astype(jnp.float32) + got_a[0].astype(jnp.float32)
        second = mine_b[...].astype(jnp.float32) + got_b[...].astype(jnp.float32)
        second = second.astype(low_type)
        for place in range(dp_count):
            part = first[place * low : (place + 1) * low]
            ends = part[:, half:]
            out[0, place, :low] = part[:, :half].astype(low_type)
            out[0, place, low : low + low // 2] = jnp.concatenate(
                [ends[: low // 2], ends[low // 2 :]], axis=1
            ).astype(low_type)
            out[0, place, low + low // 2 :] = second[place * high : (place + 1) * high]

    assert rest * 2 == half
    first_spec = pl.BlockSpec((1, half, wide), lambda j, c: (j ^ c[0], 0, 0))
    second_spec = pl.BlockSpec((tall, half), lambda j, c: (j ^ c[0], 0))
    packed = pl.pallas_call(
        kernel,
        out_shape=jax.ShapeDtypeStruct((col_count, dp_count, rows, half), low_type),
        grid_spec=pltpu.PrefetchScalarGridSpec(
            num_scalar_prefetch=1,
            grid=(col_count,),
            in_specs=[first_spec, first_spec, second_spec, second_spec],
            out_specs=pl.BlockSpec((1, dp_count, rows, half), lambda j, c: (j, 0, 0, 0)),
        ),
        cost_estimate=pl.CostEstimate(
            flops=0, bytes_accessed=6 * col_count * dp_count * rows * half, transcendentals=0
        ),
        name="pack_attention_grads",
    )(col.reshape(1), mine_first, got_first, mine_second, got_second)
    scattered = lax.psum_scatter(
        packed.reshape(col_count * dp_count, rows, half), "col", scatter_dimension=0, tiled=True
    )
    return packed, scattered


def unpack_grads(packed, half, low, high):
    ffn_rows = 2 * low + high
    expand = jnp.concatenate([packed[:low], packed[low : 2 * low]], axis=1)
    shrink = packed[2 * low : ffn_rows]
    rest = packed[ffn_rows:]
    ends = rest[low : low + low // 2]
    ends = jnp.concatenate([ends[:, : half // 2], ends[:, half // 2 :]], axis=0)
    project = jnp.concatenate([rest[:low], ends], axis=1)
    return project, rest[low + low // 2 :], expand, shrink


def halves(value, axis):
    return jnp.split(value, 2, axis=axis)


def first_grad(left, right, through):
    mine_left, theirs_left = halves(left, 1)
    theirs = [dot_rows(theirs_left, block).astype(low_type) for block in right]
    mine = [dot_rows(mine_left, block).astype(low_type) for block in right]
    return scatter_grad(mine, theirs, through)


def second_grad(left, right, through):
    mine_right, theirs_right = halves(right, 1)
    count = lax.axis_size("col")
    theirs = dot_rows(left, theirs_right).astype(low_type)
    mine = dot_rows(left, mine_right).astype(low_type)
    got = row_swap(theirs)
    total = mine.astype(jnp.float32) + got.astype(jnp.float32)
    return dp_scatter_sum(plane_sum(jnp.split(total, count, 0), through))


def to_tokens(value, row):
    parts = value.reshape((2, -1) + value.shape[1:])
    mine = lax.dynamic_index_in_dim(parts, row, 0, False)
    theirs = lax.dynamic_index_in_dim(parts, 1 - row, 0, False)
    return jnp.concatenate([mine, row_swap(theirs)], axis=1)


def to_features(value, row):
    mine, theirs = halves(value, 1)
    got = row_swap(theirs)
    first = jnp.where(row == 0, mine, got)
    second = jnp.where(row == 0, got, mine)
    return jnp.concatenate([first, second], axis=0)


def swap_features(value):
    first, second = halves(value, 1)
    return jnp.concatenate([second, first], axis=1)


def swap_rows(value):
    first, second = halves(value, 0)
    return jnp.concatenate([second, first], axis=0)


def local(
    hidden,
    lengths,
    inner_project,
    inner_merge,
    inner_expand,
    inner_shrink,
    inner_norms,
    outer_places,
    outer_project,
    outer_merge,
    outer_expand,
    outer_shrink,
    outer_norms,
    out_grad,
):
    dp_count, row_count, col_count = (lax.axis_size(name) for name in ("dp", "row", "col"))
    dp, row, col = (lax.axis_index(name) for name in ("dp", "row", "col"))
    everyone = ("dp", "row", "col")
    device_count = dp_count * row_count * col_count
    value = to_tokens(hidden, row)
    grad_in = to_tokens(out_grad, row)
    tokens, width = value.shape
    segs = tokens // SEG

    small = jnp.concatenate([inner_norms, outer_norms, outer_places], axis=1)
    small = lax.all_to_all(
        jnp.broadcast_to(small[None], (device_count,) + small.shape), everyone, 0, 0, tiled=True
    )
    small = small.reshape((dp_count, row_count, -1) + small.shape[2:])
    small = jnp.concatenate(
        [
            lax.dynamic_index_in_dim(small, row, 1, False).reshape(-1, small.shape[-1]),
            lax.dynamic_index_in_dim(small, 1 - row, 1, False).reshape(-1, small.shape[-1]),
        ],
        axis=0,
    )
    vectors = small.T
    inner_gains = vectors[0:4]
    outer_gains = vectors[4:8]
    places = vectors[8:]

    length = lax.dynamic_index_in_dim(lengths, col // 2, 0, False)
    half = col % 2
    seg_own = (half * 2 + row) * segs + jnp.arange(segs, dtype=jnp.int32)
    spot = (seg_own[:, None] * SEG + jnp.arange(SEG, dtype=jnp.int32)[None]).reshape(tokens)
    valid = (spot < length).astype(jnp.float32)
    keep_tok = ((spot < length) | (spot % SEG == 0)).astype(jnp.float32)
    seg_all = jnp.concatenate(
        [
            (h * 2 + r) * segs + jnp.arange(segs, dtype=jnp.int32)
            for h in (half, 1 - half)
            for r in (row, 1 - row)
        ]
    )
    keep_seg = (seg_all * SEG < length).astype(jnp.float32)
    one_hot = (seg_own[:, None] == jnp.arange(NSEG, dtype=jnp.int32)[None]).astype(jnp.float32)

    keep_row = keep_tok[None]
    rows_tile = 2 * SEG
    inner, outer_of, (x_in, qkv, mixed_in) = gather_weights(
        (inner_project, inner_merge, inner_expand, inner_shrink),
        (outer_project, outer_merge, outer_expand, outer_shrink),
        lambda project: project_attend(value, keep_row, project, None, SEG, rows_tile),
    )
    unit_one, inverse_one, hid_in, active_in, slope = merge_expand(
        value, mixed_in, inner[1], inner[2], inner_gains, rows_tile
    )
    inner_out, unit_two, inverse_two = shrink_norm(
        unit_one, active_in, inner[3], inner_gains, rows_tile
    )
    grid = inner_out.reshape(segs, SEG, width)
    masked_grad = (grad_in * valid[:, None]).reshape(segs, SEG, width)
    heads_in = grid[:, 0] + jnp.dot(
        one_hot, places, precision=highest, preferred_element_type=jnp.float32
    )
    rows = jnp.concatenate([heads_in, masked_grad[:, 0]], axis=0)
    rows = jnp.stack([rows, swap_features(row_swap(rows))]).reshape(2, 2, segs, width)
    rows = jnp.stack([rows, col_swap(rows, 1)])
    rows = rows.transpose(2, 0, 1, 3, 4).reshape(2, NSEG, width)

    def join(partial_sum):
        return partial_sum + swap_rows(col_swap(partial_sum, 1))

    flat_grad = masked_grad.reshape(tokens, width)
    main = ffn_backward(
        flat_grad, unit_two, inverse_two, slope, inner[3], inner[2], inner_gains, rows_tile
    )
    outer = outer_of((hid_in, inner_out, main[3]))
    rows = after(rows, main[3])
    x_low, o_qkv, mixed, attended = project_attend(
        rows[0], keep_seg[None], outer[0], outer[1], NSEG, NSEG
    )
    o_unit, o_inverse, hid_low, active, o_slope, ffn = outer_middle(
        rows[0], join(attended), outer[2], outer[3], outer_gains
    )
    outer_out, dffn, dpre, dsecond, back, o_second = outer_turn(
        o_unit, join(ffn), rows[1], o_slope, outer[3], outer[2], outer_gains
    )
    datt, dqkv, back, o_first, dfirst = attention_backward(
        dsecond + join(back),
        o_unit,
        o_inverse,
        o_qkv,
        keep_seg[None],
        outer[0],
        outer[1],
        outer_gains,
        NSEG,
        NSEG,
        False,
    )
    dheads = dfirst + join(back)
    outer_norm_grad = jnp.concatenate([o_first[0, :2], o_second[0, :2]], axis=0).T
    dheads = dheads[:segs]
    layer_out = (
        jnp.concatenate([outer_out[:segs, None], grid[:, 1:]], axis=1).reshape(tokens, width)
        * valid[:, None]
    )
    places_grad = jnp.dot(dheads.T, one_hot, precision=highest, preferred_element_type=jnp.float32)

    dffn_in, dpre_in, dhid_in, few_sums = ffn_backward_firsts(
        flat_grad,
        dheads,
        unit_two,
        inverse_two,
        slope,
        inner[3],
        inner[2],
        inner_gains,
        main[:3],
    )
    wide_dp = dp_count > 4
    if not wide_dp:
        gate, ffn_packed = ffn_grads(hid_in, dpre_in, active_in, dffn_in, col)
        dhid_in = after(dhid_in, gate)
    datt_in, dqkv_in, input_grad, first_sums = attention_backward(
        dhid_in,
        unit_one,
        inverse_one,
        qkv,
        keep_row,
        inner[0],
        inner[1],
        inner_gains,
        SEG,
        rows_tile,
        True,
    )
    inner_norm_grad = jnp.concatenate(
        [jnp.sum(first_sums, 0)[:2], jnp.sum(main[3], 0)[:2] + few_sums[0, :2]], axis=0
    ).T
    if wide_dp:
        inner_grads = (
            first_grad(x_in, dqkv_in, 1),
            second_grad(mixed_in, datt_in, 2),
            first_grad(hid_in, jnp.split(dpre_in, col_count, 1), 1),
            second_grad(active_in, dffn_in, 2),
        )
        gate = None
    else:
        gate, attention_packed = attention_grads(x_in, dqkv_in, mixed_in, datt_in, col)
    if gate is not None:
        dffn = after(dffn, gate)
    shared = [halves(part, 1)[0] for part in (x_low, hid_low, datt, dffn)]
    own, over = zip(*([halves(part, 1) for part in (active, dpre, mixed)] + [tuple(dqkv)]))
    packed = jnp.concatenate(
        [
            jnp.concatenate(shared + list(own), axis=1),
            col_swap(jnp.concatenate(shared + list(over), axis=1), 2),
        ],
        axis=0,
    )
    if dp_count > 4:
        packed = lax.all_gather(packed, "dp", axis=0, tiled=True)
    else:
        packed = jnp.concatenate(
            [packed] + [dp_shift(packed, step) for step in range(1, dp_count)], axis=0
        )
    if not wide_dp:
        grads = after(jnp.concatenate([ffn_packed, attention_packed], axis=1), packed)
        grads = lax.psum_scatter(grads, "dp", scatter_dimension=0, tiled=True)[0]
        inner_grads = unpack_grads(
            grads.astype(jnp.float32), width // 2, inner_expand.shape[0], inner_shrink.shape[0]
        )
    ends = []
    for part in shared + list(own):
        ends.append((ends[-1] if ends else 0) + part.shape[1])
    x_all, hid_all, datt_all, dffn_all, active_all, dpre_all, mixed_all, dqkv_all = jnp.split(
        packed, ends[:-1], axis=1
    )

    def own_rows(product):
        return lax.dynamic_index_in_dim(
            product.reshape((dp_count, -1) + product.shape[1:]), dp, 0, False
        )

    outer_grads = (
        own_rows(dot_rows(x_all, dqkv_all)),
        own_rows(dot_rows(mixed_all, datt_all)),
        own_rows(dot_rows(hid_all, dpre_all)),
        own_rows(dot_rows(active_all, dffn_all)),
    )

    small_grad = jnp.concatenate([inner_norm_grad, 0.25 * outer_norm_grad, places_grad], axis=1)
    columns = small_grad.shape[1]
    blocks = small_grad.reshape(2, dp_count, col_count, -1, columns)
    blocks = jnp.where(row == 0, blocks, blocks[::-1]).transpose(1, 0, 2, 3, 4)
    blocks = lax.all_to_all(
        blocks.reshape(device_count, -1, columns), everyone, 0, 0, tiled=True
    )
    small_sum = jnp.sum(blocks, axis=0)
    return (
        to_features(layer_out, row),
        to_features(input_grad, row),
        inner_grads[0],
        inner_grads[1],
        inner_grads[2],
        inner_grads[3],
        small_sum[:, 0:4],
        small_sum[:, 8:],
        outer_grads[0],
        outer_grads[1],
        outer_grads[2],
        outer_grads[3],
        small_sum[:, 4:8],
    )


def solution(mesh):
    tokens = P(("dp", "col"), "row")
    first = P(("row", "dp"), "col")
    second = P(("col", "dp"), "row")
    small = P(("row", "dp", "col"), None)
    weights = (first, second, first, second)
    return jax.shard_map(
        local,
        mesh=mesh,
        in_specs=(tokens, P("dp")) + weights + (small, small) + weights + (small, tokens),
        out_specs=(tokens, tokens) + weights + (small, small) + weights + (small,),
        check_vma=False,
    )
```

```python
import jax
import jax.numpy as jnp
from jax import lax
from jax.experimental import pallas as pl
from jax.experimental.pallas import tpu as pltpu
from jax.sharding import PartitionSpec as P


HDIM = 64
SEG = 128
NSEG = 16
epsilon = 1e-06
highest = lax.Precision.HIGHEST
low_type = jnp.bfloat16


def dot(left, right):
    return jnp.dot(left, right, preferred_element_type=jnp.float32)


def dot_t(left, right):
    return lax.dot_general(
        left, right, (((1,), (1,)), ((), ())), preferred_element_type=jnp.float32
    )


def dot_rows(left, right):
    return lax.dot_general(
        left, right, (((0,), (0,)), ((), ())), preferred_element_type=jnp.float32
    )


def row_swap(value):
    return lax.ppermute(value, "row", [(0, 1), (1, 0)])


def col_swap(value, mask):
    return lax.ppermute(value, "col", [(i, i ^ mask) for i in range(lax.axis_size("col"))])


def dp_shift(value, step):
    count = lax.axis_size("dp")
    return lax.ppermute(value, "dp", [(i, (i + step) % count) for i in range(count)])


def after(value, earlier):
    return lax.optimization_barrier((value, earlier))[0]


def dp_pieces(value):
    count = lax.axis_size("dp")
    return [value] + [dp_shift(value, step) for step in range(1, count)]


def place_pieces(pieces, cut=None):
    count = len(pieces)
    height, width = pieces[0].shape
    bounds = (0, height) if cut is None else (0, cut, height)
    spans = list(zip(bounds[:-1], bounds[1:]))

    def kernel(place_ref, *refs):
        for step in range(count):
            at = lax.rem(place_ref[0] - step + count, count)
            for (low, high), out in zip(spans, refs[count:]):
                size = high - low
                out[pl.ds(pl.multiple_of(at * size, 16), size), :] = refs[step][low:high]

    whole = pl.BlockSpec(memory_space=pltpu.VMEM)
    outs = [
        jax.ShapeDtypeStruct((count * (high - low), width), pieces[0].dtype) for low, high in spans
    ]
    placed = pl.pallas_call(
        kernel,
        out_shape=outs,
        grid_spec=pltpu.PrefetchScalarGridSpec(
            num_scalar_prefetch=1,
            grid=(),
            in_specs=[whole] * count,
            out_specs=[whole] * len(outs),
        ),
        cost_estimate=pl.CostEstimate(
            flops=0, bytes_accessed=4 * count * height * width, transcendentals=0
        ),
        name="place_pieces",
    )(lax.axis_index("dp").reshape(1), *pieces)
    return placed[0] if cut is None else placed


def dp_scatter_sum(value):
    count = lax.axis_size("dp")
    if count > 4:
        return lax.psum_scatter(value, "dp", scatter_dimension=0, tiled=True)
    place = lax.axis_index("dp")
    parts = value.reshape((count, -1) + value.shape[1:])
    total = lax.dynamic_index_in_dim(parts, place, 0, False)
    for step in range(1, count):
        piece = lax.dynamic_index_in_dim(parts, (place + step) % count, 0, False)
        total = total + dp_shift(piece.astype(low_type), step).astype(jnp.float32)
    return total


def plane_blocks(own, through):
    side = col_swap(own, 1)
    over = col_swap(own, 2)
    far = col_swap(over, 1) if through == 1 else col_swap(side, 2)
    mine = (own, side, over, far)
    return (mine, tuple(row_swap(block) for block in mine))


def pair_blocks(own):
    mine = (own, col_swap(own, 2))
    return (mine, tuple(row_swap(block) for block in mine))


def gather_wide(inner_shards, outer_shards, first_use):
    inner_own, outer_own = (
        [lax.all_gather(shard, "dp", axis=0, tiled=True) for shard in group]
        for group in (inner_shards, outer_shards)
    )
    inner = [plane_blocks(own, through) for own, through in zip(inner_own, (1, 2, 1, 2))]
    outer = [pair_blocks(own) for own in outer_own]
    steps = (lambda gate: outer[0], lambda gate: (outer[1], outer[3]), lambda gate: outer[2])
    return inner, steps, first_use(inner[0]), (inner_own[0],) * 3


def gather_weights(inner_shards, outer_shards, first_use):
    inner_shards = [shard.astype(low_type) for shard in inner_shards]
    outer_shards = [shard.astype(low_type) for shard in outer_shards]
    if lax.axis_size("dp") > 4:
        return gather_wide(inner_shards, outer_shards, first_use)
    pieces = dp_pieces(inner_shards[0])
    merge_pieces = dp_pieces(inner_shards[1])
    own = place_pieces(pieces)
    expand_pieces = dp_pieces(after(inner_shards[2], own))
    side, over = col_swap(own, 1), col_swap(own, 2)
    project = both_rows((own, side, over, col_swap(after(over, merge_pieces), 1)))
    own = place_pieces(after(merge_pieces, (expand_pieces, project[0][1])))
    side, over = col_swap(own, 1), col_swap(own, 2)
    far = col_swap(side, 2)
    merge = both_rows((own, side, over, far))
    own = place_pieces(after(expand_pieces, (side, over, project[0][3])))
    shrink_pieces = dp_pieces(after(inner_shards[3], expand_pieces))
    side, over = col_swap(own, 1), col_swap(own, 2)
    used = first_use(after(project, own))
    far_expand = col_swap(after(over, shrink_pieces), 1)
    expand = both_rows((own, side, over, far_expand))
    own = place_pieces(after(shrink_pieces, (side, over, far, used[0])))
    side, over = col_swap(own, 1), col_swap(own, 2)
    far = col_swap(after(side, far_expand), 2)
    shrink = both_rows((own, side, over, far))
    rows = jnp.concatenate([outer_shards[1], outer_shards[3]], axis=0)
    first = dp_pieces(after(outer_shards[0], shrink_pieces))
    second = dp_pieces(after(rows, first[1]))
    third = dp_pieces(after(outer_shards[2], second[1]))

    def outer_project(gate):
        return pair_blocks(place_pieces(after(first, gate)))

    def outer_rows(gate):
        merge, shrink = place_pieces(after(second, gate), outer_shards[1].shape[0])
        return pair_blocks(merge), pair_blocks(shrink)

    def outer_expand(gate):
        own = place_pieces(after(third, gate))
        return pair_blocks(own)

    gates = (first, second, third)
    return (project, merge, expand, shrink), (outer_project, outer_rows, outer_expand), used, gates


def both_rows(mine):
    return (mine, tuple(row_swap(block) for block in mine))


def plane_sum(sums, through):
    other = 3 - through
    own = sums[0] + col_swap(sums[through].astype(low_type), through).astype(jnp.float32)
    onward = sums[other] + col_swap(sums[3].astype(low_type), through).astype(jnp.float32)
    return own + col_swap(onward.astype(low_type), other).astype(jnp.float32)


def scatter_grad(mine, theirs, through):
    sums = [
        block.astype(jnp.float32) + row_swap(sent).astype(jnp.float32)
        for block, sent in zip(mine, theirs)
    ]
    return dp_scatter_sum(plane_sum(sums, through))


def whole_spec(array):
    return pl.BlockSpec(
        array.shape, lambda i: (0,) * array.ndim, pipeline_mode=pl.Buffered(1)
    )


def flat(blocks):
    return [block for half in blocks for block in half]


def grouped(refs, cols):
    return (refs[:cols], refs[cols : 2 * cols])


def down(refs, cols):
    return lambda c: jnp.concatenate([refs[c][...], refs[cols + c][...]], axis=0)


def across(refs, cols):
    return lambda c: jnp.concatenate([refs[c][...], refs[cols + c][...]], axis=1)


def kernel_norm(value, gain, shift):
    average = jnp.mean(value, axis=1, keepdims=True)
    centred = value - average
    inverse = lax.rsqrt(jnp.mean(centred * centred, axis=1, keepdims=True) + epsilon)
    unit = centred * inverse
    return unit * gain + shift, unit, inverse


def kernel_norm_backward(upstream, unit, inverse, gain):
    scaled = upstream * gain
    centre = jnp.mean(scaled, axis=1, keepdims=True)
    slope = jnp.mean(scaled * unit, axis=1, keepdims=True)
    return inverse * (scaled - centre - unit * slope)


def gelu_and_slope(value):
    share = 0.5 + 0.5 * lax.erf(value * 0.7071067811865476)
    density = 0.3989422804014327 * jnp.exp(-0.5 * value * value)
    return (value * share).astype(low_type), (share + value * density).astype(low_type)


def softmax(pairs, allowed):
    scores = [dot_t(query, key_part) * HDIM ** (-0.5) for query, key_part in pairs]
    scores = [jnp.where(allowed, one, -1000000000.0) for one in scores]
    tops = [jnp.max(one, axis=1, keepdims=True) for one in scores]
    expos = [jnp.exp(one - top) for one, top in zip(scores, tops)]
    shares = [1.0 / jnp.sum(expo, axis=1, keepdims=True) for expo in expos]
    return [expo * share for expo, share in zip(expos, shares)]


def head_parts(qkv, head):
    start = head * 3 * HDIM
    return [qkv[:, start + k * HDIM : start + (k + 1) * HDIM] for k in range(3)]


def run(kernel, grid, ins, in_specs, outs, out_specs, flops, aliases=None):
    moved = sum(x.size * x.dtype.itemsize for x in list(ins) + list(outs))
    return pl.pallas_call(
        kernel,
        out_shape=outs,
        grid=grid,
        in_specs=in_specs,
        out_specs=out_specs,
        input_output_aliases=aliases or {},
        cost_estimate=pl.CostEstimate(flops=flops, bytes_accessed=moved, transcendentals=0),
    )(*ins)


def shape(*dims, kind=low_type):
    return jax.ShapeDtypeStruct(dims, kind)


def tile(rows, width):
    return pl.BlockSpec((rows, width), lambda i: (i, 0))


def stack_tile(cols, rows, width):
    return pl.BlockSpec((cols, rows, width), lambda i: (0, i, 0))


def project_attend(value, keep, project, merge, group, rows):
    tokens, width = value.shape
    cols = len(project[0])
    wide = project[0][0].shape[1]
    heads = wide // (3 * HDIM)
    out_width = cols * heads * HDIM
    merge_in = flat(merge) if merge else []

    def kernel(value_ref, keep_ref, *refs):
        weight = down(refs, cols)
        merge_refs = refs[2 * cols : 2 * cols + len(merge_in)]
        low_ref, qkv_ref, mixed_ref = refs[2 * cols + len(merge_in) :][:3]
        low = value_ref[...].astype(low_type)
        low_ref[...] = low
        qkvs = []
        for c in range(cols):
            qkvs.append(dot(low, weight(c)).astype(low_type))
            qkv_ref[c] = qkvs[c]
        for g in range(rows // group):
            span = slice(g * group, (g + 1) * group)
            allowed = keep_ref[:, span] > 0.5
            outs = []
            for c in range(cols):
                parts = [head_parts(qkvs[c][span], head) for head in range(heads)]
                probs = softmax([part[:2] for part in parts], allowed)
                outs += [
                    dot(some.astype(low_type), part[2]) for some, part in zip(probs, parts)
                ]
            mixed_ref[span] = jnp.concatenate(outs, axis=1).astype(low_type)
        if merge_in:
            mixed = mixed_ref[...]
            for r, half in enumerate(grouped(merge_refs, cols)):
                joined = jnp.concatenate([ref[...] for ref in half], axis=0)
                size = joined.shape[1]
                refs[-1][:, r * size : (r + 1) * size] = dot(mixed, joined)

    ins = [value, keep] + flat(project) + merge_in
    outs = [
        shape(tokens, width),
        shape(cols, tokens, wide),
        shape(tokens, out_width),
    ]
    out_specs = [tile(rows, width), stack_tile(cols, rows, wide), tile(rows, out_width)]
    if merge_in:
        outs.append(shape(tokens, width, kind=jnp.float32))
        out_specs.append(tile(rows, width))
    return run(
        kernel,
        (tokens // rows,),
        ins,
        [tile(rows, width), pl.BlockSpec((1, rows), lambda i: (0, i))]
        + [whole_spec(x) for x in ins[2:]],
        outs,
        out_specs,
        2 * tokens * width * cols * wide + 4 * tokens * group * out_width,
    )


def merge_values(mixed, merge_refs, cols):
    parts = [
        dot(mixed, jnp.concatenate([ref[...] for ref in half], axis=0))
        for half in grouped(merge_refs, cols)
    ]
    return jnp.concatenate(parts, axis=1)


def merge_expand(value, mixed, merge, expand, norms, rows):
    tokens, width = value.shape
    cols = len(expand[0])
    wide = expand[0][0].shape[1]

    def kernel(value_ref, mixed_ref, norm_ref, *refs):
        merge_refs, expand_refs = refs[: 2 * cols], refs[2 * cols : 4 * cols]
        unit_ref, inverse_ref, low_ref, active_ref, slope_ref = refs[4 * cols :]
        attended = merge_values(mixed_ref[...], merge_refs, cols)
        hid, unit, inverse = kernel_norm(
            value_ref[...] + attended, norm_ref[0:1], norm_ref[1:2]
        )
        low = hid.astype(low_type)
        unit_ref[...] = unit
        inverse_ref[...] = inverse
        low_ref[...] = low
        weight = down(expand_refs, cols)
        for c in range(cols):
            span = slice(c * wide, (c + 1) * wide)
            active_ref[:, span], slope_ref[:, span] = gelu_and_slope(dot(low, weight(c)))

    ins = [value, mixed, norms] + flat(merge) + flat(expand)
    return run(
        kernel,
        (tokens // rows,),
        ins,
        [tile(rows, width), tile(rows, width)] + [whole_spec(x) for x in ins[2:]],
        [
            shape(tokens, width, kind=jnp.float32),
            shape(tokens, 1, kind=jnp.float32),
            shape(tokens, width),
            shape(tokens, cols * wide),
            shape(tokens, cols * wide),
        ],
        [tile(rows, width), tile(rows, 1), tile(rows, width)] + [tile(rows, cols * wide)] * 2,
        2 * tokens * width * (width + cols * wide),
    )


def shrink_values(active, shrink_refs, cols):
    parts = [
        dot(active, jnp.concatenate([ref[...] for ref in half], axis=0))
        for half in grouped(shrink_refs, cols)
    ]
    return jnp.concatenate(parts, axis=1)


def shrink_norm(unit, active, shrink, norms, rows):
    tokens, width = unit.shape
    cols = len(shrink[0])

    def kernel(unit_ref, active_ref, norm_ref, *refs):
        out_ref, second_ref, inverse_ref = refs[2 * cols :]
        hid = unit_ref[...] * norm_ref[0:1] + norm_ref[1:2]
        ffn = shrink_values(active_ref[...], refs[: 2 * cols], cols)
        out_ref[...], second_ref[...], inverse_ref[...] = kernel_norm(
            hid + ffn, norm_ref[2:3], norm_ref[3:4]
        )

    ins = [unit, active, norms] + flat(shrink)
    return run(
        kernel,
        (tokens // rows,),
        ins,
        [tile(rows, width), tile(rows, active.shape[1])] + [whole_spec(x) for x in ins[2:]],
        [
            shape(tokens, width, kind=jnp.float32),
            shape(tokens, width, kind=jnp.float32),
            shape(tokens, 1, kind=jnp.float32),
        ],
        [tile(rows, width), tile(rows, width), tile(rows, 1)],
        2 * tokens * width * active.shape[1],
    )


def ffn_backward_values(upstream, unit, inverse, slope, gain, shrink_refs, expand_refs, cols, put):
    dsecond = kernel_norm_backward(upstream, unit, inverse, gain)
    dffn = dsecond.astype(low_type)
    back = None
    for c in range(cols):
        dactive = dot_t(dffn, across(shrink_refs, cols)(c))
        dpre = (dactive * slope(c).astype(jnp.float32)).astype(low_type)
        put(c, dpre)
        part = dot_t(dpre, down(expand_refs, cols)(c))
        back = part if back is None else back + part
    return dffn, dsecond, back


def put_sums(ref, first, second, width):
    ref[0] = jnp.concatenate([first, second, jnp.zeros((6, width), jnp.float32)], axis=0)


def column_sum(value):
    return jnp.sum(value, axis=0, keepdims=True)


def ffn_backward(grad, unit, inverse, slope, shrink, expand, norms, rows):
    tokens, width = grad.shape
    cols = len(shrink[0])
    wide = shrink[0][0].shape[0]

    def kernel(grad_ref, unit_ref, inverse_ref, slope_ref, norm_ref, *refs):
        dffn_ref, dpre_ref, dhid_ref, sum_ref = refs[4 * cols :]
        place = lax.broadcasted_iota(jnp.int32, (rows, 1), 0)
        upstream = jnp.where(place % SEG == 0, 0.0, grad_ref[...])
        unit = unit_ref[...]

        def put(c, value):
            dpre_ref[:, c * wide : (c + 1) * wide] = value

        dffn, dsecond, back = ffn_backward_values(
            upstream,
            unit,
            inverse_ref[...],
            lambda c: slope_ref[:, c * wide : (c + 1) * wide],
            norm_ref[2:3],
            refs[: 2 * cols],
            refs[2 * cols : 4 * cols],
            cols,
            put,
        )
        dffn_ref[...] = dffn
        dhid_ref[...] = dsecond + back
        put_sums(sum_ref, column_sum(upstream * unit), column_sum(upstream), width)

    ins = [grad, unit, inverse, slope, norms] + flat(shrink) + flat(expand)
    return run(
        kernel,
        (tokens // rows,),
        ins,
        [tile(rows, width), tile(rows, width), tile(rows, 1), tile(rows, cols * wide)]
        + [whole_spec(x) for x in ins[4:]],
        [
            shape(tokens, width),
            shape(tokens, cols * wide),
            shape(tokens, width, kind=jnp.float32),
            shape(tokens // rows, 8, width, kind=jnp.float32),
        ],
        [
            tile(rows, width),
            tile(rows, cols * wide),
            tile(rows, width),
            pl.BlockSpec((1, 8, width), lambda i: (i, 0, 0)),
        ],
        4 * tokens * width * cols * wide,
    )


def ffn_backward_firsts(grad, dheads, unit, inverse, slope, shrink, expand, norms, outs):
    tokens, width = grad.shape
    segs = tokens // SEG
    few = 16
    cols = len(shrink[0])
    wide = shrink[0][0].shape[0]
    by_seg = [x.reshape(segs, SEG, -1) for x in (grad, unit, inverse, slope)]
    outs = [x.reshape(segs, SEG, -1) for x in outs]
    upstream = jnp.concatenate([dheads[:, None], by_seg[0][:, 1:few]], axis=1)

    def kernel(up_ref, unit_ref, inverse_ref, slope_ref, norm_ref, *refs):
        dffn_ref, dpre_ref, dhid_ref, sum_ref = refs[4 * cols + 3 :]
        count = segs * few
        upstream = up_ref[...].reshape(count, width)
        unit = unit_ref[...].reshape(count, width)

        def put(c, value):
            dpre_ref[:, :, c * wide : (c + 1) * wide] = value.reshape(segs, few, wide)

        dffn, dsecond, back = ffn_backward_values(
            upstream,
            unit,
            inverse_ref[...].reshape(count, 1),
            lambda c: slope_ref[:, :, c * wide : (c + 1) * wide].reshape(count, wide),
            norm_ref[2:3],
            refs[: 2 * cols],
            refs[2 * cols : 4 * cols],
            cols,
            put,
        )
        dffn_ref[...] = dffn.reshape(segs, few, width)
        dhid_ref[...] = (dsecond + back).reshape(segs, few, width)
        place = lax.broadcasted_iota(jnp.int32, (count, 1), 0)
        only = jnp.where(place % few == 0, upstream, 0.0)
        put_sums(sum_ref, column_sum(only * unit), column_sum(only), width)

    ins = [upstream] + by_seg[1:] + [norms] + flat(shrink) + flat(expand) + outs
    front = [
        pl.BlockSpec((segs, few, x.shape[2]), lambda i: (0, 0, 0)) for x in [upstream] + by_seg[1:]
    ]
    back_specs = [pl.BlockSpec((segs, few, x.shape[2]), lambda i: (0, 0, 0)) for x in outs]
    first_out = len(ins) - 3
    dffn, dpre, dhid, sums = run(
        kernel,
        (1,),
        ins,
        front
        + [whole_spec(x) for x in ins[4:first_out]]
        + [pl.BlockSpec(memory_space=pl.ANY)] * 3,
        [shape(*x.shape, kind=x.dtype) for x in outs] + [shape(1, 8, width, kind=jnp.float32)],
        back_specs + [pl.BlockSpec((1, 8, width), lambda i: (0, 0, 0))],
        4 * segs * few * width * cols * wide,
        {first_out + k: k for k in range(3)},
    )
    return [x.reshape(tokens, -1) for x in (dffn, dpre, dhid)] + [sums]


def attention_backward(dhid, unit, inverse, qkv, keep, project, merge, norms, group, rows, whole):
    tokens, width = dhid.shape
    cols = len(project[0])
    wide = project[0][0].shape[1]
    heads = wide // (3 * HDIM)

    def kernel(dhid_ref, unit_ref, inverse_ref, qkv_ref, keep_ref, norm_ref, *refs):
        project_refs, merge_refs = refs[: 2 * cols], refs[2 * cols : 4 * cols]
        datt_ref, dqkv_ref, dx_ref, sum_ref = refs[4 * cols : 4 * cols + 4]
        upstream = dhid_ref[...]
        unit = unit_ref[...]
        dfirst = kernel_norm_backward(upstream, unit, inverse_ref[...], norm_ref[0:1])
        put_sums(sum_ref, column_sum(upstream * unit), column_sum(upstream), width)
        datt = dfirst.astype(low_type)
        datt_ref[...] = datt
        back = dfirst if whole else None
        if not whole:
            refs[-1][...] = dfirst
        for c in range(cols):
            dmixed = dot_t(datt, across(merge_refs, cols)(c)).astype(low_type)
            blocks = []
            for g in range(rows // group):
                span = slice(g * group, (g + 1) * group)
                allowed = keep_ref[:, span] > 0.5
                parts = [head_parts(qkv_ref[c, span], head) for head in range(heads)]
                incoming = [
                    dmixed[span, head * HDIM : (head + 1) * HDIM] for head in range(heads)
                ]
                dprobs = [dot_t(some, part[2]) for some, part in zip(incoming, parts)]
                probs = softmax([part[:2] for part in parts], allowed)
                centres = [
                    jnp.sum(left * right, axis=1, keepdims=True)
                    for left, right in zip(dprobs, probs)
                ]
                dscores = [
                    (some * (left - centre)).astype(low_type)
                    for some, left, centre in zip(probs, dprobs, centres)
                ]
                pieces = []
                for some, dscore, up, part in zip(probs, dscores, incoming, parts):
                    pieces.append(dot(dscore, part[1]) * HDIM ** (-0.5))
                    pieces.append(dot_rows(dscore, part[0]) * HDIM ** (-0.5))
                    pieces.append(dot_rows(some.astype(low_type), up))
                blocks.append(jnp.concatenate(pieces, axis=1).astype(low_type))
            dqkv = blocks[0] if len(blocks) == 1 else jnp.concatenate(blocks, axis=0)
            dqkv_ref[c] = dqkv
            part = dot_t(dqkv, down(project_refs, cols)(c))
            back = part if back is None else back + part
        dx_ref[...] = back

    ins = [dhid, unit, inverse, qkv, keep, norms] + flat(project) + flat(merge)
    outs = [
        shape(tokens, width),
        shape(cols, tokens, wide),
        shape(tokens, width, kind=jnp.float32),
        shape(tokens // rows, 8, width, kind=jnp.float32),
    ]
    out_specs = [
        tile(rows, width),
        stack_tile(cols, rows, wide),
        tile(rows, width),
        pl.BlockSpec((1, 8, width), lambda i: (i, 0, 0)),
    ]
    if not whole:
        outs.append(shape(tokens, width, kind=jnp.float32))
        out_specs.append(tile(rows, width))
    return run(
        kernel,
        (tokens // rows,),
        ins,
        [
            tile(rows, width),
            tile(rows, width),
            tile(rows, 1),
            stack_tile(cols, rows, wide),
            pl.BlockSpec((1, rows), lambda i: (0, i)),
        ]
        + [whole_spec(x) for x in ins[5:]],
        outs,
        out_specs,
        2 * tokens * width * cols * wide + 10 * tokens * group * cols * heads * HDIM,
    )


def outer_middle(value, attended, expand, shrink, norms):
    tokens, width = value.shape
    cols = len(expand[0])
    wide = expand[0][0].shape[1]

    def kernel(value_ref, attended_ref, norm_ref, *refs):
        unit_ref, inverse_ref, low_ref, active_ref, slope_ref, ffn_ref = refs[4 * cols :]
        hid, unit, inverse = kernel_norm(
            value_ref[...] + attended_ref[...], norm_ref[0:1], norm_ref[1:2]
        )
        low = hid.astype(low_type)
        unit_ref[...] = unit
        inverse_ref[...] = inverse
        low_ref[...] = low
        for c in range(cols):
            span = slice(c * wide, (c + 1) * wide)
            active_ref[:, span], slope_ref[:, span] = gelu_and_slope(
                dot(low, down(refs[: 2 * cols], cols)(c))
            )
        ffn_ref[...] = shrink_values(active_ref[...], refs[2 * cols : 4 * cols], cols)

    ins = [value, attended, norms] + flat(expand) + flat(shrink)
    outs = [
        shape(tokens, width, kind=jnp.float32),
        shape(tokens, 1, kind=jnp.float32),
        shape(tokens, width),
        shape(tokens, cols * wide),
        shape(tokens, cols * wide),
        shape(tokens, width, kind=jnp.float32),
    ]
    return run(
        kernel,
        (1,),
        ins,
        [whole_spec(x) for x in ins],
        outs,
        [whole_spec(x) for x in outs],
        4 * tokens * width * cols * wide,
    )


def outer_turn(unit, ffn, grad, slope, shrink, expand, norms):
    tokens, width = unit.shape
    cols = len(expand[0])
    wide = expand[0][0].shape[1]

    def kernel(unit_ref, ffn_ref, grad_ref, slope_ref, norm_ref, *refs):
        out_ref, dffn_ref, dpre_ref, dsecond_ref, back_ref, sum_ref = refs[4 * cols :]
        hid = unit_ref[...] * norm_ref[0:1] + norm_ref[1:2]
        result, second, inverse = kernel_norm(hid + ffn_ref[...], norm_ref[2:3], norm_ref[3:4])
        out_ref[...] = result
        upstream = grad_ref[...]

        def put(c, value):
            dpre_ref[:, c * wide : (c + 1) * wide] = value

        dffn_ref[...], dsecond_ref[...], back_ref[...] = ffn_backward_values(
            upstream,
            second,
            inverse,
            lambda c: slope_ref[:, c * wide : (c + 1) * wide],
            norm_ref[2:3],
            refs[: 2 * cols],
            refs[2 * cols : 4 * cols],
            cols,
            put,
        )
        put_sums(sum_ref, column_sum(upstream * second), column_sum(upstream), width)

    ins = [unit, ffn, grad, slope, norms] + flat(shrink) + flat(expand)
    outs = [
        shape(tokens, width, kind=jnp.float32),
        shape(tokens, width),
        shape(tokens, cols * wide),
        shape(tokens, width, kind=jnp.float32),
        shape(tokens, width, kind=jnp.float32),
        shape(1, 8, width, kind=jnp.float32),
    ]
    return run(
        kernel,
        (1,),
        ins,
        [whole_spec(x) for x in ins],
        outs,
        [whole_spec(x) for x in outs],
        4 * tokens * width * cols * wide,
    )


def ffn_grads(hid_low, dpre, active, dffn):
    dp_count, col_count = lax.axis_size("dp"), lax.axis_size("col")
    half = hid_low.shape[1] // 2
    theirs_first = dot_rows(hid_low[:, half:], dpre).astype(low_type)
    theirs_second = dot_rows(active, dffn[:, half:]).astype(low_type)
    mine_first = dot_rows(hid_low[:, :half], dpre).astype(low_type)
    mine_second = dot_rows(active, dffn[:, :half]).astype(low_type)
    wide = mine_first.shape[1] // col_count
    tall = mine_second.shape[0] // col_count
    low, high = half // dp_count, tall // dp_count
    got_first, got_second = row_swap(theirs_first), row_swap(theirs_second)

    def kernel(*refs):
        ins, outs = refs[:8], refs[8:]
        for k in range(2):
            first = add_low(ins[2 * k][...], ins[2 * k + 1][...])
            second = add_low(ins[4 + 2 * k][...], ins[5 + 2 * k][...])
            for place in range(dp_count):
                part = first[place * low : (place + 1) * low]
                outs[k][0, place, :low] = part[:, :half]
                outs[k][0, place, low:] = part[:, half:]
                outs[2 + k][0, place] = second[place * high : (place + 1) * high]

    specs = (
        [pl.BlockSpec((half, wide), lambda i: (0, 2 * i))] * 2
        + [pl.BlockSpec((half, wide), lambda i: (0, 2 * i + 1))] * 2
        + [pl.BlockSpec((tall, half), lambda i: (i, 0))] * 2
        + [pl.BlockSpec((tall, half), lambda i: (i + 2, 0))] * 2
    )
    return pack_call(
        kernel,
        [mine_first, got_first] * 2 + [mine_second, got_second] * 2,
        specs,
        dp_count,
        (2 * low, high),
        half,
    )


def add_low(left, right):
    return (left.astype(jnp.float32) + right.astype(jnp.float32)).astype(low_type)


def pack_call(kernel, ins, specs, dp_count, heights, width):
    heights = [heights[0], heights[0], heights[1], heights[1]]
    return run(
        kernel,
        (2,),
        ins,
        specs,
        [shape(2, dp_count, height, width) for height in heights],
        [
            pl.BlockSpec((1, dp_count, height, width), lambda i: (i, 0, 0, 0))
            for height in heights
        ],
        0,
    )


def first_swaps(packed):
    keep_a, send_a, keep_b, send_b = packed
    got_a, got_b = col_swap(send_a, 1), col_swap(send_b, 2)

    def kernel(*refs):
        for half in range(2):
            total = add_low(refs[2 * half][...], refs[2 * half + 1][...])
            refs[4 + 2 * half][...] = total[0]
            refs[5 + 2 * half][...] = total[1]

    ins = [keep_a, got_a, keep_b, got_b]
    outs = [shape(*x.shape[1:]) for x in (keep_a, keep_a, keep_b, keep_b)]

    def spec(array):
        front = array.ndim - 3
        return pl.BlockSpec(
            (2,) * front + (1,) + array.shape[front + 1 :],
            lambda i: (0,) * front + (i, 0, 0),
        )

    return run(
        kernel, (keep_a.shape[1],), ins, [spec(x) for x in ins], outs, [spec(x) for x in outs], 0
    )


def second_swaps(sums):
    own_a, on_a, own_b, on_b = sums
    got_a, got_b = col_swap(on_a, 2), col_swap(on_b, 1)
    count, high_a, width = own_a.shape
    high_b = own_b.shape[1]

    def kernel(place_ref, *refs):
        for step in range(count):
            at = lax.rem(place_ref[0] + step, count)
            refs[4 + step][:high_a] = add_low(refs[0][at], refs[1][at])
            refs[4 + step][high_a:] = add_low(refs[2][at], refs[3][at])

    ins = [own_a, got_a, own_b, got_b]
    whole = pl.BlockSpec(memory_space=pltpu.VMEM)
    return pl.pallas_call(
        kernel,
        out_shape=[jax.ShapeDtypeStruct((high_a + high_b, width), low_type)] * count,
        grid_spec=pltpu.PrefetchScalarGridSpec(
            num_scalar_prefetch=1, grid=(), in_specs=[whole] * 4, out_specs=[whole] * count
        ),
        cost_estimate=pl.CostEstimate(
            flops=0, bytes_accessed=6 * count * (high_a + high_b) * width, transcendentals=0
        ),
        name="add_second",
    )(lax.axis_index("dp").reshape(1), *ins)


def dp_swaps(pieces):
    got = [dp_shift(piece, step) for step, piece in enumerate(pieces) if step]
    total = pieces[0].astype(jnp.float32)
    for piece in got:
        total = total + piece.astype(jnp.float32)
    return total


def row_products(left, right, part):
    cols, tokens, wide = right.shape
    half = left.shape[1] // 2

    def kernel(left_ref, right_ref, out_ref):
        out_ref[0] = dot_rows(left_ref[...], right_ref[0]).astype(low_type)

    return run(
        kernel,
        (cols,),
        [left, right],
        [
            pl.BlockSpec((tokens, half), lambda c: (0, part)),
            pl.BlockSpec((1, tokens, wide), lambda c: (c, 0, 0)),
        ],
        [shape(cols, half, wide)],
        [pl.BlockSpec((1, half, wide), lambda c: (c, 0, 0))],
        2 * tokens * half * cols * wide,
    )[0]


def attention_grads(x_low, dqkv, mixed, datt, ready):
    dp_count, col_count = lax.axis_size("dp"), lax.axis_size("col")
    half = x_low.shape[1] // 2
    wide = dqkv.shape[2]
    theirs_second = dot_rows(mixed, datt[:, half:]).astype(low_type)
    theirs_first = row_products(x_low, dqkv, 1)
    x_low, mixed = after((x_low, mixed), ready)
    mine_first = row_products(x_low, dqkv, 0)
    mine_second = dot_rows(mixed, datt[:, :half]).astype(low_type)
    got_first, got_second = row_swap(theirs_first), row_swap(theirs_second)
    tall = mine_second.shape[0] // col_count
    low, high = half // dp_count, tall // dp_count
    end_rows = low // 2
    assert (wide - half) * 2 == half

    def kernel(*refs):
        ins, outs = refs[:12], refs[12:]
        for k in range(2):
            first = add_low(ins[2 * k][0, :, :half], ins[2 * k + 1][0, :, :half])
            other = ins[4 + 2 * k][0, :, half:].astype(jnp.float32)
            other = other + ins[5 + 2 * k][0, :, half:].astype(jnp.float32)
            second = add_low(ins[8 + 2 * k][...], ins[9 + 2 * k][...])
            for place in range(dp_count):
                outs[k][0, place] = first[place * low : (place + 1) * low]
                ends = other[place * low : (place + 1) * low]
                outs[2 + k][0, place, :end_rows] = jnp.concatenate(
                    [ends[:end_rows], ends[end_rows:]], axis=1
                ).astype(low_type)
                outs[2 + k][0, place, end_rows:] = second[place * high : (place + 1) * high]

    def blocks(index):
        return [pl.BlockSpec((1, half, wide), lambda i: (index(i), 0, 0))] * 2

    specs = (
        blocks(lambda i: 2 * i)
        + blocks(lambda i: 2 * i + 1)
        + blocks(lambda i: i)
        + blocks(lambda i: i + 2)
        + [pl.BlockSpec((tall, half), lambda i: (i, 0))] * 2
        + [pl.BlockSpec((tall, half), lambda i: (i + 2, 0))] * 2
    )
    return pack_call(
        kernel,
        [mine_first, got_first] * 4 + [mine_second, got_second] * 2,
        specs,
        dp_count,
        (low, end_rows + high),
        half,
    )


def unpack_ffn(packed, low):
    return jnp.concatenate([packed[:low], packed[low : 2 * low]], axis=1), packed[2 * low :]


def unpack_attention(packed, low):
    half = packed.shape[1] // 2
    ends = packed[low : low + low // 2]
    ends = jnp.concatenate([ends[:, :half], ends[:, half:]], axis=0)
    return jnp.concatenate([packed[:low], ends], axis=1), packed[low + low // 2 :]


def halves(value, axis):
    return jnp.split(value, 2, axis=axis)


def first_grad(left, right, through):
    mine_left, theirs_left = halves(left, 1)
    theirs = [dot_rows(theirs_left, block).astype(low_type) for block in right]
    mine = [dot_rows(mine_left, block).astype(low_type) for block in right]
    return scatter_grad(mine, theirs, through)


def second_grad(left, right, through):
    mine_right, theirs_right = halves(right, 1)
    count = lax.axis_size("col")
    theirs = dot_rows(left, theirs_right).astype(low_type)
    mine = dot_rows(left, mine_right).astype(low_type)
    got = row_swap(theirs)
    total = mine.astype(jnp.float32) + got.astype(jnp.float32)
    return dp_scatter_sum(plane_sum(jnp.split(total, count, 0), through))


def to_tokens(value, row):
    parts = value.reshape((2, -1) + value.shape[1:])
    mine = lax.dynamic_index_in_dim(parts, row, 0, False)
    theirs = lax.dynamic_index_in_dim(parts, 1 - row, 0, False)
    return jnp.concatenate([mine, row_swap(theirs)], axis=1)


def to_features(value, row):
    mine, theirs = halves(value, 1)
    got = row_swap(theirs)
    first = jnp.where(row == 0, mine, got)
    second = jnp.where(row == 0, got, mine)
    return jnp.concatenate([first, second], axis=0)


def swap_features(value):
    first, second = halves(value, 1)
    return jnp.concatenate([second, first], axis=1)


def swap_rows(value):
    first, second = halves(value, 0)
    return jnp.concatenate([second, first], axis=0)


def layer(
    hidden,
    lengths,
    inner_project,
    inner_merge,
    inner_expand,
    inner_shrink,
    inner_norms,
    outer_places,
    outer_project,
    outer_merge,
    outer_expand,
    outer_shrink,
    outer_norms,
    out_grad,
):
    dp_count, row_count, col_count = (lax.axis_size(name) for name in ("dp", "row", "col"))
    dp, row, col = (lax.axis_index(name) for name in ("dp", "row", "col"))
    everyone = ("dp", "row", "col")
    device_count = dp_count * row_count * col_count
    value = to_tokens(hidden, row)
    grad_in = to_tokens(out_grad, row)
    tokens, width = value.shape
    segs = tokens // SEG

    small = jnp.concatenate([inner_norms, outer_norms, outer_places], axis=1)
    small = lax.all_to_all(
        jnp.broadcast_to(small[None], (device_count,) + small.shape), everyone, 0, 0, tiled=True
    )
    small = small.reshape((dp_count, row_count, -1) + small.shape[2:])
    small = jnp.concatenate(
        [
            lax.dynamic_index_in_dim(small, row, 1, False).reshape(-1, small.shape[-1]),
            lax.dynamic_index_in_dim(small, 1 - row, 1, False).reshape(-1, small.shape[-1]),
        ],
        axis=0,
    )
    vectors = small.T
    inner_gains = vectors[0:4]
    outer_gains = vectors[4:8]
    places = vectors[8:]

    length = lax.dynamic_index_in_dim(lengths, col // 2, 0, False)
    half = col % 2
    seg_own = (half * 2 + row) * segs + jnp.arange(segs, dtype=jnp.int32)
    spot = (seg_own[:, None] * SEG + jnp.arange(SEG, dtype=jnp.int32)[None]).reshape(tokens)
    valid = (spot < length).astype(jnp.float32)
    keep_tok = ((spot < length) | (spot % SEG == 0)).astype(jnp.float32)
    seg_all = jnp.concatenate(
        [
            (h * 2 + r) * segs + jnp.arange(segs, dtype=jnp.int32)
            for h in (half, 1 - half)
            for r in (row, 1 - row)
        ]
    )
    keep_seg = (seg_all * SEG < length).astype(jnp.float32)
    one_hot = (seg_own[:, None] == jnp.arange(NSEG, dtype=jnp.int32)[None]).astype(jnp.float32)

    keep_row = keep_tok[None]
    rows_tile = 2 * SEG
    inner, outer_steps, (x_in, qkv, mixed_in), gates = gather_weights(
        (inner_project, inner_merge, inner_expand, inner_shrink),
        (outer_project, outer_merge, outer_expand, outer_shrink),
        lambda project: project_attend(value, keep_row, project, None, SEG, rows_tile),
    )
    unit_one, inverse_one, hid_in, active_in, slope = merge_expand(
        after(value, gates[0]), mixed_in, inner[1], inner[2], inner_gains, rows_tile
    )
    outer_project = outer_steps[0](hid_in)
    outer_merge, outer_shrink = outer_steps[1](outer_project[0][1])
    inner_out, unit_two, inverse_two = shrink_norm(
        unit_one,
        after(active_in, (gates[1], outer_project[0][1])),
        inner[3],
        inner_gains,
        rows_tile,
    )
    grid = inner_out.reshape(segs, SEG, width)
    masked_grad = (grad_in * valid[:, None]).reshape(segs, SEG, width)
    heads_in = grid[:, 0] + jnp.dot(
        one_hot, places, precision=highest, preferred_element_type=jnp.float32
    )
    rows = jnp.concatenate([heads_in, masked_grad[:, 0]], axis=0)
    rows = jnp.stack([rows, swap_features(row_swap(rows))]).reshape(2, 2, segs, width)
    rows = jnp.stack([rows, col_swap(rows, 1)])
    rows = rows.transpose(2, 0, 1, 3, 4).reshape(2, NSEG, width)

    def join(partial_sum):
        return partial_sum + swap_rows(col_swap(partial_sum, 1))

    flat_grad = masked_grad.reshape(tokens, width)
    outer_expand = outer_steps[2]((outer_shrink[0][1], inner_out))
    main = ffn_backward(
        after(flat_grad, gates[2]),
        unit_two,
        inverse_two,
        slope,
        inner[3],
        inner[2],
        inner_gains,
        rows_tile,
    )
    outer = (outer_project, outer_merge, outer_expand, outer_shrink)
    rows = after(rows, main[3])
    x_low, o_qkv, mixed, attended = project_attend(
        rows[0], keep_seg[None], outer[0], outer[1], NSEG, NSEG
    )
    o_unit, o_inverse, hid_low, active, o_slope, ffn = outer_middle(
        rows[0], join(attended), outer[2], outer[3], outer_gains
    )
    outer_out, dffn, dpre, dsecond, back, o_second = outer_turn(
        o_unit, join(ffn), rows[1], o_slope, outer[3], outer[2], outer_gains
    )
    datt, dqkv, back, o_first, dfirst = attention_backward(
        dsecond + join(back),
        o_unit,
        o_inverse,
        o_qkv,
        keep_seg[None],
        outer[0],
        outer[1],
        outer_gains,
        NSEG,
        NSEG,
        False,
    )
    dheads = dfirst + join(back)
    outer_norm_grad = jnp.concatenate([o_first[0, :2], o_second[0, :2]], axis=0).T
    dheads = dheads[:segs]
    layer_out = (
        jnp.concatenate([outer_out[:segs, None], grid[:, 1:]], axis=1).reshape(tokens, width)
        * valid[:, None]
    )
    places_grad = jnp.dot(dheads.T, one_hot, precision=highest, preferred_element_type=jnp.float32)

    dffn_in, dpre_in, dhid_in, few_sums = ffn_backward_firsts(
        flat_grad,
        dheads,
        unit_two,
        inverse_two,
        slope,
        inner[3],
        inner[2],
        inner_gains,
        main[:3],
    )
    wide_dp = dp_count > 4
    if not wide_dp:
        ffn_packed = ffn_grads(hid_in, dpre_in, active_in, dffn_in)
        dhid_in = after(dhid_in, ffn_packed[0])
    datt_in, dqkv_in, input_grad, first_sums = attention_backward(
        dhid_in,
        unit_one,
        inverse_one,
        qkv,
        keep_row,
        inner[0],
        inner[1],
        inner_gains,
        SEG,
        rows_tile,
        True,
    )
    inner_norm_grad = jnp.concatenate(
        [jnp.sum(first_sums, 0)[:2], jnp.sum(main[3], 0)[:2] + few_sums[0, :2]], axis=0
    ).T
    if wide_dp:
        inner_grads = (
            first_grad(x_in, dqkv_in, 1),
            second_grad(mixed_in, datt_in, 2),
            first_grad(hid_in, jnp.split(dpre_in, col_count, 1), 1),
            second_grad(active_in, dffn_in, 2),
        )
        gate = None
    else:
        ffn_sums = first_swaps(ffn_packed)
        attention_packed = attention_grads(x_in, dqkv_in, mixed_in, datt_in, ffn_sums[0])
        ffn_pieces = second_swaps(ffn_sums)
        gate = attention_packed[0]
    if gate is not None:
        dffn = after(dffn, gate)
    shared = [halves(part, 1)[0] for part in (x_low, hid_low, datt, dffn)]
    own, over = zip(*([halves(part, 1) for part in (active, dpre, mixed)] + [tuple(dqkv)]))
    packed = jnp.concatenate(
        [
            jnp.concatenate(shared + list(own), axis=1),
            col_swap(jnp.concatenate(shared + list(over), axis=1), 2),
        ],
        axis=0,
    )
    if dp_count > 4:
        packed = lax.all_gather(packed, "dp", axis=0, tiled=True)
    else:
        packed = jnp.concatenate(
            [packed] + [dp_shift(packed, step) for step in range(1, dp_count)], axis=0
        )
    if not wide_dp:
        attention_sums = first_swaps(attention_packed)
        ffn_total = dp_swaps(ffn_pieces)
        attention_pieces = second_swaps(attention_sums)
        attention_total = dp_swaps(after(attention_pieces, packed))
        inner_grads = unpack_attention(attention_total, inner_expand.shape[0]) + unpack_ffn(
            ffn_total, inner_expand.shape[0]
        )
    ends = []
    for part in shared + list(own):
        ends.append((ends[-1] if ends else 0) + part.shape[1])
    x_all, hid_all, datt_all, dffn_all, active_all, dpre_all, mixed_all, dqkv_all = jnp.split(
        packed, ends[:-1], axis=1
    )

    def own_rows(product):
        return lax.dynamic_index_in_dim(
            product.reshape((dp_count, -1) + product.shape[1:]), dp, 0, False
        )

    outer_grads = (
        own_rows(dot_rows(x_all, dqkv_all)),
        own_rows(dot_rows(mixed_all, datt_all)),
        own_rows(dot_rows(hid_all, dpre_all)),
        own_rows(dot_rows(active_all, dffn_all)),
    )

    small_grad = jnp.concatenate([inner_norm_grad, 0.25 * outer_norm_grad, places_grad], axis=1)
    columns = small_grad.shape[1]
    blocks = small_grad.reshape(2, dp_count, col_count, -1, columns)
    blocks = jnp.where(row == 0, blocks, blocks[::-1]).transpose(1, 0, 2, 3, 4)
    blocks = lax.all_to_all(
        blocks.reshape(device_count, -1, columns), everyone, 0, 0, tiled=True
    )
    small_sum = jnp.sum(blocks, axis=0)
    return (
        to_features(layer_out, row),
        to_features(input_grad, row),
        inner_grads[0],
        inner_grads[1],
        inner_grads[2],
        inner_grads[3],
        small_sum[:, 0:4],
        small_sum[:, 8:],
        outer_grads[0],
        outer_grads[1],
        outer_grads[2],
        outer_grads[3],
        small_sum[:, 4:8],
    )


def solution(mesh):
    tokens = P(("dp", "col"), "row")
    first = P(("row", "dp"), "col")
    second = P(("col", "dp"), "row")
    small = P(("row", "dp", "col"), None)
    weights = (first, second, first, second)
    return jax.shard_map(
        layer,
        mesh=mesh,
        in_specs=(tokens, P("dp")) + weights + (small, small) + weights + (small, tokens),
        out_specs=(tokens, tokens) + weights + (small, small) + weights + (small,),
        check_vma=False,
    )
```

```python
import jax
import jax.numpy as jnp
from jax import lax
from jax.experimental import pallas as pl
from jax.experimental.pallas import tpu as pltpu
from jax.sharding import PartitionSpec as P


HDIM = 64
SEG = 128
NSEG = 16
epsilon = 1e-06
highest = lax.Precision.HIGHEST
low_type = jnp.bfloat16


def dot(left, right):
    return jnp.dot(left, right, preferred_element_type=jnp.float32)


def dot_t(left, right):
    return lax.dot_general(
        left, right, (((1,), (1,)), ((), ())), preferred_element_type=jnp.float32
    )


def dot_rows(left, right):
    return lax.dot_general(
        left, right, (((0,), (0,)), ((), ())), preferred_element_type=jnp.float32
    )


def row_swap(value):
    return lax.ppermute(value, "row", [(0, 1), (1, 0)])


def col_swap(value, mask):
    return lax.ppermute(value, "col", [(i, i ^ mask) for i in range(lax.axis_size("col"))])


def dp_shift(value, step):
    count = lax.axis_size("dp")
    return lax.ppermute(value, "dp", [(i, (i + step) % count) for i in range(count)])


def after(value, earlier):
    return lax.optimization_barrier((value, earlier))[0]


def dp_pieces(value):
    count = lax.axis_size("dp")
    return [value] + [dp_shift(value, step) for step in range(1, count)]


def place_pieces(pieces, cut=None):
    count = len(pieces)
    height, width = pieces[0].shape
    bounds = (0, height) if cut is None else (0, cut, height)
    spans = list(zip(bounds[:-1], bounds[1:]))

    def kernel(place_ref, *refs):
        for step in range(count):
            at = lax.rem(place_ref[0] - step + count, count)
            for (low, high), out in zip(spans, refs[count:]):
                size = high - low
                out[pl.ds(pl.multiple_of(at * size, 16), size), :] = refs[step][low:high]

    whole = pl.BlockSpec(memory_space=pltpu.VMEM)
    outs = [
        jax.ShapeDtypeStruct((count * (high - low), width), pieces[0].dtype) for low, high in spans
    ]
    placed = pl.pallas_call(
        kernel,
        out_shape=outs,
        grid_spec=pltpu.PrefetchScalarGridSpec(
            num_scalar_prefetch=1,
            grid=(),
            in_specs=[whole] * count,
            out_specs=[whole] * len(outs),
        ),
        cost_estimate=pl.CostEstimate(
            flops=0, bytes_accessed=4 * count * height * width, transcendentals=0
        ),
        name="place_pieces",
    )(lax.axis_index("dp").reshape(1), *pieces)
    return placed[0] if cut is None else placed


def dp_scatter_sum(value):
    count = lax.axis_size("dp")
    if count > 4:
        return lax.psum_scatter(value, "dp", scatter_dimension=0, tiled=True)
    place = lax.axis_index("dp")
    parts = value.reshape((count, -1) + value.shape[1:])
    total = lax.dynamic_index_in_dim(parts, place, 0, False)
    for step in range(1, count):
        piece = lax.dynamic_index_in_dim(parts, (place + step) % count, 0, False)
        total = total + dp_shift(piece.astype(low_type), step).astype(jnp.float32)
    return total


def plane_blocks(own, through):
    side = col_swap(own, 1)
    over = col_swap(own, 2)
    far = col_swap(over, 1) if through == 1 else col_swap(side, 2)
    mine = (own, side, over, far)
    return (mine, tuple(row_swap(block) for block in mine))


def pair_blocks(own):
    mine = (own, col_swap(own, 2))
    return (mine, tuple(row_swap(block) for block in mine))


def gather_wide(inner_shards, outer_shards, first_use):
    inner_own, outer_own = (
        [lax.all_gather(shard, "dp", axis=0, tiled=True) for shard in group]
        for group in (inner_shards, outer_shards)
    )
    inner = [plane_blocks(own, through) for own, through in zip(inner_own, (1, 2, 1, 2))]
    outer = [pair_blocks(own) for own in outer_own]
    steps = (lambda gate: outer[0], lambda gate: (outer[1], outer[3]), lambda gate: outer[2])
    return inner, steps, first_use(inner[0])


def gather_weights(inner_shards, outer_shards, first_use):
    inner_shards = [shard.astype(low_type) for shard in inner_shards]
    outer_shards = [shard.astype(low_type) for shard in outer_shards]
    if lax.axis_size("dp") > 4:
        return gather_wide(inner_shards, outer_shards, first_use)
    pieces = dp_pieces(inner_shards[0])
    merge_pieces = dp_pieces(inner_shards[1])
    own = place_pieces(pieces)
    expand_pieces = dp_pieces(after(inner_shards[2], own))
    side, over = col_swap(own, 1), col_swap(own, 2)
    far_project = col_swap(after(over, merge_pieces), 1)
    project = both_rows((own, side, over, far_project))
    own = place_pieces(after(merge_pieces, side))
    side, over = col_swap(own, 1), col_swap(own, 2)
    far_merge = col_swap(side, 2)
    merge = both_rows((own, side, over, far_merge))
    own = place_pieces(after(expand_pieces, (side, over, far_project)))
    shrink_pieces = dp_pieces(after(inner_shards[3], expand_pieces))
    side, over = col_swap(own, 1), col_swap(own, 2)
    used = first_use(after(project, (own, merge)))
    far_expand = col_swap(after(over, shrink_pieces), 1)
    expand = both_rows((own, side, over, far_expand))
    own = place_pieces(after(shrink_pieces, (side, over, used[0])))
    side, over = col_swap(own, 1), col_swap(own, 2)
    far = col_swap(after(side, far_expand), 2)
    shrink = both_rows((own, side, over, far))
    rows = jnp.concatenate([outer_shards[1], outer_shards[3]], axis=0)
    first = dp_pieces(after(outer_shards[0], shrink_pieces))
    second = dp_pieces(after(rows, first[1]))
    third = dp_pieces(after(outer_shards[2], second[1]))

    def outer_project(gate):
        return pair_blocks(place_pieces(after(first, gate)))

    def outer_rows(gate):
        merge, shrink = place_pieces(after(second, gate), outer_shards[1].shape[0])
        return pair_blocks(merge), pair_blocks(shrink)

    def outer_expand(gate):
        own = place_pieces(after(third, gate))
        return pair_blocks(own)

    return (project, merge, expand, shrink), (outer_project, outer_rows, outer_expand), used


def both_rows(mine):
    return (mine, tuple(row_swap(block) for block in mine))


def plane_sum(sums, through):
    other = 3 - through
    own = sums[0] + col_swap(sums[through].astype(low_type), through).astype(jnp.float32)
    onward = sums[other] + col_swap(sums[3].astype(low_type), through).astype(jnp.float32)
    return own + col_swap(onward.astype(low_type), other).astype(jnp.float32)


def scatter_grad(mine, theirs, through):
    sums = [
        block.astype(jnp.float32) + row_swap(sent).astype(jnp.float32)
        for block, sent in zip(mine, theirs)
    ]
    return dp_scatter_sum(plane_sum(sums, through))


def whole_spec(array):
    return pl.BlockSpec(
        array.shape, lambda i: (0,) * array.ndim, pipeline_mode=pl.Buffered(1)
    )


def flat(blocks):
    return [block for half in blocks for block in half]


def grouped(refs, cols):
    return (refs[:cols], refs[cols : 2 * cols])


def down(refs, cols):
    return lambda c: jnp.concatenate([refs[c][...], refs[cols + c][...]], axis=0)


def across(refs, cols):
    return lambda c: jnp.concatenate([refs[c][...], refs[cols + c][...]], axis=1)


def kernel_norm(value, gain, shift):
    average = jnp.mean(value, axis=1, keepdims=True)
    centred = value - average
    inverse = lax.rsqrt(jnp.mean(centred * centred, axis=1, keepdims=True) + epsilon)
    unit = centred * inverse
    return unit * gain + shift, unit, inverse


def kernel_norm_backward(upstream, unit, inverse, gain):
    scaled = upstream * gain
    centre = jnp.mean(scaled, axis=1, keepdims=True)
    slope = jnp.mean(scaled * unit, axis=1, keepdims=True)
    return inverse * (scaled - centre - unit * slope)


def gelu_and_slope(value):
    share = 0.5 + 0.5 * lax.erf(value * 0.7071067811865476)
    density = 0.3989422804014327 * jnp.exp(-0.5 * value * value)
    return (value * share).astype(low_type), (share + value * density).astype(low_type)


def softmax(pairs, allowed):
    scores = [dot_t(query, key_part) * HDIM ** (-0.5) for query, key_part in pairs]
    scores = [jnp.where(allowed, one, -1000000000.0) for one in scores]
    tops = [jnp.max(one, axis=1, keepdims=True) for one in scores]
    expos = [jnp.exp(one - top) for one, top in zip(scores, tops)]
    shares = [1.0 / jnp.sum(expo, axis=1, keepdims=True) for expo in expos]
    return [expo * share for expo, share in zip(expos, shares)]


def head_parts(qkv, head):
    start = head * 3 * HDIM
    return [qkv[:, start + k * HDIM : start + (k + 1) * HDIM] for k in range(3)]


def run(kernel, grid, ins, in_specs, outs, out_specs, flops, aliases=None):
    moved = sum(x.size * x.dtype.itemsize for x in list(ins) + list(outs))
    return pl.pallas_call(
        kernel,
        out_shape=outs,
        grid=grid,
        in_specs=in_specs,
        out_specs=out_specs,
        input_output_aliases=aliases or {},
        cost_estimate=pl.CostEstimate(flops=flops, bytes_accessed=moved, transcendentals=0),
    )(*ins)


def shape(*dims, kind=low_type):
    return jax.ShapeDtypeStruct(dims, kind)


def tile(rows, width):
    return pl.BlockSpec((rows, width), lambda i: (i, 0))


def stack_tile(cols, rows, width):
    return pl.BlockSpec((cols, rows, width), lambda i: (0, i, 0))


def project_attend(value, keep, project, merge, group, rows):
    tokens, width = value.shape
    cols = len(project[0])
    wide = project[0][0].shape[1]
    heads = wide // (3 * HDIM)
    out_width = cols * heads * HDIM
    merge_in = flat(merge) if merge else []

    def kernel(value_ref, keep_ref, *refs):
        weight = down(refs, cols)
        merge_refs = refs[2 * cols : 2 * cols + len(merge_in)]
        low_ref, qkv_ref, mixed_ref = refs[2 * cols + len(merge_in) :][:3]
        low = value_ref[...].astype(low_type)
        low_ref[...] = low
        qkvs = []
        for c in range(cols):
            qkvs.append(dot(low, weight(c)).astype(low_type))
            qkv_ref[c] = qkvs[c]
        for g in range(rows // group):
            span = slice(g * group, (g + 1) * group)
            allowed = keep_ref[:, span] > 0.5
            outs = []
            for c in range(cols):
                parts = [head_parts(qkvs[c][span], head) for head in range(heads)]
                probs = softmax([part[:2] for part in parts], allowed)
                outs += [
                    dot(some.astype(low_type), part[2]) for some, part in zip(probs, parts)
                ]
            mixed_ref[span] = jnp.concatenate(outs, axis=1).astype(low_type)
        if merge_in:
            mixed = mixed_ref[...]
            for r, half in enumerate(grouped(merge_refs, cols)):
                joined = jnp.concatenate([ref[...] for ref in half], axis=0)
                size = joined.shape[1]
                refs[-1][:, r * size : (r + 1) * size] = dot(mixed, joined)

    ins = [value, keep] + flat(project) + merge_in
    outs = [
        shape(tokens, width),
        shape(cols, tokens, wide),
        shape(tokens, out_width),
    ]
    out_specs = [tile(rows, width), stack_tile(cols, rows, wide), tile(rows, out_width)]
    if merge_in:
        outs.append(shape(tokens, width, kind=jnp.float32))
        out_specs.append(tile(rows, width))
    return run(
        kernel,
        (tokens // rows,),
        ins,
        [tile(rows, width), pl.BlockSpec((1, rows), lambda i: (0, i))]
        + [whole_spec(x) for x in ins[2:]],
        outs,
        out_specs,
        2 * tokens * width * cols * wide + 4 * tokens * group * out_width,
    )


def merge_values(mixed, merge_refs, cols):
    parts = [
        dot(mixed, jnp.concatenate([ref[...] for ref in half], axis=0))
        for half in grouped(merge_refs, cols)
    ]
    return jnp.concatenate(parts, axis=1)


def merge_expand(value, mixed, merge, expand, norms, rows):
    tokens, width = value.shape
    cols = len(expand[0])
    wide = expand[0][0].shape[1]

    def kernel(value_ref, mixed_ref, norm_ref, *refs):
        merge_refs, expand_refs = refs[: 2 * cols], refs[2 * cols : 4 * cols]
        unit_ref, inverse_ref, low_ref, active_ref, slope_ref = refs[4 * cols :]
        attended = merge_values(mixed_ref[...], merge_refs, cols)
        hid, unit, inverse = kernel_norm(
            value_ref[...] + attended, norm_ref[0:1], norm_ref[1:2]
        )
        low = hid.astype(low_type)
        unit_ref[...] = unit
        inverse_ref[...] = inverse
        low_ref[...] = low
        weight = down(expand_refs, cols)
        for c in range(cols):
            span = slice(c * wide, (c + 1) * wide)
            active_ref[:, span], slope_ref[:, span] = gelu_and_slope(dot(low, weight(c)))

    ins = [value, mixed, norms] + flat(merge) + flat(expand)
    return run(
        kernel,
        (tokens // rows,),
        ins,
        [tile(rows, width), tile(rows, width)] + [whole_spec(x) for x in ins[2:]],
        [
            shape(tokens, width, kind=jnp.float32),
            shape(tokens, 1, kind=jnp.float32),
            shape(tokens, width),
            shape(tokens, cols * wide),
            shape(tokens, cols * wide),
        ],
        [tile(rows, width), tile(rows, 1), tile(rows, width)] + [tile(rows, cols * wide)] * 2,
        2 * tokens * width * (width + cols * wide),
    )


def shrink_values(active, shrink_refs, cols):
    parts = [
        dot(active, jnp.concatenate([ref[...] for ref in half], axis=0))
        for half in grouped(shrink_refs, cols)
    ]
    return jnp.concatenate(parts, axis=1)


def shrink_norm(unit, active, shrink, norms, rows):
    tokens, width = unit.shape
    cols = len(shrink[0])

    def kernel(unit_ref, active_ref, norm_ref, *refs):
        out_ref, second_ref, inverse_ref = refs[2 * cols :]
        hid = unit_ref[...] * norm_ref[0:1] + norm_ref[1:2]
        ffn = shrink_values(active_ref[...], refs[: 2 * cols], cols)
        out_ref[...], second_ref[...], inverse_ref[...] = kernel_norm(
            hid + ffn, norm_ref[2:3], norm_ref[3:4]
        )

    ins = [unit, active, norms] + flat(shrink)
    return run(
        kernel,
        (tokens // rows,),
        ins,
        [tile(rows, width), tile(rows, active.shape[1])] + [whole_spec(x) for x in ins[2:]],
        [
            shape(tokens, width, kind=jnp.float32),
            shape(tokens, width, kind=jnp.float32),
            shape(tokens, 1, kind=jnp.float32),
        ],
        [tile(rows, width), tile(rows, width), tile(rows, 1)],
        2 * tokens * width * active.shape[1],
    )


def ffn_backward_values(upstream, unit, inverse, slope, gain, shrink_refs, expand_refs, cols, put):
    dsecond = kernel_norm_backward(upstream, unit, inverse, gain)
    dffn = dsecond.astype(low_type)
    back = None
    for c in range(cols):
        dactive = dot_t(dffn, across(shrink_refs, cols)(c))
        dpre = (dactive * slope(c).astype(jnp.float32)).astype(low_type)
        put(c, dpre)
        part = dot_t(dpre, down(expand_refs, cols)(c))
        back = part if back is None else back + part
    return dffn, dsecond, back


def put_sums(ref, first, second, width):
    ref[0] = jnp.concatenate([first, second, jnp.zeros((6, width), jnp.float32)], axis=0)


def column_sum(value):
    return jnp.sum(value, axis=0, keepdims=True)


def ffn_backward(grad, unit, inverse, slope, shrink, expand, norms, rows):
    tokens, width = grad.shape
    cols = len(shrink[0])
    wide = shrink[0][0].shape[0]

    def kernel(grad_ref, unit_ref, inverse_ref, slope_ref, norm_ref, *refs):
        dffn_ref, dpre_ref, dhid_ref, sum_ref = refs[4 * cols :]
        place = lax.broadcasted_iota(jnp.int32, (rows, 1), 0)
        upstream = jnp.where(place % SEG == 0, 0.0, grad_ref[...])
        unit = unit_ref[...]

        def put(c, value):
            dpre_ref[:, c * wide : (c + 1) * wide] = value

        dffn, dsecond, back = ffn_backward_values(
            upstream,
            unit,
            inverse_ref[...],
            lambda c: slope_ref[:, c * wide : (c + 1) * wide],
            norm_ref[2:3],
            refs[: 2 * cols],
            refs[2 * cols : 4 * cols],
            cols,
            put,
        )
        dffn_ref[...] = dffn
        dhid_ref[...] = dsecond + back
        put_sums(sum_ref, column_sum(upstream * unit), column_sum(upstream), width)

    ins = [grad, unit, inverse, slope, norms] + flat(shrink) + flat(expand)
    return run(
        kernel,
        (tokens // rows,),
        ins,
        [tile(rows, width), tile(rows, width), tile(rows, 1), tile(rows, cols * wide)]
        + [whole_spec(x) for x in ins[4:]],
        [
            shape(tokens, width),
            shape(tokens, cols * wide),
            shape(tokens, width, kind=jnp.float32),
            shape(tokens // rows, 8, width, kind=jnp.float32),
        ],
        [
            tile(rows, width),
            tile(rows, cols * wide),
            tile(rows, width),
            pl.BlockSpec((1, 8, width), lambda i: (i, 0, 0)),
        ],
        4 * tokens * width * cols * wide,
    )


def ffn_backward_firsts(grad, dheads, unit, inverse, slope, shrink, expand, norms, outs):
    tokens, width = grad.shape
    segs = tokens // SEG
    few = 16
    cols = len(shrink[0])
    wide = shrink[0][0].shape[0]
    by_seg = [x.reshape(segs, SEG, -1) for x in (grad, unit, inverse, slope)]
    outs = [x.reshape(segs, SEG, -1) for x in outs]
    upstream = jnp.concatenate([dheads[:, None], by_seg[0][:, 1:few]], axis=1)

    def kernel(up_ref, unit_ref, inverse_ref, slope_ref, norm_ref, *refs):
        dffn_ref, dpre_ref, dhid_ref, sum_ref = refs[4 * cols + 3 :]
        count = segs * few
        upstream = up_ref[...].reshape(count, width)
        unit = unit_ref[...].reshape(count, width)

        def put(c, value):
            dpre_ref[:, :, c * wide : (c + 1) * wide] = value.reshape(segs, few, wide)

        dffn, dsecond, back = ffn_backward_values(
            upstream,
            unit,
            inverse_ref[...].reshape(count, 1),
            lambda c: slope_ref[:, :, c * wide : (c + 1) * wide].reshape(count, wide),
            norm_ref[2:3],
            refs[: 2 * cols],
            refs[2 * cols : 4 * cols],
            cols,
            put,
        )
        dffn_ref[...] = dffn.reshape(segs, few, width)
        dhid_ref[...] = (dsecond + back).reshape(segs, few, width)
        place = lax.broadcasted_iota(jnp.int32, (count, 1), 0)
        only = jnp.where(place % few == 0, upstream, 0.0)
        put_sums(sum_ref, column_sum(only * unit), column_sum(only), width)

    ins = [upstream] + by_seg[1:] + [norms] + flat(shrink) + flat(expand) + outs
    front = [
        pl.BlockSpec((segs, few, x.shape[2]), lambda i: (0, 0, 0)) for x in [upstream] + by_seg[1:]
    ]
    back_specs = [pl.BlockSpec((segs, few, x.shape[2]), lambda i: (0, 0, 0)) for x in outs]
    first_out = len(ins) - 3
    dffn, dpre, dhid, sums = run(
        kernel,
        (1,),
        ins,
        front
        + [whole_spec(x) for x in ins[4:first_out]]
        + [pl.BlockSpec(memory_space=pl.ANY)] * 3,
        [shape(*x.shape, kind=x.dtype) for x in outs] + [shape(1, 8, width, kind=jnp.float32)],
        back_specs + [pl.BlockSpec((1, 8, width), lambda i: (0, 0, 0))],
        4 * segs * few * width * cols * wide,
        {first_out + k: k for k in range(3)},
    )
    return [x.reshape(tokens, -1) for x in (dffn, dpre, dhid)] + [sums]


def attention_backward(dhid, unit, inverse, qkv, keep, project, merge, norms, group, rows, whole):
    tokens, width = dhid.shape
    cols = len(project[0])
    wide = project[0][0].shape[1]
    heads = wide // (3 * HDIM)

    def kernel(dhid_ref, unit_ref, inverse_ref, qkv_ref, keep_ref, norm_ref, *refs):
        project_refs, merge_refs = refs[: 2 * cols], refs[2 * cols : 4 * cols]
        datt_ref, dqkv_ref, dx_ref, sum_ref = refs[4 * cols : 4 * cols + 4]
        upstream = dhid_ref[...]
        unit = unit_ref[...]
        dfirst = kernel_norm_backward(upstream, unit, inverse_ref[...], norm_ref[0:1])
        put_sums(sum_ref, column_sum(upstream * unit), column_sum(upstream), width)
        datt = dfirst.astype(low_type)
        datt_ref[...] = datt
        back = dfirst if whole else None
        if not whole:
            refs[-1][...] = dfirst
        for c in range(cols):
            dmixed = dot_t(datt, across(merge_refs, cols)(c)).astype(low_type)
            blocks = []
            for g in range(rows // group):
                span = slice(g * group, (g + 1) * group)
                allowed = keep_ref[:, span] > 0.5
                parts = [head_parts(qkv_ref[c, span], head) for head in range(heads)]
                incoming = [
                    dmixed[span, head * HDIM : (head + 1) * HDIM] for head in range(heads)
                ]
                dprobs = [dot_t(some, part[2]) for some, part in zip(incoming, parts)]
                probs = softmax([part[:2] for part in parts], allowed)
                centres = [
                    jnp.sum(left * right, axis=1, keepdims=True)
                    for left, right in zip(dprobs, probs)
                ]
                dscores = [
                    (some * (left - centre)).astype(low_type)
                    for some, left, centre in zip(probs, dprobs, centres)
                ]
                pieces = []
                for some, dscore, up, part in zip(probs, dscores, incoming, parts):
                    pieces.append(dot(dscore, part[1]) * HDIM ** (-0.5))
                    pieces.append(dot_rows(dscore, part[0]) * HDIM ** (-0.5))
                    pieces.append(dot_rows(some.astype(low_type), up))
                blocks.append(jnp.concatenate(pieces, axis=1).astype(low_type))
            dqkv = blocks[0] if len(blocks) == 1 else jnp.concatenate(blocks, axis=0)
            dqkv_ref[c] = dqkv
            part = dot_t(dqkv, down(project_refs, cols)(c))
            back = part if back is None else back + part
        dx_ref[...] = back

    ins = [dhid, unit, inverse, qkv, keep, norms] + flat(project) + flat(merge)
    outs = [
        shape(tokens, width),
        shape(cols, tokens, wide),
        shape(tokens, width, kind=jnp.float32),
        shape(tokens // rows, 8, width, kind=jnp.float32),
    ]
    out_specs = [
        tile(rows, width),
        stack_tile(cols, rows, wide),
        tile(rows, width),
        pl.BlockSpec((1, 8, width), lambda i: (i, 0, 0)),
    ]
    if not whole:
        outs.append(shape(tokens, width, kind=jnp.float32))
        out_specs.append(tile(rows, width))
    return run(
        kernel,
        (tokens // rows,),
        ins,
        [
            tile(rows, width),
            tile(rows, width),
            tile(rows, 1),
            stack_tile(cols, rows, wide),
            pl.BlockSpec((1, rows), lambda i: (0, i)),
        ]
        + [whole_spec(x) for x in ins[5:]],
        outs,
        out_specs,
        2 * tokens * width * cols * wide + 10 * tokens * group * cols * heads * HDIM,
    )


def outer_middle(value, attended, expand, shrink, norms):
    tokens, width = value.shape
    cols = len(expand[0])
    wide = expand[0][0].shape[1]

    def kernel(value_ref, attended_ref, norm_ref, *refs):
        unit_ref, inverse_ref, low_ref, active_ref, slope_ref, ffn_ref = refs[4 * cols :]
        hid, unit, inverse = kernel_norm(
            value_ref[...] + attended_ref[...], norm_ref[0:1], norm_ref[1:2]
        )
        low = hid.astype(low_type)
        unit_ref[...] = unit
        inverse_ref[...] = inverse
        low_ref[...] = low
        for c in range(cols):
            span = slice(c * wide, (c + 1) * wide)
            active_ref[:, span], slope_ref[:, span] = gelu_and_slope(
                dot(low, down(refs[: 2 * cols], cols)(c))
            )
        ffn_ref[...] = shrink_values(active_ref[...], refs[2 * cols : 4 * cols], cols)

    ins = [value, attended, norms] + flat(expand) + flat(shrink)
    outs = [
        shape(tokens, width, kind=jnp.float32),
        shape(tokens, 1, kind=jnp.float32),
        shape(tokens, width),
        shape(tokens, cols * wide),
        shape(tokens, cols * wide),
        shape(tokens, width, kind=jnp.float32),
    ]
    return run(
        kernel,
        (1,),
        ins,
        [whole_spec(x) for x in ins],
        outs,
        [whole_spec(x) for x in outs],
        4 * tokens * width * cols * wide,
    )


def outer_turn(unit, ffn, grad, slope, shrink, expand, norms):
    tokens, width = unit.shape
    cols = len(expand[0])
    wide = expand[0][0].shape[1]

    def kernel(unit_ref, ffn_ref, grad_ref, slope_ref, norm_ref, *refs):
        out_ref, dffn_ref, dpre_ref, dsecond_ref, back_ref, sum_ref = refs[4 * cols :]
        hid = unit_ref[...] * norm_ref[0:1] + norm_ref[1:2]
        result, second, inverse = kernel_norm(hid + ffn_ref[...], norm_ref[2:3], norm_ref[3:4])
        out_ref[...] = result
        upstream = grad_ref[...]

        def put(c, value):
            dpre_ref[:, c * wide : (c + 1) * wide] = value

        dffn_ref[...], dsecond_ref[...], back_ref[...] = ffn_backward_values(
            upstream,
            second,
            inverse,
            lambda c: slope_ref[:, c * wide : (c + 1) * wide],
            norm_ref[2:3],
            refs[: 2 * cols],
            refs[2 * cols : 4 * cols],
            cols,
            put,
        )
        put_sums(sum_ref, column_sum(upstream * second), column_sum(upstream), width)

    ins = [unit, ffn, grad, slope, norms] + flat(shrink) + flat(expand)
    outs = [
        shape(tokens, width, kind=jnp.float32),
        shape(tokens, width),
        shape(tokens, cols * wide),
        shape(tokens, width, kind=jnp.float32),
        shape(tokens, width, kind=jnp.float32),
        shape(1, 8, width, kind=jnp.float32),
    ]
    return run(
        kernel,
        (1,),
        ins,
        [whole_spec(x) for x in ins],
        outs,
        [whole_spec(x) for x in outs],
        4 * tokens * width * cols * wide,
    )


def ffn_grads(hid_low, dpre, active, dffn):
    dp_count, col_count = lax.axis_size("dp"), lax.axis_size("col")
    half = hid_low.shape[1] // 2
    theirs_first = dot_rows(hid_low[:, half:], dpre).astype(low_type)
    theirs_second = dot_rows(active, dffn[:, half:]).astype(low_type)
    mine_first = dot_rows(hid_low[:, :half], dpre).astype(low_type)
    mine_second = dot_rows(active, dffn[:, :half]).astype(low_type)
    wide = mine_first.shape[1] // col_count
    tall = mine_second.shape[0] // col_count
    low, high = half // dp_count, tall // dp_count
    got_first, got_second = row_swap(theirs_first), row_swap(theirs_second)

    def kernel(*refs):
        ins, outs = refs[:8], refs[8:]
        for k in range(2):
            first = add_low(ins[2 * k][...], ins[2 * k + 1][...])
            second = add_low(ins[4 + 2 * k][...], ins[5 + 2 * k][...])
            for place in range(dp_count):
                part = first[place * low : (place + 1) * low]
                outs[k][0, place, :low] = part[:, :half]
                outs[k][0, place, low:] = part[:, half:]
                outs[2 + k][0, place] = second[place * high : (place + 1) * high]

    specs = (
        [pl.BlockSpec((half, wide), lambda i: (0, 2 * i))] * 2
        + [pl.BlockSpec((half, wide), lambda i: (0, 2 * i + 1))] * 2
        + [pl.BlockSpec((tall, half), lambda i: (i, 0))] * 2
        + [pl.BlockSpec((tall, half), lambda i: (i + 2, 0))] * 2
    )
    return pack_call(
        kernel,
        [mine_first, got_first] * 2 + [mine_second, got_second] * 2,
        specs,
        dp_count,
        (2 * low, high),
        half,
    )


def add_low(left, right):
    return (left.astype(jnp.float32) + right.astype(jnp.float32)).astype(low_type)


def pack_call(kernel, ins, specs, dp_count, heights, width):
    heights = [heights[0], heights[0], heights[1], heights[1]]
    return run(
        kernel,
        (2,),
        ins,
        specs,
        [shape(2, dp_count, height, width) for height in heights],
        [
            pl.BlockSpec((1, dp_count, height, width), lambda i: (i, 0, 0, 0))
            for height in heights
        ],
        0,
    )


def first_swaps(packed):
    keep_a, send_a, keep_b, send_b = packed
    got_a, got_b = col_swap(send_a, 1), col_swap(send_b, 2)

    def kernel(*refs):
        for half in range(2):
            total = add_low(refs[2 * half][...], refs[2 * half + 1][...])
            refs[4 + 2 * half][...] = total[0]
            refs[5 + 2 * half][...] = total[1]

    ins = [keep_a, got_a, keep_b, got_b]
    outs = [shape(*x.shape[1:]) for x in (keep_a, keep_a, keep_b, keep_b)]

    def spec(array):
        front = array.ndim - 3
        return pl.BlockSpec(
            (2,) * front + (1,) + array.shape[front + 1 :],
            lambda i: (0,) * front + (i, 0, 0),
        )

    return run(
        kernel, (keep_a.shape[1],), ins, [spec(x) for x in ins], outs, [spec(x) for x in outs], 0
    )


def second_swaps(sums):
    own_a, on_a, own_b, on_b = sums
    got_a, got_b = col_swap(on_a, 2), col_swap(on_b, 1)
    count, high_a, width = own_a.shape
    high_b = own_b.shape[1]

    def kernel(place_ref, *refs):
        for step in range(count):
            at = lax.rem(place_ref[0] + step, count)
            refs[4 + step][:high_a] = add_low(refs[0][at], refs[1][at])
            refs[4 + step][high_a:] = add_low(refs[2][at], refs[3][at])

    ins = [own_a, got_a, own_b, got_b]
    whole = pl.BlockSpec(memory_space=pltpu.VMEM)
    return pl.pallas_call(
        kernel,
        out_shape=[jax.ShapeDtypeStruct((high_a + high_b, width), low_type)] * count,
        grid_spec=pltpu.PrefetchScalarGridSpec(
            num_scalar_prefetch=1, grid=(), in_specs=[whole] * 4, out_specs=[whole] * count
        ),
        cost_estimate=pl.CostEstimate(
            flops=0, bytes_accessed=6 * count * (high_a + high_b) * width, transcendentals=0
        ),
        name="add_second",
    )(lax.axis_index("dp").reshape(1), *ins)


def rows_over(value):
    return col_swap(value, 2)


def dp_swaps(pieces):
    got = [dp_shift(piece, step) for step, piece in enumerate(pieces) if step]
    total = pieces[0].astype(jnp.float32)
    for piece in got:
        total = total + piece.astype(jnp.float32)
    return total


def row_products(left, right, part):
    cols, tokens, wide = right.shape
    half = left.shape[1] // 2

    def kernel(left_ref, right_ref, out_ref):
        out_ref[0] = dot_rows(left_ref[...], right_ref[0]).astype(low_type)

    return run(
        kernel,
        (cols,),
        [left, right],
        [
            pl.BlockSpec((tokens, half), lambda c: (0, part)),
            pl.BlockSpec((1, tokens, wide), lambda c: (c, 0, 0)),
        ],
        [shape(cols, half, wide)],
        [pl.BlockSpec((1, half, wide), lambda c: (c, 0, 0))],
        2 * tokens * half * cols * wide,
    )[0]


def attention_grads(x_low, dqkv, mixed, datt, ready):
    dp_count, col_count = lax.axis_size("dp"), lax.axis_size("col")
    half = x_low.shape[1] // 2
    wide = dqkv.shape[2]
    theirs_second = dot_rows(mixed, datt[:, half:]).astype(low_type)
    theirs_first = row_products(x_low, dqkv, 1)
    x_low, mixed = after((x_low, mixed), ready)
    mine_first = row_products(x_low, dqkv, 0)
    mine_second = dot_rows(mixed, datt[:, :half]).astype(low_type)
    got_first, got_second = row_swap(theirs_first), row_swap(theirs_second)
    tall = mine_second.shape[0] // col_count
    low, high = half // dp_count, tall // dp_count
    end_rows = low // 2
    assert (wide - half) * 2 == half

    def kernel(*refs):
        ins, outs = refs[:12], refs[12:]
        for k in range(2):
            first = add_low(ins[2 * k][0, :, :half], ins[2 * k + 1][0, :, :half])
            other = ins[4 + 2 * k][0, :, half:].astype(jnp.float32)
            other = other + ins[5 + 2 * k][0, :, half:].astype(jnp.float32)
            second = add_low(ins[8 + 2 * k][...], ins[9 + 2 * k][...])
            for place in range(dp_count):
                outs[k][0, place] = first[place * low : (place + 1) * low]
                ends = other[place * low : (place + 1) * low]
                outs[2 + k][0, place, :end_rows] = jnp.concatenate(
                    [ends[:end_rows], ends[end_rows:]], axis=1
                ).astype(low_type)
                outs[2 + k][0, place, end_rows:] = second[place * high : (place + 1) * high]

    def blocks(index):
        return [pl.BlockSpec((1, half, wide), lambda i: (index(i), 0, 0))] * 2

    specs = (
        blocks(lambda i: 2 * i)
        + blocks(lambda i: 2 * i + 1)
        + blocks(lambda i: i)
        + blocks(lambda i: i + 2)
        + [pl.BlockSpec((tall, half), lambda i: (i, 0))] * 2
        + [pl.BlockSpec((tall, half), lambda i: (i + 2, 0))] * 2
    )
    return pack_call(
        kernel,
        [mine_first, got_first] * 4 + [mine_second, got_second] * 2,
        specs,
        dp_count,
        (low, end_rows + high),
        half,
    )


def unpack_ffn(packed, low):
    return jnp.concatenate([packed[:low], packed[low : 2 * low]], axis=1), packed[2 * low :]


def unpack_attention(packed, low):
    half = packed.shape[1] // 2
    ends = packed[low : low + low // 2]
    ends = jnp.concatenate([ends[:, :half], ends[:, half:]], axis=0)
    return jnp.concatenate([packed[:low], ends], axis=1), packed[low + low // 2 :]


def halves(value, axis):
    return jnp.split(value, 2, axis=axis)


def first_grad(left, right, through):
    mine_left, theirs_left = halves(left, 1)
    theirs = [dot_rows(theirs_left, block).astype(low_type) for block in right]
    mine = [dot_rows(mine_left, block).astype(low_type) for block in right]
    return scatter_grad(mine, theirs, through)


def second_grad(left, right, through):
    mine_right, theirs_right = halves(right, 1)
    count = lax.axis_size("col")
    theirs = dot_rows(left, theirs_right).astype(low_type)
    mine = dot_rows(left, mine_right).astype(low_type)
    got = row_swap(theirs)
    total = mine.astype(jnp.float32) + got.astype(jnp.float32)
    return dp_scatter_sum(plane_sum(jnp.split(total, count, 0), through))


def to_tokens(value, row):
    parts = value.reshape((2, -1) + value.shape[1:])
    mine = lax.dynamic_index_in_dim(parts, row, 0, False)
    theirs = lax.dynamic_index_in_dim(parts, 1 - row, 0, False)
    return jnp.concatenate([mine, row_swap(theirs)], axis=1)


def to_features(value, row):
    mine, theirs = halves(value, 1)
    got = row_swap(theirs)
    first = jnp.where(row == 0, mine, got)
    second = jnp.where(row == 0, got, mine)
    return jnp.concatenate([first, second], axis=0)


def swap_features(value):
    first, second = halves(value, 1)
    return jnp.concatenate([second, first], axis=1)


def swap_rows(value):
    first, second = halves(value, 0)
    return jnp.concatenate([second, first], axis=0)


def layer(
    hidden,
    lengths,
    inner_project,
    inner_merge,
    inner_expand,
    inner_shrink,
    inner_norms,
    outer_places,
    outer_project,
    outer_merge,
    outer_expand,
    outer_shrink,
    outer_norms,
    out_grad,
):
    dp_count, row_count, col_count = (lax.axis_size(name) for name in ("dp", "row", "col"))
    dp, row, col = (lax.axis_index(name) for name in ("dp", "row", "col"))
    everyone = ("dp", "row", "col")
    device_count = dp_count * row_count * col_count
    value = to_tokens(hidden, row)
    grad_in = to_tokens(out_grad, row)
    tokens, width = value.shape
    segs = tokens // SEG

    small = jnp.concatenate([inner_norms, outer_norms, outer_places], axis=1)
    small = lax.all_to_all(
        jnp.broadcast_to(small[None], (device_count,) + small.shape), everyone, 0, 0, tiled=True
    )
    small = small.reshape((dp_count, row_count, -1) + small.shape[2:])
    small = jnp.concatenate(
        [
            lax.dynamic_index_in_dim(small, row, 1, False).reshape(-1, small.shape[-1]),
            lax.dynamic_index_in_dim(small, 1 - row, 1, False).reshape(-1, small.shape[-1]),
        ],
        axis=0,
    )
    vectors = small.T
    inner_gains = vectors[0:4]
    outer_gains = vectors[4:8]
    places = vectors[8:]

    length = lax.dynamic_index_in_dim(lengths, col // 2, 0, False)
    half = col % 2
    seg_own = (half * 2 + row) * segs + jnp.arange(segs, dtype=jnp.int32)
    spot = (seg_own[:, None] * SEG + jnp.arange(SEG, dtype=jnp.int32)[None]).reshape(tokens)
    valid = (spot < length).astype(jnp.float32)
    keep_tok = ((spot < length) | (spot % SEG == 0)).astype(jnp.float32)
    seg_all = jnp.concatenate(
        [
            (h * 2 + r) * segs + jnp.arange(segs, dtype=jnp.int32)
            for h in (half, 1 - half)
            for r in (row, 1 - row)
        ]
    )
    keep_seg = (seg_all * SEG < length).astype(jnp.float32)
    one_hot = (seg_own[:, None] == jnp.arange(NSEG, dtype=jnp.int32)[None]).astype(jnp.float32)

    keep_row = keep_tok[None]
    rows_tile = 2 * SEG
    inner, outer_steps, (x_in, qkv, mixed_in) = gather_weights(
        (inner_project, inner_merge, inner_expand, inner_shrink),
        (outer_project, outer_merge, outer_expand, outer_shrink),
        lambda project: project_attend(value, keep_row, project, None, SEG, rows_tile),
    )
    unit_one, inverse_one, hid_in, active_in, slope = merge_expand(
        value, mixed_in, inner[1], inner[2], inner_gains, rows_tile
    )
    outer_project = outer_steps[0](hid_in)
    inner_out, unit_two, inverse_two = shrink_norm(
        unit_one, active_in, inner[3], inner_gains, rows_tile
    )
    outer_merge, outer_shrink = outer_steps[1](inner_out)
    grid = inner_out.reshape(segs, SEG, width)
    masked_grad = (grad_in * valid[:, None]).reshape(segs, SEG, width)
    heads_in = grid[:, 0] + jnp.dot(
        one_hot, places, precision=highest, preferred_element_type=jnp.float32
    )
    rows = jnp.concatenate([heads_in, masked_grad[:, 0]], axis=0)
    rows = jnp.stack([rows, swap_features(row_swap(rows))]).reshape(2, 2, segs, width)
    rows = jnp.stack([rows, col_swap(rows, 1)])
    rows = rows.transpose(2, 0, 1, 3, 4).reshape(2, NSEG, width)

    def join(partial_sum):
        return partial_sum + swap_rows(col_swap(partial_sum, 1))

    flat_grad = masked_grad.reshape(tokens, width)
    main = ffn_backward(
        flat_grad, unit_two, inverse_two, slope, inner[3], inner[2], inner_gains, rows_tile
    )
    outer_expand = outer_steps[2](main[3])
    outer = (outer_project, outer_merge, outer_expand, outer_shrink)
    rows = after(rows, main[3])
    x_low, o_qkv, mixed, attended = project_attend(
        rows[0], keep_seg[None], outer[0], outer[1], NSEG, NSEG
    )
    o_unit, o_inverse, hid_low, active, o_slope, ffn = outer_middle(
        rows[0], join(attended), outer[2], outer[3], outer_gains
    )
    outer_out, dffn, dpre, dsecond, back, o_second = outer_turn(
        o_unit, join(ffn), rows[1], o_slope, outer[3], outer[2], outer_gains
    )
    datt, dqkv, back, o_first, dfirst = attention_backward(
        dsecond + join(back),
        o_unit,
        o_inverse,
        o_qkv,
        keep_seg[None],
        outer[0],
        outer[1],
        outer_gains,
        NSEG,
        NSEG,
        False,
    )
    dheads = dfirst + join(back)
    outer_norm_grad = jnp.concatenate([o_first[0, :2], o_second[0, :2]], axis=0).T
    dheads = dheads[:segs]
    layer_out = (
        jnp.concatenate([outer_out[:segs, None], grid[:, 1:]], axis=1).reshape(tokens, width)
        * valid[:, None]
    )
    places_grad = jnp.dot(dheads.T, one_hot, precision=highest, preferred_element_type=jnp.float32)

    dffn_in, dpre_in, dhid_in, few_sums = ffn_backward_firsts(
        flat_grad,
        dheads,
        unit_two,
        inverse_two,
        slope,
        inner[3],
        inner[2],
        inner_gains,
        main[:3],
    )
    wide_dp = dp_count > 4
    if not wide_dp:
        ffn_packed = ffn_grads(hid_in, dpre_in, active_in, dffn_in)
        dhid_in = after(dhid_in, ffn_packed[0])
    datt_in, dqkv_in, input_grad, first_sums = attention_backward(
        dhid_in,
        unit_one,
        inverse_one,
        qkv,
        keep_row,
        inner[0],
        inner[1],
        inner_gains,
        SEG,
        rows_tile,
        True,
    )
    inner_norm_grad = jnp.concatenate(
        [jnp.sum(first_sums, 0)[:2], jnp.sum(main[3], 0)[:2] + few_sums[0, :2]], axis=0
    ).T
    if wide_dp:
        inner_grads = (
            first_grad(x_in, dqkv_in, 1),
            second_grad(mixed_in, datt_in, 2),
            first_grad(hid_in, jnp.split(dpre_in, col_count, 1), 1),
            second_grad(active_in, dffn_in, 2),
        )
        gate = None
    else:
        ffn_sums = first_swaps(ffn_packed)
        attention_packed = attention_grads(x_in, dqkv_in, mixed_in, datt_in, ffn_sums[0])
        ffn_pieces = second_swaps(ffn_sums)
        gate = attention_packed[0]
    shared = [halves(part, 1)[0] for part in (x_low, hid_low, datt, dffn)]
    own, over = zip(*([halves(part, 1) for part in (active, dpre, mixed)] + [tuple(dqkv)]))
    packed = jnp.concatenate(
        [
            jnp.concatenate(shared + list(own), axis=1),
            rows_over(jnp.concatenate(shared + list(over), axis=1)),
        ],
        axis=0,
    )
    if dp_count > 4:
        packed = lax.all_gather(packed, "dp", axis=0, tiled=True)
    else:
        got = [dp_shift(packed, step) for step in range(1, dp_count)]
        packed = jnp.concatenate([packed] + got, axis=0)
    small_grad = jnp.concatenate([inner_norm_grad, 0.25 * outer_norm_grad, places_grad], axis=1)
    if gate is not None:
        small_grad = after(small_grad, gate)
    columns = small_grad.shape[1]
    blocks = small_grad.reshape(2, dp_count, col_count, -1, columns)
    blocks = jnp.where(row == 0, blocks, blocks[::-1]).transpose(1, 0, 2, 3, 4)
    blocks = lax.all_to_all(
        blocks.reshape(device_count, -1, columns), everyone, 0, 0, tiled=True
    )
    small_sum = jnp.sum(blocks, axis=0)
    if not wide_dp:
        attention_sums = first_swaps(attention_packed)
        ffn_total = dp_swaps(ffn_pieces)
        attention_pieces = second_swaps(after(attention_sums, small_sum))
        attention_total = dp_swaps(attention_pieces)
        inner_grads = unpack_attention(attention_total, inner_expand.shape[0]) + unpack_ffn(
            ffn_total, inner_expand.shape[0]
        )
    ends = []
    for part in shared + list(own):
        ends.append((ends[-1] if ends else 0) + part.shape[1])
    x_all, hid_all, datt_all, dffn_all, active_all, dpre_all, mixed_all, dqkv_all = jnp.split(
        packed, ends[:-1], axis=1
    )

    def own_rows(product):
        return lax.dynamic_index_in_dim(
            product.reshape((dp_count, -1) + product.shape[1:]), dp, 0, False
        )

    outer_grads = (
        own_rows(dot_rows(x_all, dqkv_all)),
        own_rows(dot_rows(mixed_all, datt_all)),
        own_rows(dot_rows(hid_all, dpre_all)),
        own_rows(dot_rows(active_all, dffn_all)),
    )

    return (
        to_features(layer_out, row),
        to_features(input_grad, row),
        inner_grads[0],
        inner_grads[1],
        inner_grads[2],
        inner_grads[3],
        small_sum[:, 0:4],
        small_sum[:, 8:],
        outer_grads[0],
        outer_grads[1],
        outer_grads[2],
        outer_grads[3],
        small_sum[:, 4:8],
    )


def solution(mesh):
    tokens = P(("dp", "col"), "row")
    first = P(("row", "dp"), "col")
    second = P(("col", "dp"), "row")
    small = P(("row", "dp", "col"), None)
    weights = (first, second, first, second)
    return jax.shard_map(
        layer,
        mesh=mesh,
        in_specs=(tokens, P("dp")) + weights + (small, small) + weights + (small, tokens),
        out_specs=(tokens, tokens) + weights + (small, small) + weights + (small,),
        check_vma=False,
    )
```

```python
import jax
import jax.numpy as jnp
from jax import lax
from jax.experimental import pallas as pl
from jax.experimental.pallas import tpu as pltpu
from jax.sharding import PartitionSpec as P


HDIM = 64
SEG = 128
NSEG = 16
epsilon = 1e-06
highest = lax.Precision.HIGHEST
low_type = jnp.bfloat16


def dot(left, right):
    return jnp.dot(left, right, preferred_element_type=jnp.float32)


def dot_t(left, right):
    return lax.dot_general(
        left, right, (((1,), (1,)), ((), ())), preferred_element_type=jnp.float32
    )


def dot_rows(left, right):
    return lax.dot_general(
        left, right, (((0,), (0,)), ((), ())), preferred_element_type=jnp.float32
    )


def row_swap(value):
    return lax.ppermute(value, "row", [(0, 1), (1, 0)])


def col_swap(value, mask):
    return lax.ppermute(value, "col", [(i, i ^ mask) for i in range(lax.axis_size("col"))])


def dp_shift(value, step):
    count = lax.axis_size("dp")
    return lax.ppermute(value, "dp", [(i, (i + step) % count) for i in range(count)])


def after(value, earlier):
    return lax.optimization_barrier((value, earlier))[0]


def dp_pieces(value):
    count = lax.axis_size("dp")
    return [value] + [dp_shift(value, step) for step in range(1, count)]


def place_pieces(pieces, cut=None):
    count = len(pieces)
    height, width = pieces[0].shape
    bounds = (0, height) if cut is None else (0, cut, height)
    spans = list(zip(bounds[:-1], bounds[1:]))

    def kernel(place_ref, *refs):
        for step in range(count):
            at = lax.rem(place_ref[0] - step + count, count)
            for (low, high), out in zip(spans, refs[count:]):
                size = high - low
                out[pl.ds(pl.multiple_of(at * size, 16), size), :] = refs[step][low:high]

    whole = pl.BlockSpec(memory_space=pltpu.VMEM)
    outs = [
        jax.ShapeDtypeStruct((count * (high - low), width), pieces[0].dtype) for low, high in spans
    ]
    placed = pl.pallas_call(
        kernel,
        out_shape=outs,
        grid_spec=pltpu.PrefetchScalarGridSpec(
            num_scalar_prefetch=1,
            grid=(),
            in_specs=[whole] * count,
            out_specs=[whole] * len(outs),
        ),
        cost_estimate=pl.CostEstimate(
            flops=0, bytes_accessed=4 * count * height * width, transcendentals=0
        ),
        name="place_pieces",
    )(lax.axis_index("dp").reshape(1), *pieces)
    return placed[0] if cut is None else placed


def dp_scatter_sum(value):
    count = lax.axis_size("dp")
    if count > 4:
        return lax.psum_scatter(value, "dp", scatter_dimension=0, tiled=True)
    place = lax.axis_index("dp")
    parts = value.reshape((count, -1) + value.shape[1:])
    total = lax.dynamic_index_in_dim(parts, place, 0, False)
    for step in range(1, count):
        piece = lax.dynamic_index_in_dim(parts, (place + step) % count, 0, False)
        total = total + dp_shift(piece.astype(low_type), step).astype(jnp.float32)
    return total


def plane_blocks(own, through):
    side = col_swap(own, 1)
    over = col_swap(own, 2)
    far = col_swap(over, 1) if through == 1 else col_swap(side, 2)
    mine = (own, side, over, far)
    return (mine, tuple(row_swap(block) for block in mine))


def pair_blocks(own):
    mine = (own, col_swap(own, 2))
    return (mine, tuple(row_swap(block) for block in mine))


def gather_wide(inner_shards, outer_shards, first_use):
    inner_own, outer_own = (
        [lax.all_gather(shard, "dp", axis=0, tiled=True) for shard in group]
        for group in (inner_shards, outer_shards)
    )
    inner = [plane_blocks(own, through) for own, through in zip(inner_own, (1, 2, 1, 2))]
    outer = [pair_blocks(own) for own in outer_own]
    steps = (lambda gate: outer[0], lambda gate: (outer[1], outer[3]), lambda gate: outer[2])
    return inner, steps, first_use(inner[0])


def gather_weights(inner_shards, outer_shards, first_use, early):
    inner_shards = [shard.astype(low_type) for shard in inner_shards]
    outer_shards = [shard.astype(low_type) for shard in outer_shards]
    if lax.axis_size("dp") > 4:
        return gather_wide(inner_shards, outer_shards, first_use)
    pieces = dp_pieces(inner_shards[0])
    merge_pieces = dp_pieces(inner_shards[1])
    own = place_pieces(pieces)
    expand_pieces = dp_pieces(after(inner_shards[2], own))
    side, over = col_swap(own, 1), col_swap(own, 2)
    far_project = col_swap(after(over, merge_pieces), 1)
    project = both_rows((own, side, over, far_project))
    own = place_pieces(after(merge_pieces, side))
    side, over = col_swap(own, 1), col_swap(own, 2)
    far_merge = col_swap(side, 2)
    merge = both_rows((own, side, over, far_merge))
    own = place_pieces(after(expand_pieces, (far_merge, over, far_project, early)))
    shrink_pieces = dp_pieces(after(inner_shards[3], expand_pieces))
    side, over = col_swap(own, 1), col_swap(own, 2)
    used = first_use(after(project, (own, merge)))
    far_expand = col_swap(after(over, shrink_pieces), 1)
    expand = both_rows((own, side, over, far_expand))
    own = place_pieces(after(shrink_pieces, (side, over, used[0])))
    side, over = col_swap(own, 1), col_swap(own, 2)
    far = col_swap(after(side, far_expand), 2)
    shrink = both_rows((own, side, over, far))
    rows = jnp.concatenate([outer_shards[1], outer_shards[3]], axis=0)
    first = dp_pieces(after(outer_shards[0], shrink_pieces))
    second = dp_pieces(after(rows, first[1]))
    third = dp_pieces(after(outer_shards[2], second[1]))

    def outer_project(gate):
        return pair_blocks(place_pieces(after(first, gate)))

    def outer_rows(gate):
        merge, shrink = place_pieces(after(second, gate), outer_shards[1].shape[0])
        return pair_blocks(merge), pair_blocks(shrink)

    def outer_expand(gate):
        own = place_pieces(after(third, gate))
        return pair_blocks(own)

    return (project, merge, expand, shrink), (outer_project, outer_rows, outer_expand), used


def both_rows(mine):
    return (mine, tuple(row_swap(block) for block in mine))


def plane_sum(sums, through):
    other = 3 - through
    own = sums[0] + col_swap(sums[through].astype(low_type), through).astype(jnp.float32)
    onward = sums[other] + col_swap(sums[3].astype(low_type), through).astype(jnp.float32)
    return own + col_swap(onward.astype(low_type), other).astype(jnp.float32)


def scatter_grad(mine, theirs, through):
    sums = [
        block.astype(jnp.float32) + row_swap(sent).astype(jnp.float32)
        for block, sent in zip(mine, theirs)
    ]
    return dp_scatter_sum(plane_sum(sums, through))


def whole_spec(array):
    return pl.BlockSpec(
        array.shape, lambda i: (0,) * array.ndim, pipeline_mode=pl.Buffered(1)
    )


def flat(blocks):
    return [block for half in blocks for block in half]


def grouped(refs, cols):
    return (refs[:cols], refs[cols : 2 * cols])


def down(refs, cols):
    return lambda c: jnp.concatenate([refs[c][...], refs[cols + c][...]], axis=0)


def across(refs, cols):
    return lambda c: jnp.concatenate([refs[c][...], refs[cols + c][...]], axis=1)


def kernel_norm(value, gain, shift):
    average = jnp.mean(value, axis=1, keepdims=True)
    centred = value - average
    inverse = lax.rsqrt(jnp.mean(centred * centred, axis=1, keepdims=True) + epsilon)
    unit = centred * inverse
    return unit * gain + shift, unit, inverse


def kernel_norm_backward(upstream, unit, inverse, gain):
    scaled = upstream * gain
    centre = jnp.mean(scaled, axis=1, keepdims=True)
    slope = jnp.mean(scaled * unit, axis=1, keepdims=True)
    return inverse * (scaled - centre - unit * slope)


def gelu_and_slope(value):
    share = 0.5 + 0.5 * lax.erf(value * 0.7071067811865476)
    density = 0.3989422804014327 * jnp.exp(-0.5 * value * value)
    return (value * share).astype(low_type), (share + value * density).astype(low_type)


def softmax(pairs, allowed):
    scores = [dot_t(query, key_part) * HDIM ** (-0.5) for query, key_part in pairs]
    scores = [jnp.where(allowed, one, -1000000000.0) for one in scores]
    tops = [jnp.max(one, axis=1, keepdims=True) for one in scores]
    expos = [jnp.exp(one - top) for one, top in zip(scores, tops)]
    shares = [1.0 / jnp.sum(expo, axis=1, keepdims=True) for expo in expos]
    return [expo * share for expo, share in zip(expos, shares)]


def head_parts(qkv, head):
    start = head * 3 * HDIM
    return [qkv[:, start + k * HDIM : start + (k + 1) * HDIM] for k in range(3)]


def run(kernel, grid, ins, in_specs, outs, out_specs, flops, aliases=None):
    moved = sum(x.size * x.dtype.itemsize for x in list(ins) + list(outs))
    return pl.pallas_call(
        kernel,
        out_shape=outs,
        grid=grid,
        in_specs=in_specs,
        out_specs=out_specs,
        input_output_aliases=aliases or {},
        cost_estimate=pl.CostEstimate(flops=flops, bytes_accessed=moved, transcendentals=0),
    )(*ins)


def shape(*dims, kind=low_type):
    return jax.ShapeDtypeStruct(dims, kind)


def tile(rows, width):
    return pl.BlockSpec((rows, width), lambda i: (i, 0))


def stack_tile(cols, rows, width):
    return pl.BlockSpec((cols, rows, width), lambda i: (0, i, 0))


def project_attend(value, keep, project, merge, group, rows):
    tokens, width = value.shape
    cols = len(project[0])
    wide = project[0][0].shape[1]
    heads = wide // (3 * HDIM)
    out_width = cols * heads * HDIM
    merge_in = flat(merge) if merge else []

    def kernel(value_ref, keep_ref, *refs):
        weight = down(refs, cols)
        merge_refs = refs[2 * cols : 2 * cols + len(merge_in)]
        low_ref, qkv_ref, mixed_ref = refs[2 * cols + len(merge_in) :][:3]
        low = value_ref[...].astype(low_type)
        low_ref[...] = low
        qkvs = []
        for c in range(cols):
            qkvs.append(dot(low, weight(c)).astype(low_type))
            qkv_ref[c] = qkvs[c]
        for g in range(rows // group):
            span = slice(g * group, (g + 1) * group)
            allowed = keep_ref[:, span] > 0.5
            outs = []
            for c in range(cols):
                parts = [head_parts(qkvs[c][span], head) for head in range(heads)]
                probs = softmax([part[:2] for part in parts], allowed)
                outs += [
                    dot(some.astype(low_type), part[2]) for some, part in zip(probs, parts)
                ]
            mixed_ref[span] = jnp.concatenate(outs, axis=1).astype(low_type)
        if merge_in:
            mixed = mixed_ref[...]
            for r, half in enumerate(grouped(merge_refs, cols)):
                joined = jnp.concatenate([ref[...] for ref in half], axis=0)
                size = joined.shape[1]
                refs[-1][:, r * size : (r + 1) * size] = dot(mixed, joined)

    ins = [value, keep] + flat(project) + merge_in
    outs = [
        shape(tokens, width),
        shape(cols, tokens, wide),
        shape(tokens, out_width),
    ]
    out_specs = [tile(rows, width), stack_tile(cols, rows, wide), tile(rows, out_width)]
    if merge_in:
        outs.append(shape(tokens, width, kind=jnp.float32))
        out_specs.append(tile(rows, width))
    return run(
        kernel,
        (tokens // rows,),
        ins,
        [tile(rows, width), pl.BlockSpec((1, rows), lambda i: (0, i))]
        + [whole_spec(x) for x in ins[2:]],
        outs,
        out_specs,
        2 * tokens * width * cols * wide + 4 * tokens * group * out_width,
    )


def merge_values(mixed, merge_refs, cols):
    parts = [
        dot(mixed, jnp.concatenate([ref[...] for ref in half], axis=0))
        for half in grouped(merge_refs, cols)
    ]
    return jnp.concatenate(parts, axis=1)


def merge_expand(value, mixed, merge, expand, norms, rows):
    tokens, width = value.shape
    cols = len(expand[0])
    wide = expand[0][0].shape[1]

    def kernel(value_ref, mixed_ref, norm_ref, *refs):
        merge_refs, expand_refs = refs[: 2 * cols], refs[2 * cols : 4 * cols]
        unit_ref, inverse_ref, low_ref, active_ref, slope_ref = refs[4 * cols :]
        attended = merge_values(mixed_ref[...], merge_refs, cols)
        hid, unit, inverse = kernel_norm(
            value_ref[...] + attended, norm_ref[0:1], norm_ref[1:2]
        )
        low = hid.astype(low_type)
        unit_ref[...] = unit
        inverse_ref[...] = inverse
        low_ref[...] = low
        weight = down(expand_refs, cols)
        for c in range(cols):
            span = slice(c * wide, (c + 1) * wide)
            active_ref[:, span], slope_ref[:, span] = gelu_and_slope(dot(low, weight(c)))

    ins = [value, mixed, norms] + flat(merge) + flat(expand)
    return run(
        kernel,
        (tokens // rows,),
        ins,
        [tile(rows, width), tile(rows, width)] + [whole_spec(x) for x in ins[2:]],
        [
            shape(tokens, width, kind=jnp.float32),
            shape(tokens, 1, kind=jnp.float32),
            shape(tokens, width),
            shape(tokens, cols * wide),
            shape(tokens, cols * wide),
        ],
        [tile(rows, width), tile(rows, 1), tile(rows, width)] + [tile(rows, cols * wide)] * 2,
        2 * tokens * width * (width + cols * wide),
    )


def shrink_values(active, shrink_refs, cols):
    parts = [
        dot(active, jnp.concatenate([ref[...] for ref in half], axis=0))
        for half in grouped(shrink_refs, cols)
    ]
    return jnp.concatenate(parts, axis=1)


def shrink_norm(unit, active, shrink, norms, rows):
    tokens, width = unit.shape
    cols = len(shrink[0])

    def kernel(unit_ref, active_ref, norm_ref, *refs):
        out_ref, second_ref, inverse_ref = refs[2 * cols :]
        hid = unit_ref[...] * norm_ref[0:1] + norm_ref[1:2]
        ffn = shrink_values(active_ref[...], refs[: 2 * cols], cols)
        out_ref[...], second_ref[...], inverse_ref[...] = kernel_norm(
            hid + ffn, norm_ref[2:3], norm_ref[3:4]
        )

    ins = [unit, active, norms] + flat(shrink)
    return run(
        kernel,
        (tokens // rows,),
        ins,
        [tile(rows, width), tile(rows, active.shape[1])] + [whole_spec(x) for x in ins[2:]],
        [
            shape(tokens, width, kind=jnp.float32),
            shape(tokens, width, kind=jnp.float32),
            shape(tokens, 1, kind=jnp.float32),
        ],
        [tile(rows, width), tile(rows, width), tile(rows, 1)],
        2 * tokens * width * active.shape[1],
    )


def ffn_backward_values(upstream, unit, inverse, slope, gain, shrink_refs, expand_refs, cols, put):
    dsecond = kernel_norm_backward(upstream, unit, inverse, gain)
    dffn = dsecond.astype(low_type)
    back = None
    for c in range(cols):
        dactive = dot_t(dffn, across(shrink_refs, cols)(c))
        dpre = (dactive * slope(c).astype(jnp.float32)).astype(low_type)
        put(c, dpre)
        part = dot_t(dpre, down(expand_refs, cols)(c))
        back = part if back is None else back + part
    return dffn, dsecond, back


def put_sums(ref, first, second, width):
    ref[0] = jnp.concatenate([first, second, jnp.zeros((6, width), jnp.float32)], axis=0)


def column_sum(value):
    return jnp.sum(value, axis=0, keepdims=True)


def ffn_backward(grad, unit, inverse, slope, shrink, expand, norms, rows):
    tokens, width = grad.shape
    cols = len(shrink[0])
    wide = shrink[0][0].shape[0]

    def kernel(grad_ref, unit_ref, inverse_ref, slope_ref, norm_ref, *refs):
        dffn_ref, dpre_ref, dhid_ref, sum_ref = refs[4 * cols :]
        place = lax.broadcasted_iota(jnp.int32, (rows, 1), 0)
        upstream = jnp.where(place % SEG == 0, 0.0, grad_ref[...])
        unit = unit_ref[...]

        def put(c, value):
            dpre_ref[:, c * wide : (c + 1) * wide] = value

        dffn, dsecond, back = ffn_backward_values(
            upstream,
            unit,
            inverse_ref[...],
            lambda c: slope_ref[:, c * wide : (c + 1) * wide],
            norm_ref[2:3],
            refs[: 2 * cols],
            refs[2 * cols : 4 * cols],
            cols,
            put,
        )
        dffn_ref[...] = dffn
        dhid_ref[...] = dsecond + back
        put_sums(sum_ref, column_sum(upstream * unit), column_sum(upstream), width)

    ins = [grad, unit, inverse, slope, norms] + flat(shrink) + flat(expand)
    return run(
        kernel,
        (tokens // rows,),
        ins,
        [tile(rows, width), tile(rows, width), tile(rows, 1), tile(rows, cols * wide)]
        + [whole_spec(x) for x in ins[4:]],
        [
            shape(tokens, width),
            shape(tokens, cols * wide),
            shape(tokens, width, kind=jnp.float32),
            shape(tokens // rows, 8, width, kind=jnp.float32),
        ],
        [
            tile(rows, width),
            tile(rows, cols * wide),
            tile(rows, width),
            pl.BlockSpec((1, 8, width), lambda i: (i, 0, 0)),
        ],
        4 * tokens * width * cols * wide,
    )


def ffn_backward_firsts(grad, dheads, unit, inverse, slope, shrink, expand, norms, outs):
    tokens, width = grad.shape
    segs = tokens // SEG
    few = 16
    cols = len(shrink[0])
    wide = shrink[0][0].shape[0]
    by_seg = [x.reshape(segs, SEG, -1) for x in (grad, unit, inverse, slope)]
    outs = [x.reshape(segs, SEG, -1) for x in outs]
    upstream = jnp.concatenate([dheads[:, None], by_seg[0][:, 1:few]], axis=1)

    def kernel(up_ref, unit_ref, inverse_ref, slope_ref, norm_ref, *refs):
        dffn_ref, dpre_ref, dhid_ref, sum_ref = refs[4 * cols + 3 :]
        count = segs * few
        upstream = up_ref[...].reshape(count, width)
        unit = unit_ref[...].reshape(count, width)

        def put(c, value):
            dpre_ref[:, :, c * wide : (c + 1) * wide] = value.reshape(segs, few, wide)

        dffn, dsecond, back = ffn_backward_values(
            upstream,
            unit,
            inverse_ref[...].reshape(count, 1),
            lambda c: slope_ref[:, :, c * wide : (c + 1) * wide].reshape(count, wide),
            norm_ref[2:3],
            refs[: 2 * cols],
            refs[2 * cols : 4 * cols],
            cols,
            put,
        )
        dffn_ref[...] = dffn.reshape(segs, few, width)
        dhid_ref[...] = (dsecond + back).reshape(segs, few, width)
        place = lax.broadcasted_iota(jnp.int32, (count, 1), 0)
        only = jnp.where(place % few == 0, upstream, 0.0)
        put_sums(sum_ref, column_sum(only * unit), column_sum(only), width)

    ins = [upstream] + by_seg[1:] + [norms] + flat(shrink) + flat(expand) + outs
    front = [
        pl.BlockSpec((segs, few, x.shape[2]), lambda i: (0, 0, 0)) for x in [upstream] + by_seg[1:]
    ]
    back_specs = [pl.BlockSpec((segs, few, x.shape[2]), lambda i: (0, 0, 0)) for x in outs]
    first_out = len(ins) - 3
    dffn, dpre, dhid, sums = run(
        kernel,
        (1,),
        ins,
        front
        + [whole_spec(x) for x in ins[4:first_out]]
        + [pl.BlockSpec(memory_space=pl.ANY)] * 3,
        [shape(*x.shape, kind=x.dtype) for x in outs] + [shape(1, 8, width, kind=jnp.float32)],
        back_specs + [pl.BlockSpec((1, 8, width), lambda i: (0, 0, 0))],
        4 * segs * few * width * cols * wide,
        {first_out + k: k for k in range(3)},
    )
    return [x.reshape(tokens, -1) for x in (dffn, dpre, dhid)] + [sums]


def attention_backward(dhid, unit, inverse, qkv, keep, project, merge, norms, group, rows, whole):
    tokens, width = dhid.shape
    cols = len(project[0])
    wide = project[0][0].shape[1]
    heads = wide // (3 * HDIM)

    def kernel(dhid_ref, unit_ref, inverse_ref, qkv_ref, keep_ref, norm_ref, *refs):
        project_refs, merge_refs = refs[: 2 * cols], refs[2 * cols : 4 * cols]
        datt_ref, dqkv_ref, dx_ref, sum_ref = refs[4 * cols : 4 * cols + 4]
        upstream = dhid_ref[...]
        unit = unit_ref[...]
        dfirst = kernel_norm_backward(upstream, unit, inverse_ref[...], norm_ref[0:1])
        put_sums(sum_ref, column_sum(upstream * unit), column_sum(upstream), width)
        datt = dfirst.astype(low_type)
        datt_ref[...] = datt
        back = dfirst if whole else None
        if not whole:
            refs[-1][...] = dfirst
        for c in range(cols):
            dmixed = dot_t(datt, across(merge_refs, cols)(c)).astype(low_type)
            blocks = []
            for g in range(rows // group):
                span = slice(g * group, (g + 1) * group)
                allowed = keep_ref[:, span] > 0.5
                parts = [head_parts(qkv_ref[c, span], head) for head in range(heads)]
                incoming = [
                    dmixed[span, head * HDIM : (head + 1) * HDIM] for head in range(heads)
                ]
                dprobs = [dot_t(some, part[2]) for some, part in zip(incoming, parts)]
                probs = softmax([part[:2] for part in parts], allowed)
                centres = [
                    jnp.sum(left * right, axis=1, keepdims=True)
                    for left, right in zip(dprobs, probs)
                ]
                dscores = [
                    (some * (left - centre)).astype(low_type)
                    for some, left, centre in zip(probs, dprobs, centres)
                ]
                pieces = []
                for some, dscore, up, part in zip(probs, dscores, incoming, parts):
                    pieces.append(dot(dscore, part[1]) * HDIM ** (-0.5))
                    pieces.append(dot_rows(dscore, part[0]) * HDIM ** (-0.5))
                    pieces.append(dot_rows(some.astype(low_type), up))
                blocks.append(jnp.concatenate(pieces, axis=1).astype(low_type))
            dqkv = blocks[0] if len(blocks) == 1 else jnp.concatenate(blocks, axis=0)
            dqkv_ref[c] = dqkv
            part = dot_t(dqkv, down(project_refs, cols)(c))
            back = part if back is None else back + part
        dx_ref[...] = back

    ins = [dhid, unit, inverse, qkv, keep, norms] + flat(project) + flat(merge)
    outs = [
        shape(tokens, width),
        shape(cols, tokens, wide),
        shape(tokens, width, kind=jnp.float32),
        shape(tokens // rows, 8, width, kind=jnp.float32),
    ]
    out_specs = [
        tile(rows, width),
        stack_tile(cols, rows, wide),
        tile(rows, width),
        pl.BlockSpec((1, 8, width), lambda i: (i, 0, 0)),
    ]
    if not whole:
        outs.append(shape(tokens, width, kind=jnp.float32))
        out_specs.append(tile(rows, width))
    return run(
        kernel,
        (tokens // rows,),
        ins,
        [
            tile(rows, width),
            tile(rows, width),
            tile(rows, 1),
            stack_tile(cols, rows, wide),
            pl.BlockSpec((1, rows), lambda i: (0, i)),
        ]
        + [whole_spec(x) for x in ins[5:]],
        outs,
        out_specs,
        2 * tokens * width * cols * wide + 10 * tokens * group * cols * heads * HDIM,
    )


def outer_middle(value, attended, expand, shrink, norms):
    tokens, width = value.shape
    cols = len(expand[0])
    wide = expand[0][0].shape[1]

    def kernel(value_ref, attended_ref, norm_ref, *refs):
        unit_ref, inverse_ref, low_ref, active_ref, slope_ref, ffn_ref = refs[4 * cols :]
        hid, unit, inverse = kernel_norm(
            value_ref[...] + attended_ref[...], norm_ref[0:1], norm_ref[1:2]
        )
        low = hid.astype(low_type)
        unit_ref[...] = unit
        inverse_ref[...] = inverse
        low_ref[...] = low
        for c in range(cols):
            span = slice(c * wide, (c + 1) * wide)
            active_ref[:, span], slope_ref[:, span] = gelu_and_slope(
                dot(low, down(refs[: 2 * cols], cols)(c))
            )
        ffn_ref[...] = shrink_values(active_ref[...], refs[2 * cols : 4 * cols], cols)

    ins = [value, attended, norms] + flat(expand) + flat(shrink)
    outs = [
        shape(tokens, width, kind=jnp.float32),
        shape(tokens, 1, kind=jnp.float32),
        shape(tokens, width),
        shape(tokens, cols * wide),
        shape(tokens, cols * wide),
        shape(tokens, width, kind=jnp.float32),
    ]
    return run(
        kernel,
        (1,),
        ins,
        [whole_spec(x) for x in ins],
        outs,
        [whole_spec(x) for x in outs],
        4 * tokens * width * cols * wide,
    )


def outer_turn(unit, ffn, grad, slope, shrink, expand, norms):
    tokens, width = unit.shape
    cols = len(expand[0])
    wide = expand[0][0].shape[1]

    def kernel(unit_ref, ffn_ref, grad_ref, slope_ref, norm_ref, *refs):
        out_ref, dffn_ref, dpre_ref, dsecond_ref, back_ref, sum_ref = refs[4 * cols :]
        hid = unit_ref[...] * norm_ref[0:1] + norm_ref[1:2]
        result, second, inverse = kernel_norm(hid + ffn_ref[...], norm_ref[2:3], norm_ref[3:4])
        out_ref[...] = result
        upstream = grad_ref[...]

        def put(c, value):
            dpre_ref[:, c * wide : (c + 1) * wide] = value

        dffn_ref[...], dsecond_ref[...], back_ref[...] = ffn_backward_values(
            upstream,
            second,
            inverse,
            lambda c: slope_ref[:, c * wide : (c + 1) * wide],
            norm_ref[2:3],
            refs[: 2 * cols],
            refs[2 * cols : 4 * cols],
            cols,
            put,
        )
        put_sums(sum_ref, column_sum(upstream * second), column_sum(upstream), width)

    ins = [unit, ffn, grad, slope, norms] + flat(shrink) + flat(expand)
    outs = [
        shape(tokens, width, kind=jnp.float32),
        shape(tokens, width),
        shape(tokens, cols * wide),
        shape(tokens, width, kind=jnp.float32),
        shape(tokens, width, kind=jnp.float32),
        shape(1, 8, width, kind=jnp.float32),
    ]
    return run(
        kernel,
        (1,),
        ins,
        [whole_spec(x) for x in ins],
        outs,
        [whole_spec(x) for x in outs],
        4 * tokens * width * cols * wide,
    )


def ffn_grads(hid_low, dpre, active, dffn):
    dp_count, col_count = lax.axis_size("dp"), lax.axis_size("col")
    half = hid_low.shape[1] // 2
    theirs_first = dot_rows(hid_low[:, half:], dpre).astype(low_type)
    theirs_second = dot_rows(active, dffn[:, half:]).astype(low_type)
    mine_first = dot_rows(hid_low[:, :half], dpre).astype(low_type)
    mine_second = dot_rows(active, dffn[:, :half]).astype(low_type)
    wide = mine_first.shape[1] // col_count
    tall = mine_second.shape[0] // col_count
    low, high = half // dp_count, tall // dp_count
    got_first, got_second = row_swap(theirs_first), row_swap(theirs_second)

    def kernel(*refs):
        ins, outs = refs[:8], refs[8:]
        for k in range(2):
            first = add_low(ins[2 * k][...], ins[2 * k + 1][...])
            second = add_low(ins[4 + 2 * k][...], ins[5 + 2 * k][...])
            for place in range(dp_count):
                part = first[place * low : (place + 1) * low]
                outs[k][0, place, :low] = part[:, :half]
                outs[k][0, place, low:] = part[:, half:]
                outs[2 + k][0, place] = second[place * high : (place + 1) * high]

    specs = (
        [pl.BlockSpec((half, wide), lambda i: (0, 2 * i))] * 2
        + [pl.BlockSpec((half, wide), lambda i: (0, 2 * i + 1))] * 2
        + [pl.BlockSpec((tall, half), lambda i: (i, 0))] * 2
        + [pl.BlockSpec((tall, half), lambda i: (i + 2, 0))] * 2
    )
    return pack_call(
        kernel,
        [mine_first, got_first] * 2 + [mine_second, got_second] * 2,
        specs,
        dp_count,
        (2 * low, high),
        half,
    )


def add_low(left, right):
    return (left.astype(jnp.float32) + right.astype(jnp.float32)).astype(low_type)


def pack_call(kernel, ins, specs, dp_count, heights, width):
    heights = [heights[0], heights[0], heights[1], heights[1]]
    return run(
        kernel,
        (2,),
        ins,
        specs,
        [shape(2, dp_count, height, width) for height in heights],
        [
            pl.BlockSpec((1, dp_count, height, width), lambda i: (i, 0, 0, 0))
            for height in heights
        ],
        0,
    )


def first_swaps(packed):
    keep_a, send_a, keep_b, send_b = packed
    got_a, got_b = col_swap(send_a, 1), col_swap(send_b, 2)

    def kernel(*refs):
        for half in range(2):
            total = add_low(refs[2 * half][...], refs[2 * half + 1][...])
            refs[4 + 2 * half][...] = total[0]
            refs[5 + 2 * half][...] = total[1]

    ins = [keep_a, got_a, keep_b, got_b]
    outs = [shape(*x.shape[1:]) for x in (keep_a, keep_a, keep_b, keep_b)]

    def spec(array):
        front = array.ndim - 3
        return pl.BlockSpec(
            (2,) * front + (1,) + array.shape[front + 1 :],
            lambda i: (0,) * front + (i, 0, 0),
        )

    return run(
        kernel, (keep_a.shape[1],), ins, [spec(x) for x in ins], outs, [spec(x) for x in outs], 0
    )


def second_swaps(sums):
    own_a, on_a, own_b, on_b = sums
    got_a, got_b = col_swap(on_a, 2), col_swap(on_b, 1)
    count, high_a, width = own_a.shape
    high_b = own_b.shape[1]

    def kernel(place_ref, *refs):
        for step in range(count):
            at = lax.rem(place_ref[0] + step, count)
            refs[4 + step][:high_a] = add_low(refs[0][at], refs[1][at])
            refs[4 + step][high_a:] = add_low(refs[2][at], refs[3][at])

    ins = [own_a, got_a, own_b, got_b]
    whole = pl.BlockSpec(memory_space=pltpu.VMEM)
    return pl.pallas_call(
        kernel,
        out_shape=[jax.ShapeDtypeStruct((high_a + high_b, width), low_type)] * count,
        grid_spec=pltpu.PrefetchScalarGridSpec(
            num_scalar_prefetch=1, grid=(), in_specs=[whole] * 4, out_specs=[whole] * count
        ),
        cost_estimate=pl.CostEstimate(
            flops=0, bytes_accessed=6 * count * (high_a + high_b) * width, transcendentals=0
        ),
        name="add_second",
    )(lax.axis_index("dp").reshape(1), *ins)


def rows_over(value):
    return col_swap(value, 2)


def dp_swaps(pieces):
    got = [dp_shift(piece, step) for step, piece in enumerate(pieces) if step]
    total = pieces[0].astype(jnp.float32)
    for piece in got:
        total = total + piece.astype(jnp.float32)
    return total


def row_products(left, right, part):
    cols, tokens, wide = right.shape
    half = left.shape[1] // 2

    def kernel(left_ref, right_ref, out_ref):
        out_ref[0] = dot_rows(left_ref[...], right_ref[0]).astype(low_type)

    return run(
        kernel,
        (cols,),
        [left, right],
        [
            pl.BlockSpec((tokens, half), lambda c: (0, part)),
            pl.BlockSpec((1, tokens, wide), lambda c: (c, 0, 0)),
        ],
        [shape(cols, half, wide)],
        [pl.BlockSpec((1, half, wide), lambda c: (c, 0, 0))],
        2 * tokens * half * cols * wide,
    )[0]


def attention_grads(x_low, dqkv, mixed, datt, ready):
    dp_count, col_count = lax.axis_size("dp"), lax.axis_size("col")
    half = x_low.shape[1] // 2
    wide = dqkv.shape[2]
    theirs_second = dot_rows(mixed, datt[:, half:]).astype(low_type)
    theirs_first = row_products(x_low, dqkv, 1)
    x_low, mixed = after((x_low, mixed), ready)
    mine_first = row_products(x_low, dqkv, 0)
    mine_second = dot_rows(mixed, datt[:, :half]).astype(low_type)
    got_first, got_second = row_swap(theirs_first), row_swap(theirs_second)
    tall = mine_second.shape[0] // col_count
    low, high = half // dp_count, tall // dp_count
    end_rows = low // 2
    assert (wide - half) * 2 == half

    def kernel(*refs):
        ins, outs = refs[:12], refs[12:]
        for k in range(2):
            first = add_low(ins[2 * k][0, :, :half], ins[2 * k + 1][0, :, :half])
            other = ins[4 + 2 * k][0, :, half:].astype(jnp.float32)
            other = other + ins[5 + 2 * k][0, :, half:].astype(jnp.float32)
            second = add_low(ins[8 + 2 * k][...], ins[9 + 2 * k][...])
            for place in range(dp_count):
                outs[k][0, place] = first[place * low : (place + 1) * low]
                ends = other[place * low : (place + 1) * low]
                outs[2 + k][0, place, :end_rows] = jnp.concatenate(
                    [ends[:end_rows], ends[end_rows:]], axis=1
                ).astype(low_type)
                outs[2 + k][0, place, end_rows:] = second[place * high : (place + 1) * high]

    def blocks(index):
        return [pl.BlockSpec((1, half, wide), lambda i: (index(i), 0, 0))] * 2

    specs = (
        blocks(lambda i: 2 * i)
        + blocks(lambda i: 2 * i + 1)
        + blocks(lambda i: i)
        + blocks(lambda i: i + 2)
        + [pl.BlockSpec((tall, half), lambda i: (i, 0))] * 2
        + [pl.BlockSpec((tall, half), lambda i: (i + 2, 0))] * 2
    )
    return pack_call(
        kernel,
        [mine_first, got_first] * 4 + [mine_second, got_second] * 2,
        specs,
        dp_count,
        (low, end_rows + high),
        half,
    )


def unpack_ffn(packed, low):
    return jnp.concatenate([packed[:low], packed[low : 2 * low]], axis=1), packed[2 * low :]


def unpack_attention(packed, low):
    half = packed.shape[1] // 2
    ends = packed[low : low + low // 2]
    ends = jnp.concatenate([ends[:, :half], ends[:, half:]], axis=0)
    return jnp.concatenate([packed[:low], ends], axis=1), packed[low + low // 2 :]


def halves(value, axis):
    return jnp.split(value, 2, axis=axis)


def first_grad(left, right, through):
    mine_left, theirs_left = halves(left, 1)
    theirs = [dot_rows(theirs_left, block).astype(low_type) for block in right]
    mine = [dot_rows(mine_left, block).astype(low_type) for block in right]
    return scatter_grad(mine, theirs, through)


def second_grad(left, right, through):
    mine_right, theirs_right = halves(right, 1)
    count = lax.axis_size("col")
    theirs = dot_rows(left, theirs_right).astype(low_type)
    mine = dot_rows(left, mine_right).astype(low_type)
    got = row_swap(theirs)
    total = mine.astype(jnp.float32) + got.astype(jnp.float32)
    return dp_scatter_sum(plane_sum(jnp.split(total, count, 0), through))


def to_tokens(value, row):
    parts = value.reshape((2, -1) + value.shape[1:])
    mine = lax.dynamic_index_in_dim(parts, row, 0, False)
    theirs = lax.dynamic_index_in_dim(parts, 1 - row, 0, False)
    return jnp.concatenate([mine, row_swap(theirs)], axis=1)


def to_features(value, row):
    mine, theirs = halves(value, 1)
    got = row_swap(theirs)
    first = jnp.where(row == 0, mine, got)
    second = jnp.where(row == 0, got, mine)
    return jnp.concatenate([first, second], axis=0)


def swap_features(value):
    first, second = halves(value, 1)
    return jnp.concatenate([second, first], axis=1)


def swap_rows(value):
    first, second = halves(value, 0)
    return jnp.concatenate([second, first], axis=0)


def layer(
    hidden,
    lengths,
    inner_project,
    inner_merge,
    inner_expand,
    inner_shrink,
    inner_norms,
    outer_places,
    outer_project,
    outer_merge,
    outer_expand,
    outer_shrink,
    outer_norms,
    out_grad,
):
    dp_count, row_count, col_count = (lax.axis_size(name) for name in ("dp", "row", "col"))
    dp, row, col = (lax.axis_index(name) for name in ("dp", "row", "col"))
    everyone = ("dp", "row", "col")
    device_count = dp_count * row_count * col_count
    value = to_tokens(hidden, row)
    grad_in = to_tokens(out_grad, row)
    tokens, width = value.shape
    segs = tokens // SEG

    small = jnp.concatenate([inner_norms, outer_norms, outer_places], axis=1)
    small = lax.all_to_all(
        jnp.broadcast_to(small[None], (device_count,) + small.shape), everyone, 0, 0, tiled=True
    )
    small_got = small
    small = small.reshape((dp_count, row_count, -1) + small.shape[2:])
    small = jnp.concatenate(
        [
            lax.dynamic_index_in_dim(small, row, 1, False).reshape(-1, small.shape[-1]),
            lax.dynamic_index_in_dim(small, 1 - row, 1, False).reshape(-1, small.shape[-1]),
        ],
        axis=0,
    )
    vectors = small.T
    inner_gains = vectors[0:4]
    outer_gains = vectors[4:8]
    places = vectors[8:]

    length = lax.dynamic_index_in_dim(lengths, col // 2, 0, False)
    half = col % 2
    seg_own = (half * 2 + row) * segs + jnp.arange(segs, dtype=jnp.int32)
    spot = (seg_own[:, None] * SEG + jnp.arange(SEG, dtype=jnp.int32)[None]).reshape(tokens)
    valid = (spot < length).astype(jnp.float32)
    keep_tok = ((spot < length) | (spot % SEG == 0)).astype(jnp.float32)
    seg_all = jnp.concatenate(
        [
            (h * 2 + r) * segs + jnp.arange(segs, dtype=jnp.int32)
            for h in (half, 1 - half)
            for r in (row, 1 - row)
        ]
    )
    keep_seg = (seg_all * SEG < length).astype(jnp.float32)
    one_hot = (seg_own[:, None] == jnp.arange(NSEG, dtype=jnp.int32)[None]).astype(jnp.float32)

    keep_row = keep_tok[None]
    rows_tile = 2 * SEG
    inner, outer_steps, (x_in, qkv, mixed_in) = gather_weights(
        (inner_project, inner_merge, inner_expand, inner_shrink),
        (outer_project, outer_merge, outer_expand, outer_shrink),
        lambda project: project_attend(value, keep_row, project, None, SEG, rows_tile),
        small_got,
    )
    unit_one, inverse_one, hid_in, active_in, slope = merge_expand(
        value, mixed_in, inner[1], inner[2], inner_gains, rows_tile
    )
    outer_project = outer_steps[0](hid_in)
    inner_out, unit_two, inverse_two = shrink_norm(
        unit_one, active_in, inner[3], inner_gains, rows_tile
    )
    outer_merge, outer_shrink = outer_steps[1](inner_out)
    grid = inner_out.reshape(segs, SEG, width)
    masked_grad = (grad_in * valid[:, None]).reshape(segs, SEG, width)
    heads_in = grid[:, 0] + jnp.dot(
        one_hot, places, precision=highest, preferred_element_type=jnp.float32
    )
    rows = jnp.concatenate([heads_in, masked_grad[:, 0]], axis=0)
    rows = jnp.stack([rows, swap_features(row_swap(rows))]).reshape(2, 2, segs, width)
    rows = jnp.stack([rows, col_swap(rows, 1)])
    rows = rows.transpose(2, 0, 1, 3, 4).reshape(2, NSEG, width)

    def join(partial_sum):
        return partial_sum + swap_rows(col_swap(partial_sum, 1))

    flat_grad = masked_grad.reshape(tokens, width)
    main = ffn_backward(
        flat_grad, unit_two, inverse_two, slope, inner[3], inner[2], inner_gains, rows_tile
    )
    outer_expand = outer_steps[2](main[3])
    outer = (outer_project, outer_merge, outer_expand, outer_shrink)
    rows = after(rows, main[3])
    x_low, o_qkv, mixed, attended = project_attend(
        rows[0], keep_seg[None], outer[0], outer[1], NSEG, NSEG
    )
    o_unit, o_inverse, hid_low, active, o_slope, ffn = outer_middle(
        rows[0], join(attended), outer[2], outer[3], outer_gains
    )
    outer_out, dffn, dpre, dsecond, back, o_second = outer_turn(
        o_unit, join(ffn), rows[1], o_slope, outer[3], outer[2], outer_gains
    )
    datt, dqkv, back, o_first, dfirst = attention_backward(
        dsecond + join(back),
        o_unit,
        o_inverse,
        o_qkv,
        keep_seg[None],
        outer[0],
        outer[1],
        outer_gains,
        NSEG,
        NSEG,
        False,
    )
    dheads = dfirst + join(back)
    outer_norm_grad = jnp.concatenate([o_first[0, :2], o_second[0, :2]], axis=0).T
    dheads = dheads[:segs]
    layer_out = (
        jnp.concatenate([outer_out[:segs, None], grid[:, 1:]], axis=1).reshape(tokens, width)
        * valid[:, None]
    )
    places_grad = jnp.dot(dheads.T, one_hot, precision=highest, preferred_element_type=jnp.float32)

    dffn_in, dpre_in, dhid_in, few_sums = ffn_backward_firsts(
        flat_grad,
        dheads,
        unit_two,
        inverse_two,
        slope,
        inner[3],
        inner[2],
        inner_gains,
        main[:3],
    )
    wide_dp = dp_count > 4
    if not wide_dp:
        ffn_packed = ffn_grads(hid_in, dpre_in, active_in, dffn_in)
        dhid_in = after(dhid_in, ffn_packed[0])
    datt_in, dqkv_in, input_grad, first_sums = attention_backward(
        dhid_in,
        unit_one,
        inverse_one,
        qkv,
        keep_row,
        inner[0],
        inner[1],
        inner_gains,
        SEG,
        rows_tile,
        True,
    )
    inner_norm_grad = jnp.concatenate(
        [jnp.sum(first_sums, 0)[:2], jnp.sum(main[3], 0)[:2] + few_sums[0, :2]], axis=0
    ).T
    if wide_dp:
        inner_grads = (
            first_grad(x_in, dqkv_in, 1),
            second_grad(mixed_in, datt_in, 2),
            first_grad(hid_in, jnp.split(dpre_in, col_count, 1), 1),
            second_grad(active_in, dffn_in, 2),
        )
        gate = None
    else:
        ffn_sums = first_swaps(ffn_packed)
        attention_packed = attention_grads(x_in, dqkv_in, mixed_in, datt_in, ffn_sums[0])
        ffn_pieces = second_swaps(ffn_sums)
        gate = attention_packed[0]
    shared = [halves(part, 1)[0] for part in (x_low, hid_low, datt, dffn)]
    own, over = zip(*([halves(part, 1) for part in (active, dpre, mixed)] + [tuple(dqkv)]))
    packed = jnp.concatenate(
        [
            jnp.concatenate(shared + list(own), axis=1),
            rows_over(jnp.concatenate(shared + list(over), axis=1)),
        ],
        axis=0,
    )
    if dp_count > 4:
        packed = lax.all_gather(packed, "dp", axis=0, tiled=True)
    else:
        got = [dp_shift(packed, step) for step in range(1, dp_count)]
        packed = jnp.concatenate([packed] + got, axis=0)
    small_grad = jnp.concatenate([inner_norm_grad, 0.25 * outer_norm_grad, places_grad], axis=1)
    if gate is not None:
        small_grad = after(small_grad, gate)
    columns = small_grad.shape[1]
    blocks = small_grad.reshape(2, dp_count, col_count, -1, columns)
    blocks = jnp.where(row == 0, blocks, blocks[::-1]).transpose(1, 0, 2, 3, 4)
    blocks = lax.all_to_all(
        blocks.reshape(device_count, -1, columns), everyone, 0, 0, tiled=True
    )
    small_sum = jnp.sum(blocks, axis=0)
    if not wide_dp:
        attention_sums = first_swaps(attention_packed)
        ffn_total = dp_swaps(after(ffn_pieces, small_sum))
        attention_pieces = second_swaps(after(attention_sums, small_sum))
        attention_total = dp_swaps(attention_pieces)
        inner_grads = unpack_attention(attention_total, inner_expand.shape[0]) + unpack_ffn(
            ffn_total, inner_expand.shape[0]
        )
    ends = []
    for part in shared + list(own):
        ends.append((ends[-1] if ends else 0) + part.shape[1])
    x_all, hid_all, datt_all, dffn_all, active_all, dpre_all, mixed_all, dqkv_all = jnp.split(
        packed, ends[:-1], axis=1
    )

    def own_rows(product):
        return lax.dynamic_index_in_dim(
            product.reshape((dp_count, -1) + product.shape[1:]), dp, 0, False
        )

    outer_grads = (
        own_rows(dot_rows(x_all, dqkv_all)),
        own_rows(dot_rows(mixed_all, datt_all)),
        own_rows(dot_rows(hid_all, dpre_all)),
        own_rows(dot_rows(active_all, dffn_all)),
    )

    return (
        to_features(layer_out, row),
        to_features(input_grad, row),
        inner_grads[0],
        inner_grads[1],
        inner_grads[2],
        inner_grads[3],
        small_sum[:, 0:4],
        small_sum[:, 8:],
        outer_grads[0],
        outer_grads[1],
        outer_grads[2],
        outer_grads[3],
        small_sum[:, 4:8],
    )


def solution(mesh):
    tokens = P(("dp", "col"), "row")
    first = P(("row", "dp"), "col")
    second = P(("col", "dp"), "row")
    small = P(("row", "dp", "col"), None)
    weights = (first, second, first, second)
    return jax.shard_map(
        layer,
        mesh=mesh,
        in_specs=(tokens, P("dp")) + weights + (small, small) + weights + (small, tokens),
        out_specs=(tokens, tokens) + weights + (small, small) + weights + (small,),
        check_vma=False,
    )
```

```python
import jax
import jax.numpy as jnp
from jax import lax
from jax.experimental import pallas as pl
from jax.experimental.pallas import tpu as pltpu
from jax.sharding import PartitionSpec as P


HDIM = 64
SEG = 128
NSEG = 16
epsilon = 1e-06
highest = lax.Precision.HIGHEST
low_type = jnp.bfloat16


def dot(left, right):
    return jnp.dot(left, right, preferred_element_type=jnp.float32)


def dot_t(left, right):
    return lax.dot_general(
        left, right, (((1,), (1,)), ((), ())), preferred_element_type=jnp.float32
    )


def dot_rows(left, right):
    return lax.dot_general(
        left, right, (((0,), (0,)), ((), ())), preferred_element_type=jnp.float32
    )


def row_swap(value):
    return lax.ppermute(value, "row", [(0, 1), (1, 0)])


def col_swap(value, mask):
    return lax.ppermute(value, "col", [(i, i ^ mask) for i in range(lax.axis_size("col"))])


def dp_shift(value, step):
    count = lax.axis_size("dp")
    return lax.ppermute(value, "dp", [(i, (i + step) % count) for i in range(count)])


def after(value, earlier):
    return lax.optimization_barrier((value, earlier))[0]


def dp_pieces(value):
    count = lax.axis_size("dp")
    return [value] + [dp_shift(value, step) for step in range(1, count)]


def place_pieces(pieces, cut=None):
    count = len(pieces)
    height, width = pieces[0].shape
    bounds = (0, height) if cut is None else (0, cut, height)
    spans = list(zip(bounds[:-1], bounds[1:]))

    def kernel(place_ref, *refs):
        for step in range(count):
            at = lax.rem(place_ref[0] - step + count, count)
            for (low, high), out in zip(spans, refs[count:]):
                size = high - low
                out[pl.ds(pl.multiple_of(at * size, 16), size), :] = refs[step][low:high]

    whole = pl.BlockSpec(memory_space=pltpu.VMEM)
    outs = [
        jax.ShapeDtypeStruct((count * (high - low), width), pieces[0].dtype) for low, high in spans
    ]
    placed = pl.pallas_call(
        kernel,
        out_shape=outs,
        grid_spec=pltpu.PrefetchScalarGridSpec(
            num_scalar_prefetch=1,
            grid=(),
            in_specs=[whole] * count,
            out_specs=[whole] * len(outs),
        ),
        cost_estimate=pl.CostEstimate(
            flops=0, bytes_accessed=4 * count * height * width, transcendentals=0
        ),
        name="place_pieces",
    )(lax.axis_index("dp").reshape(1), *pieces)
    return placed[0] if cut is None else placed


def dp_scatter_sum(value):
    count = lax.axis_size("dp")
    if count > 4:
        return lax.psum_scatter(value, "dp", scatter_dimension=0, tiled=True)
    place = lax.axis_index("dp")
    parts = value.reshape((count, -1) + value.shape[1:])
    total = lax.dynamic_index_in_dim(parts, place, 0, False)
    for step in range(1, count):
        piece = lax.dynamic_index_in_dim(parts, (place + step) % count, 0, False)
        total = total + dp_shift(piece.astype(low_type), step).astype(jnp.float32)
    return total


def plane_blocks(own, through):
    side = col_swap(own, 1)
    over = col_swap(own, 2)
    far = col_swap(over, 1) if through == 1 else col_swap(side, 2)
    mine = (own, side, over, far)
    return (mine, tuple(row_swap(block) for block in mine))


def pair_blocks(own):
    mine = (own, col_swap(own, 2))
    return (mine, tuple(row_swap(block) for block in mine))


def gather_wide(inner_shards, outer_shards, first_use):
    inner_own, outer_own = (
        [lax.all_gather(shard, "dp", axis=0, tiled=True) for shard in group]
        for group in (inner_shards, outer_shards)
    )
    inner = [plane_blocks(own, through) for own, through in zip(inner_own, (1, 2, 1, 2))]
    outer = [pair_blocks(own) for own in outer_own]
    steps = (lambda gate: outer[0], lambda gate: (outer[1], outer[3]), lambda gate: outer[2])
    return inner, steps, first_use(inner[0])


def gather_weights(inner_shards, outer_shards, first_use, early):
    inner_shards = [shard.astype(low_type) for shard in inner_shards]
    outer_shards = [shard.astype(low_type) for shard in outer_shards]
    if lax.axis_size("dp") > 4:
        return gather_wide(inner_shards, outer_shards, first_use)
    pieces = dp_pieces(inner_shards[0])
    merge_pieces = dp_pieces(inner_shards[1])
    own = place_pieces(pieces)
    expand_pieces = dp_pieces(after(inner_shards[2], own))
    side, over, far_project = (col_swap(own, mask) for mask in (1, 2, 3))
    project = both_rows((own, side, over, far_project))
    own = place_pieces(after(merge_pieces, (side, early)))
    side, over, far_merge = (col_swap(own, mask) for mask in (1, 2, 3))
    merge = both_rows((own, side, over, far_merge))
    own = place_pieces(after(expand_pieces, (side, over, far_merge, far_project)))
    shrink_pieces = dp_pieces(after(inner_shards[3], expand_pieces))
    side, over, far_expand = (col_swap(own, mask) for mask in (1, 2, 3))
    used = first_use(after(project, (own, merge)))
    expand = both_rows((own, side, over, far_expand))
    own = place_pieces(after(shrink_pieces, (side, over, used[0])))
    side, over, far = (col_swap(own, mask) for mask in (1, 2, 3))
    shrink = both_rows((own, side, over, far))
    rows = jnp.concatenate([outer_shards[1], outer_shards[3]], axis=0)
    first = dp_pieces(after(outer_shards[0], shrink_pieces))
    second = dp_pieces(after(rows, first[1]))
    third = dp_pieces(after(outer_shards[2], second[1]))

    def outer_project(gate):
        return pair_blocks(place_pieces(after(first, gate)))

    def outer_rows(gate):
        merge, shrink = place_pieces(after(second, gate), outer_shards[1].shape[0])
        return pair_blocks(merge), pair_blocks(shrink)

    def outer_expand(gate):
        own = place_pieces(after(third, gate))
        return pair_blocks(own)

    return (project, merge, expand, shrink), (outer_project, outer_rows, outer_expand), used


def both_rows(mine):
    return (mine, tuple(row_swap(block) for block in mine))


def plane_sum(sums, through):
    other = 3 - through
    own = sums[0] + col_swap(sums[through].astype(low_type), through).astype(jnp.float32)
    onward = sums[other] + col_swap(sums[3].astype(low_type), through).astype(jnp.float32)
    return own + col_swap(onward.astype(low_type), other).astype(jnp.float32)


def scatter_grad(mine, theirs, through):
    sums = [
        block.astype(jnp.float32) + row_swap(sent).astype(jnp.float32)
        for block, sent in zip(mine, theirs)
    ]
    return dp_scatter_sum(plane_sum(sums, through))


def whole_spec(array):
    return pl.BlockSpec(
        array.shape, lambda i: (0,) * array.ndim, pipeline_mode=pl.Buffered(1)
    )


def flat(blocks):
    return [block for half in blocks for block in half]


def grouped(refs, cols):
    return (refs[:cols], refs[cols : 2 * cols])


def down(refs, cols):
    return lambda c: jnp.concatenate([refs[c][...], refs[cols + c][...]], axis=0)


def across(refs, cols):
    return lambda c: jnp.concatenate([refs[c][...], refs[cols + c][...]], axis=1)


def kernel_norm(value, gain, shift):
    average = jnp.mean(value, axis=1, keepdims=True)
    centred = value - average
    inverse = lax.rsqrt(jnp.mean(centred * centred, axis=1, keepdims=True) + epsilon)
    unit = centred * inverse
    return unit * gain + shift, unit, inverse


def kernel_norm_backward(upstream, unit, inverse, gain):
    scaled = upstream * gain
    centre = jnp.mean(scaled, axis=1, keepdims=True)
    slope = jnp.mean(scaled * unit, axis=1, keepdims=True)
    return inverse * (scaled - centre - unit * slope)


def gelu_and_slope(value):
    share = 0.5 + 0.5 * lax.erf(value * 0.7071067811865476)
    density = 0.3989422804014327 * jnp.exp(-0.5 * value * value)
    return (value * share).astype(low_type), (share + value * density).astype(low_type)


def softmax(pairs, allowed):
    scores = [dot_t(query, key_part) * HDIM ** (-0.5) for query, key_part in pairs]
    scores = [jnp.where(allowed, one, -1000000000.0) for one in scores]
    tops = [jnp.max(one, axis=1, keepdims=True) for one in scores]
    expos = [jnp.exp(one - top) for one, top in zip(scores, tops)]
    shares = [1.0 / jnp.sum(expo, axis=1, keepdims=True) for expo in expos]
    return [expo * share for expo, share in zip(expos, shares)]


def head_parts(qkv, head):
    start = head * 3 * HDIM
    return [qkv[:, start + k * HDIM : start + (k + 1) * HDIM] for k in range(3)]


def run(kernel, grid, ins, in_specs, outs, out_specs, flops, aliases=None):
    moved = sum(x.size * x.dtype.itemsize for x in list(ins) + list(outs))
    return pl.pallas_call(
        kernel,
        out_shape=outs,
        grid=grid,
        in_specs=in_specs,
        out_specs=out_specs,
        input_output_aliases=aliases or {},
        cost_estimate=pl.CostEstimate(flops=flops, bytes_accessed=moved, transcendentals=0),
    )(*ins)


def shape(*dims, kind=low_type):
    return jax.ShapeDtypeStruct(dims, kind)


def tile(rows, width):
    return pl.BlockSpec((rows, width), lambda i: (i, 0))


def stack_tile(cols, rows, width):
    return pl.BlockSpec((cols, rows, width), lambda i: (0, i, 0))


def project_attend(value, keep, project, merge, group, rows):
    tokens, width = value.shape
    cols = len(project[0])
    wide = project[0][0].shape[1]
    heads = wide // (3 * HDIM)
    out_width = cols * heads * HDIM
    merge_in = flat(merge) if merge else []

    def kernel(value_ref, keep_ref, *refs):
        weight = down(refs, cols)
        merge_refs = refs[2 * cols : 2 * cols + len(merge_in)]
        low_ref, qkv_ref, mixed_ref = refs[2 * cols + len(merge_in) :][:3]
        low = value_ref[...].astype(low_type)
        low_ref[...] = low
        qkvs = []
        for c in range(cols):
            qkvs.append(dot(low, weight(c)).astype(low_type))
            qkv_ref[c] = qkvs[c]
        for g in range(rows // group):
            span = slice(g * group, (g + 1) * group)
            allowed = keep_ref[:, span] > 0.5
            outs = []
            for c in range(cols):
                parts = [head_parts(qkvs[c][span], head) for head in range(heads)]
                probs = softmax([part[:2] for part in parts], allowed)
                outs += [
                    dot(some.astype(low_type), part[2]) for some, part in zip(probs, parts)
                ]
            mixed_ref[span] = jnp.concatenate(outs, axis=1).astype(low_type)
        if merge_in:
            mixed = mixed_ref[...]
            for r, half in enumerate(grouped(merge_refs, cols)):
                joined = jnp.concatenate([ref[...] for ref in half], axis=0)
                size = joined.shape[1]
                refs[-1][:, r * size : (r + 1) * size] = dot(mixed, joined)

    ins = [value, keep] + flat(project) + merge_in
    outs = [
        shape(tokens, width),
        shape(cols, tokens, wide),
        shape(tokens, out_width),
    ]
    out_specs = [tile(rows, width), stack_tile(cols, rows, wide), tile(rows, out_width)]
    if merge_in:
        outs.append(shape(tokens, width, kind=jnp.float32))
        out_specs.append(tile(rows, width))
    return run(
        kernel,
        (tokens // rows,),
        ins,
        [tile(rows, width), pl.BlockSpec((1, rows), lambda i: (0, i))]
        + [whole_spec(x) for x in ins[2:]],
        outs,
        out_specs,
        2 * tokens * width * cols * wide + 4 * tokens * group * out_width,
    )


def merge_values(mixed, merge_refs, cols):
    parts = [
        dot(mixed, jnp.concatenate([ref[...] for ref in half], axis=0))
        for half in grouped(merge_refs, cols)
    ]
    return jnp.concatenate(parts, axis=1)


def merge_expand(value, mixed, merge, expand, norms, rows):
    tokens, width = value.shape
    cols = len(expand[0])
    wide = expand[0][0].shape[1]

    def kernel(value_ref, mixed_ref, norm_ref, *refs):
        merge_refs, expand_refs = refs[: 2 * cols], refs[2 * cols : 4 * cols]
        unit_ref, inverse_ref, low_ref, active_ref, slope_ref = refs[4 * cols :]
        attended = merge_values(mixed_ref[...], merge_refs, cols)
        hid, unit, inverse = kernel_norm(
            value_ref[...] + attended, norm_ref[0:1], norm_ref[1:2]
        )
        low = hid.astype(low_type)
        unit_ref[...] = unit
        inverse_ref[...] = inverse
        low_ref[...] = low
        weight = down(expand_refs, cols)
        for c in range(cols):
            span = slice(c * wide, (c + 1) * wide)
            active_ref[:, span], slope_ref[:, span] = gelu_and_slope(dot(low, weight(c)))

    ins = [value, mixed, norms] + flat(merge) + flat(expand)
    return run(
        kernel,
        (tokens // rows,),
        ins,
        [tile(rows, width), tile(rows, width)] + [whole_spec(x) for x in ins[2:]],
        [
            shape(tokens, width, kind=jnp.float32),
            shape(tokens, 1, kind=jnp.float32),
            shape(tokens, width),
            shape(tokens, cols * wide),
            shape(tokens, cols * wide),
        ],
        [tile(rows, width), tile(rows, 1), tile(rows, width)] + [tile(rows, cols * wide)] * 2,
        2 * tokens * width * (width + cols * wide),
    )


def shrink_values(active, shrink_refs, cols):
    parts = [
        dot(active, jnp.concatenate([ref[...] for ref in half], axis=0))
        for half in grouped(shrink_refs, cols)
    ]
    return jnp.concatenate(parts, axis=1)


def shrink_norm(unit, active, shrink, norms, rows):
    tokens, width = unit.shape
    cols = len(shrink[0])

    def kernel(unit_ref, active_ref, norm_ref, *refs):
        out_ref, second_ref, inverse_ref = refs[2 * cols :]
        hid = unit_ref[...] * norm_ref[0:1] + norm_ref[1:2]
        ffn = shrink_values(active_ref[...], refs[: 2 * cols], cols)
        out_ref[...], second_ref[...], inverse_ref[...] = kernel_norm(
            hid + ffn, norm_ref[2:3], norm_ref[3:4]
        )

    ins = [unit, active, norms] + flat(shrink)
    return run(
        kernel,
        (tokens // rows,),
        ins,
        [tile(rows, width), tile(rows, active.shape[1])] + [whole_spec(x) for x in ins[2:]],
        [
            shape(tokens, width, kind=jnp.float32),
            shape(tokens, width, kind=jnp.float32),
            shape(tokens, 1, kind=jnp.float32),
        ],
        [tile(rows, width), tile(rows, width), tile(rows, 1)],
        2 * tokens * width * active.shape[1],
    )


def ffn_backward_values(upstream, unit, inverse, slope, gain, shrink_refs, expand_refs, cols, put):
    dsecond = kernel_norm_backward(upstream, unit, inverse, gain)
    dffn = dsecond.astype(low_type)
    back = None
    for c in range(cols):
        dactive = dot_t(dffn, across(shrink_refs, cols)(c))
        dpre = (dactive * slope(c).astype(jnp.float32)).astype(low_type)
        put(c, dpre)
        part = dot_t(dpre, down(expand_refs, cols)(c))
        back = part if back is None else back + part
    return dffn, dsecond, back


def put_sums(ref, first, second, width):
    ref[0] = jnp.concatenate([first, second, jnp.zeros((6, width), jnp.float32)], axis=0)


def column_sum(value):
    return jnp.sum(value, axis=0, keepdims=True)


def ffn_backward(grad, unit, inverse, slope, shrink, expand, norms, rows):
    tokens, width = grad.shape
    cols = len(shrink[0])
    wide = shrink[0][0].shape[0]

    def kernel(grad_ref, unit_ref, inverse_ref, slope_ref, norm_ref, *refs):
        dffn_ref, dpre_ref, dhid_ref, sum_ref = refs[4 * cols :]
        place = lax.broadcasted_iota(jnp.int32, (rows, 1), 0)
        upstream = jnp.where(place % SEG == 0, 0.0, grad_ref[...])
        unit = unit_ref[...]

        def put(c, value):
            dpre_ref[:, c * wide : (c + 1) * wide] = value

        dffn, dsecond, back = ffn_backward_values(
            upstream,
            unit,
            inverse_ref[...],
            lambda c: slope_ref[:, c * wide : (c + 1) * wide],
            norm_ref[2:3],
            refs[: 2 * cols],
            refs[2 * cols : 4 * cols],
            cols,
            put,
        )
        dffn_ref[...] = dffn
        dhid_ref[...] = dsecond + back
        put_sums(sum_ref, column_sum(upstream * unit), column_sum(upstream), width)

    ins = [grad, unit, inverse, slope, norms] + flat(shrink) + flat(expand)
    return run(
        kernel,
        (tokens // rows,),
        ins,
        [tile(rows, width), tile(rows, width), tile(rows, 1), tile(rows, cols * wide)]
        + [whole_spec(x) for x in ins[4:]],
        [
            shape(tokens, width),
            shape(tokens, cols * wide),
            shape(tokens, width, kind=jnp.float32),
            shape(tokens // rows, 8, width, kind=jnp.float32),
        ],
        [
            tile(rows, width),
            tile(rows, cols * wide),
            tile(rows, width),
            pl.BlockSpec((1, 8, width), lambda i: (i, 0, 0)),
        ],
        4 * tokens * width * cols * wide,
    )


def ffn_backward_firsts(grad, dheads, unit, inverse, slope, shrink, expand, norms, outs):
    tokens, width = grad.shape
    segs = tokens // SEG
    few = 16
    cols = len(shrink[0])
    wide = shrink[0][0].shape[0]
    by_seg = [x.reshape(segs, SEG, -1) for x in (grad, unit, inverse, slope)]
    outs = [x.reshape(segs, SEG, -1) for x in outs]
    upstream = jnp.concatenate([dheads[:, None], by_seg[0][:, 1:few]], axis=1)

    def kernel(up_ref, unit_ref, inverse_ref, slope_ref, norm_ref, *refs):
        dffn_ref, dpre_ref, dhid_ref, sum_ref = refs[4 * cols + 3 :]
        count = segs * few
        upstream = up_ref[...].reshape(count, width)
        unit = unit_ref[...].reshape(count, width)

        def put(c, value):
            dpre_ref[:, :, c * wide : (c + 1) * wide] = value.reshape(segs, few, wide)

        dffn, dsecond, back = ffn_backward_values(
            upstream,
            unit,
            inverse_ref[...].reshape(count, 1),
            lambda c: slope_ref[:, :, c * wide : (c + 1) * wide].reshape(count, wide),
            norm_ref[2:3],
            refs[: 2 * cols],
            refs[2 * cols : 4 * cols],
            cols,
            put,
        )
        dffn_ref[...] = dffn.reshape(segs, few, width)
        dhid_ref[...] = (dsecond + back).reshape(segs, few, width)
        place = lax.broadcasted_iota(jnp.int32, (count, 1), 0)
        only = jnp.where(place % few == 0, upstream, 0.0)
        put_sums(sum_ref, column_sum(only * unit), column_sum(only), width)

    ins = [upstream] + by_seg[1:] + [norms] + flat(shrink) + flat(expand) + outs
    front = [
        pl.BlockSpec((segs, few, x.shape[2]), lambda i: (0, 0, 0)) for x in [upstream] + by_seg[1:]
    ]
    back_specs = [pl.BlockSpec((segs, few, x.shape[2]), lambda i: (0, 0, 0)) for x in outs]
    first_out = len(ins) - 3
    dffn, dpre, dhid, sums = run(
        kernel,
        (1,),
        ins,
        front
        + [whole_spec(x) for x in ins[4:first_out]]
        + [pl.BlockSpec(memory_space=pl.ANY)] * 3,
        [shape(*x.shape, kind=x.dtype) for x in outs] + [shape(1, 8, width, kind=jnp.float32)],
        back_specs + [pl.BlockSpec((1, 8, width), lambda i: (0, 0, 0))],
        4 * segs * few * width * cols * wide,
        {first_out + k: k for k in range(3)},
    )
    return [x.reshape(tokens, -1) for x in (dffn, dpre, dhid)] + [sums]


def attention_backward(dhid, unit, inverse, qkv, keep, project, merge, norms, group, rows, whole):
    tokens, width = dhid.shape
    cols = len(project[0])
    wide = project[0][0].shape[1]
    heads = wide // (3 * HDIM)

    def kernel(dhid_ref, unit_ref, inverse_ref, qkv_ref, keep_ref, norm_ref, *refs):
        project_refs, merge_refs = refs[: 2 * cols], refs[2 * cols : 4 * cols]
        datt_ref, dqkv_ref, dx_ref, sum_ref = refs[4 * cols : 4 * cols + 4]
        upstream = dhid_ref[...]
        unit = unit_ref[...]
        dfirst = kernel_norm_backward(upstream, unit, inverse_ref[...], norm_ref[0:1])
        put_sums(sum_ref, column_sum(upstream * unit), column_sum(upstream), width)
        datt = dfirst.astype(low_type)
        datt_ref[...] = datt
        back = dfirst if whole else None
        if not whole:
            refs[-1][...] = dfirst
        for c in range(cols):
            dmixed = dot_t(datt, across(merge_refs, cols)(c)).astype(low_type)
            blocks = []
            for g in range(rows // group):
                span = slice(g * group, (g + 1) * group)
                allowed = keep_ref[:, span] > 0.5
                parts = [head_parts(qkv_ref[c, span], head) for head in range(heads)]
                incoming = [
                    dmixed[span, head * HDIM : (head + 1) * HDIM] for head in range(heads)
                ]
                dprobs = [dot_t(some, part[2]) for some, part in zip(incoming, parts)]
                probs = softmax([part[:2] for part in parts], allowed)
                centres = [
                    jnp.sum(left * right, axis=1, keepdims=True)
                    for left, right in zip(dprobs, probs)
                ]
                dscores = [
                    (some * (left - centre)).astype(low_type)
                    for some, left, centre in zip(probs, dprobs, centres)
                ]
                pieces = []
                for some, dscore, up, part in zip(probs, dscores, incoming, parts):
                    pieces.append(dot(dscore, part[1]) * HDIM ** (-0.5))
                    pieces.append(dot_rows(dscore, part[0]) * HDIM ** (-0.5))
                    pieces.append(dot_rows(some.astype(low_type), up))
                blocks.append(jnp.concatenate(pieces, axis=1).astype(low_type))
            dqkv = blocks[0] if len(blocks) == 1 else jnp.concatenate(blocks, axis=0)
            dqkv_ref[c] = dqkv
            part = dot_t(dqkv, down(project_refs, cols)(c))
            back = part if back is None else back + part
        dx_ref[...] = back

    ins = [dhid, unit, inverse, qkv, keep, norms] + flat(project) + flat(merge)
    outs = [
        shape(tokens, width),
        shape(cols, tokens, wide),
        shape(tokens, width, kind=jnp.float32),
        shape(tokens // rows, 8, width, kind=jnp.float32),
    ]
    out_specs = [
        tile(rows, width),
        stack_tile(cols, rows, wide),
        tile(rows, width),
        pl.BlockSpec((1, 8, width), lambda i: (i, 0, 0)),
    ]
    if not whole:
        outs.append(shape(tokens, width, kind=jnp.float32))
        out_specs.append(tile(rows, width))
    return run(
        kernel,
        (tokens // rows,),
        ins,
        [
            tile(rows, width),
            tile(rows, width),
            tile(rows, 1),
            stack_tile(cols, rows, wide),
            pl.BlockSpec((1, rows), lambda i: (0, i)),
        ]
        + [whole_spec(x) for x in ins[5:]],
        outs,
        out_specs,
        2 * tokens * width * cols * wide + 10 * tokens * group * cols * heads * HDIM,
    )


def outer_middle(value, attended, expand, shrink, norms):
    tokens, width = value.shape
    cols = len(expand[0])
    wide = expand[0][0].shape[1]

    def kernel(value_ref, attended_ref, norm_ref, *refs):
        unit_ref, inverse_ref, low_ref, active_ref, slope_ref, ffn_ref = refs[4 * cols :]
        hid, unit, inverse = kernel_norm(
            value_ref[...] + attended_ref[...], norm_ref[0:1], norm_ref[1:2]
        )
        low = hid.astype(low_type)
        unit_ref[...] = unit
        inverse_ref[...] = inverse
        low_ref[...] = low
        for c in range(cols):
            span = slice(c * wide, (c + 1) * wide)
            active_ref[:, span], slope_ref[:, span] = gelu_and_slope(
                dot(low, down(refs[: 2 * cols], cols)(c))
            )
        ffn_ref[...] = shrink_values(active_ref[...], refs[2 * cols : 4 * cols], cols)

    ins = [value, attended, norms] + flat(expand) + flat(shrink)
    outs = [
        shape(tokens, width, kind=jnp.float32),
        shape(tokens, 1, kind=jnp.float32),
        shape(tokens, width),
        shape(tokens, cols * wide),
        shape(tokens, cols * wide),
        shape(tokens, width, kind=jnp.float32),
    ]
    return run(
        kernel,
        (1,),
        ins,
        [whole_spec(x) for x in ins],
        outs,
        [whole_spec(x) for x in outs],
        4 * tokens * width * cols * wide,
    )


def outer_turn(unit, ffn, grad, slope, shrink, expand, norms):
    tokens, width = unit.shape
    cols = len(expand[0])
    wide = expand[0][0].shape[1]

    def kernel(unit_ref, ffn_ref, grad_ref, slope_ref, norm_ref, *refs):
        out_ref, dffn_ref, dpre_ref, dsecond_ref, back_ref, sum_ref = refs[4 * cols :]
        hid = unit_ref[...] * norm_ref[0:1] + norm_ref[1:2]
        result, second, inverse = kernel_norm(hid + ffn_ref[...], norm_ref[2:3], norm_ref[3:4])
        out_ref[...] = result
        upstream = grad_ref[...]

        def put(c, value):
            dpre_ref[:, c * wide : (c + 1) * wide] = value

        dffn_ref[...], dsecond_ref[...], back_ref[...] = ffn_backward_values(
            upstream,
            second,
            inverse,
            lambda c: slope_ref[:, c * wide : (c + 1) * wide],
            norm_ref[2:3],
            refs[: 2 * cols],
            refs[2 * cols : 4 * cols],
            cols,
            put,
        )
        put_sums(sum_ref, column_sum(upstream * second), column_sum(upstream), width)

    ins = [unit, ffn, grad, slope, norms] + flat(shrink) + flat(expand)
    outs = [
        shape(tokens, width, kind=jnp.float32),
        shape(tokens, width),
        shape(tokens, cols * wide),
        shape(tokens, width, kind=jnp.float32),
        shape(tokens, width, kind=jnp.float32),
        shape(1, 8, width, kind=jnp.float32),
    ]
    return run(
        kernel,
        (1,),
        ins,
        [whole_spec(x) for x in ins],
        outs,
        [whole_spec(x) for x in outs],
        4 * tokens * width * cols * wide,
    )


def ffn_grads(hid_low, dpre, active, dffn):
    dp_count, col_count = lax.axis_size("dp"), lax.axis_size("col")
    half = hid_low.shape[1] // 2
    theirs_first = dot_rows(hid_low[:, half:], dpre).astype(low_type)
    theirs_second = dot_rows(active, dffn[:, half:]).astype(low_type)
    mine_first = dot_rows(hid_low[:, :half], dpre).astype(low_type)
    mine_second = dot_rows(active, dffn[:, :half]).astype(low_type)
    wide = mine_first.shape[1] // col_count
    tall = mine_second.shape[0] // col_count
    low, high = half // dp_count, tall // dp_count
    got_first, got_second = row_swap(theirs_first), row_swap(theirs_second)

    def kernel(*refs):
        ins, outs = refs[:8], refs[8:]
        for k in range(2):
            first = add_low(ins[2 * k][...], ins[2 * k + 1][...])
            second = add_low(ins[4 + 2 * k][...], ins[5 + 2 * k][...])
            for place in range(dp_count):
                part = first[place * low : (place + 1) * low]
                outs[k][0, place, :low] = part[:, :half]
                outs[k][0, place, low:] = part[:, half:]
                outs[2 + k][0, place] = second[place * high : (place + 1) * high]

    specs = (
        [pl.BlockSpec((half, wide), lambda i: (0, 2 * i))] * 2
        + [pl.BlockSpec((half, wide), lambda i: (0, 2 * i + 1))] * 2
        + [pl.BlockSpec((tall, half), lambda i: (i, 0))] * 2
        + [pl.BlockSpec((tall, half), lambda i: (i + 2, 0))] * 2
    )
    return pack_call(
        kernel,
        [mine_first, got_first] * 2 + [mine_second, got_second] * 2,
        specs,
        dp_count,
        (2 * low, high),
        half,
    )


def add_low(left, right):
    return (left.astype(jnp.float32) + right.astype(jnp.float32)).astype(low_type)


def pack_call(kernel, ins, specs, dp_count, heights, width):
    heights = [heights[0], heights[0], heights[1], heights[1]]
    return run(
        kernel,
        (2,),
        ins,
        specs,
        [shape(2, dp_count, height, width) for height in heights],
        [
            pl.BlockSpec((1, dp_count, height, width), lambda i: (i, 0, 0, 0))
            for height in heights
        ],
        0,
    )


def first_swaps(packed):
    keep_a, send_a, keep_b, send_b = packed
    got_a, got_b = col_swap(send_a, 1), col_swap(send_b, 2)

    def kernel(*refs):
        for half in range(2):
            total = add_low(refs[2 * half][...], refs[2 * half + 1][...])
            refs[4 + 2 * half][...] = total[0]
            refs[5 + 2 * half][...] = total[1]

    ins = [keep_a, got_a, keep_b, got_b]
    outs = [shape(*x.shape[1:]) for x in (keep_a, keep_a, keep_b, keep_b)]

    def spec(array):
        front = array.ndim - 3
        return pl.BlockSpec(
            (2,) * front + (1,) + array.shape[front + 1 :],
            lambda i: (0,) * front + (i, 0, 0),
        )

    return run(
        kernel, (keep_a.shape[1],), ins, [spec(x) for x in ins], outs, [spec(x) for x in outs], 0
    )


def second_swaps(sums):
    own_a, on_a, own_b, on_b = sums
    got_a, got_b = col_swap(on_a, 2), col_swap(on_b, 1)
    count, high_a, width = own_a.shape
    high_b = own_b.shape[1]

    def kernel(place_ref, *refs):
        for step in range(count):
            at = lax.rem(place_ref[0] + step, count)
            refs[4 + step][:high_a] = add_low(refs[0][at], refs[1][at])
            refs[4 + step][high_a:] = add_low(refs[2][at], refs[3][at])

    ins = [own_a, got_a, own_b, got_b]
    whole = pl.BlockSpec(memory_space=pltpu.VMEM)
    return pl.pallas_call(
        kernel,
        out_shape=[jax.ShapeDtypeStruct((high_a + high_b, width), low_type)] * count,
        grid_spec=pltpu.PrefetchScalarGridSpec(
            num_scalar_prefetch=1, grid=(), in_specs=[whole] * 4, out_specs=[whole] * count
        ),
        cost_estimate=pl.CostEstimate(
            flops=0, bytes_accessed=6 * count * (high_a + high_b) * width, transcendentals=0
        ),
        name="add_second",
    )(lax.axis_index("dp").reshape(1), *ins)


def rows_over(value):
    return col_swap(value, 2)


def dp_swaps(pieces):
    got = [dp_shift(piece, step) for step, piece in enumerate(pieces) if step]
    total = pieces[0].astype(jnp.float32)
    for piece in got:
        total = total + piece.astype(jnp.float32)
    return total


def row_products(left, right, part):
    cols, tokens, wide = right.shape
    half = left.shape[1] // 2

    def kernel(left_ref, right_ref, out_ref):
        out_ref[0] = dot_rows(left_ref[...], right_ref[0]).astype(low_type)

    return run(
        kernel,
        (cols,),
        [left, right],
        [
            pl.BlockSpec((tokens, half), lambda c: (0, part)),
            pl.BlockSpec((1, tokens, wide), lambda c: (c, 0, 0)),
        ],
        [shape(cols, half, wide)],
        [pl.BlockSpec((1, half, wide), lambda c: (c, 0, 0))],
        2 * tokens * half * cols * wide,
    )[0]


def attention_grads(x_low, dqkv, mixed, datt, ready):
    dp_count, col_count = lax.axis_size("dp"), lax.axis_size("col")
    half = x_low.shape[1] // 2
    wide = dqkv.shape[2]
    theirs_second = dot_rows(mixed, datt[:, half:]).astype(low_type)
    theirs_first = row_products(x_low, dqkv, 1)
    x_low, mixed = after((x_low, mixed), ready)
    mine_first = row_products(x_low, dqkv, 0)
    mine_second = dot_rows(mixed, datt[:, :half]).astype(low_type)
    got_first, got_second = row_swap(theirs_first), row_swap(theirs_second)
    tall = mine_second.shape[0] // col_count
    low, high = half // dp_count, tall // dp_count
    end_rows = low // 2
    assert (wide - half) * 2 == half

    def kernel(*refs):
        ins, outs = refs[:12], refs[12:]
        for k in range(2):
            first = add_low(ins[2 * k][0, :, :half], ins[2 * k + 1][0, :, :half])
            other = ins[4 + 2 * k][0, :, half:].astype(jnp.float32)
            other = other + ins[5 + 2 * k][0, :, half:].astype(jnp.float32)
            second = add_low(ins[8 + 2 * k][...], ins[9 + 2 * k][...])
            for place in range(dp_count):
                outs[k][0, place] = first[place * low : (place + 1) * low]
                ends = other[place * low : (place + 1) * low]
                outs[2 + k][0, place, :end_rows] = jnp.concatenate(
                    [ends[:end_rows], ends[end_rows:]], axis=1
                ).astype(low_type)
                outs[2 + k][0, place, end_rows:] = second[place * high : (place + 1) * high]

    def blocks(index):
        return [pl.BlockSpec((1, half, wide), lambda i: (index(i), 0, 0))] * 2

    specs = (
        blocks(lambda i: 2 * i)
        + blocks(lambda i: 2 * i + 1)
        + blocks(lambda i: i)
        + blocks(lambda i: i + 2)
        + [pl.BlockSpec((tall, half), lambda i: (i, 0))] * 2
        + [pl.BlockSpec((tall, half), lambda i: (i + 2, 0))] * 2
    )
    return pack_call(
        kernel,
        [mine_first, got_first] * 4 + [mine_second, got_second] * 2,
        specs,
        dp_count,
        (low, end_rows + high),
        half,
    )


def unpack_ffn(packed, low):
    return jnp.concatenate([packed[:low], packed[low : 2 * low]], axis=1), packed[2 * low :]


def unpack_attention(packed, low):
    half = packed.shape[1] // 2
    ends = packed[low : low + low // 2]
    ends = jnp.concatenate([ends[:, :half], ends[:, half:]], axis=0)
    return jnp.concatenate([packed[:low], ends], axis=1), packed[low + low // 2 :]


def halves(value, axis):
    return jnp.split(value, 2, axis=axis)


def first_grad(left, right, through):
    mine_left, theirs_left = halves(left, 1)
    theirs = [dot_rows(theirs_left, block).astype(low_type) for block in right]
    mine = [dot_rows(mine_left, block).astype(low_type) for block in right]
    return scatter_grad(mine, theirs, through)


def second_grad(left, right, through):
    mine_right, theirs_right = halves(right, 1)
    count = lax.axis_size("col")
    theirs = dot_rows(left, theirs_right).astype(low_type)
    mine = dot_rows(left, mine_right).astype(low_type)
    got = row_swap(theirs)
    total = mine.astype(jnp.float32) + got.astype(jnp.float32)
    return dp_scatter_sum(plane_sum(jnp.split(total, count, 0), through))


def to_tokens(value, row):
    parts = value.reshape((2, -1) + value.shape[1:])
    mine = lax.dynamic_index_in_dim(parts, row, 0, False)
    theirs = lax.dynamic_index_in_dim(parts, 1 - row, 0, False)
    return jnp.concatenate([mine, row_swap(theirs)], axis=1)


def to_features(value, row):
    mine, theirs = halves(value, 1)
    got = row_swap(theirs)
    first = jnp.where(row == 0, mine, got)
    second = jnp.where(row == 0, got, mine)
    return jnp.concatenate([first, second], axis=0)


def swap_features(value):
    first, second = halves(value, 1)
    return jnp.concatenate([second, first], axis=1)


def swap_rows(value):
    first, second = halves(value, 0)
    return jnp.concatenate([second, first], axis=0)


def layer(
    hidden,
    lengths,
    inner_project,
    inner_merge,
    inner_expand,
    inner_shrink,
    inner_norms,
    outer_places,
    outer_project,
    outer_merge,
    outer_expand,
    outer_shrink,
    outer_norms,
    out_grad,
):
    dp_count, row_count, col_count = (lax.axis_size(name) for name in ("dp", "row", "col"))
    dp, row, col = (lax.axis_index(name) for name in ("dp", "row", "col"))
    everyone = ("dp", "row", "col")
    device_count = dp_count * row_count * col_count
    value = to_tokens(hidden, row)
    grad_in = to_tokens(out_grad, row)
    tokens, width = value.shape
    segs = tokens // SEG

    small = jnp.concatenate([inner_norms, outer_norms, outer_places], axis=1)
    small = lax.all_to_all(
        jnp.broadcast_to(small[None], (device_count,) + small.shape), everyone, 0, 0, tiled=True
    )
    small_got = small
    small = small.reshape((dp_count, row_count, -1) + small.shape[2:])
    small = jnp.concatenate(
        [
            lax.dynamic_index_in_dim(small, row, 1, False).reshape(-1, small.shape[-1]),
            lax.dynamic_index_in_dim(small, 1 - row, 1, False).reshape(-1, small.shape[-1]),
        ],
        axis=0,
    )
    vectors = small.T
    inner_gains = vectors[0:4]
    outer_gains = vectors[4:8]
    places = vectors[8:]

    length = lax.dynamic_index_in_dim(lengths, col // 2, 0, False)
    half = col % 2
    seg_own = (half * 2 + row) * segs + jnp.arange(segs, dtype=jnp.int32)
    spot = (seg_own[:, None] * SEG + jnp.arange(SEG, dtype=jnp.int32)[None]).reshape(tokens)
    valid = (spot < length).astype(jnp.float32)
    keep_tok = ((spot < length) | (spot % SEG == 0)).astype(jnp.float32)
    seg_all = jnp.concatenate(
        [
            (h * 2 + r) * segs + jnp.arange(segs, dtype=jnp.int32)
            for h in (half, 1 - half)
            for r in (row, 1 - row)
        ]
    )
    keep_seg = (seg_all * SEG < length).astype(jnp.float32)
    one_hot = (seg_own[:, None] == jnp.arange(NSEG, dtype=jnp.int32)[None]).astype(jnp.float32)

    keep_row = keep_tok[None]
    rows_tile = 2 * SEG
    inner, outer_steps, (x_in, qkv, mixed_in) = gather_weights(
        (inner_project, inner_merge, inner_expand, inner_shrink),
        (outer_project, outer_merge, outer_expand, outer_shrink),
        lambda project: project_attend(value, keep_row, project, None, SEG, rows_tile),
        small_got,
    )
    unit_one, inverse_one, hid_in, active_in, slope = merge_expand(
        value, mixed_in, inner[1], inner[2], inner_gains, rows_tile
    )
    outer_project = outer_steps[0](hid_in)
    inner_out, unit_two, inverse_two = shrink_norm(
        unit_one, active_in, inner[3], inner_gains, rows_tile
    )
    outer_merge, outer_shrink = outer_steps[1](inner_out)
    grid = inner_out.reshape(segs, SEG, width)
    masked_grad = (grad_in * valid[:, None]).reshape(segs, SEG, width)
    heads_in = grid[:, 0] + jnp.dot(
        one_hot, places, precision=highest, preferred_element_type=jnp.float32
    )
    rows = jnp.concatenate([heads_in, masked_grad[:, 0]], axis=0)
    rows = jnp.stack([rows, swap_features(row_swap(rows))]).reshape(2, 2, segs, width)
    rows = jnp.stack([rows, col_swap(rows, 1)])
    rows = rows.transpose(2, 0, 1, 3, 4).reshape(2, NSEG, width)

    def join(partial_sum):
        return partial_sum + swap_rows(col_swap(partial_sum, 1))

    flat_grad = masked_grad.reshape(tokens, width)
    main = ffn_backward(
        flat_grad, unit_two, inverse_two, slope, inner[3], inner[2], inner_gains, rows_tile
    )
    outer_expand = outer_steps[2](main[3])
    outer = (outer_project, outer_merge, outer_expand, outer_shrink)
    rows = after(rows, main[3])
    x_low, o_qkv, mixed, attended = project_attend(
        rows[0], keep_seg[None], outer[0], outer[1], NSEG, NSEG
    )
    o_unit, o_inverse, hid_low, active, o_slope, ffn = outer_middle(
        rows[0], join(attended), outer[2], outer[3], outer_gains
    )
    outer_out, dffn, dpre, dsecond, back, o_second = outer_turn(
        o_unit, join(ffn), rows[1], o_slope, outer[3], outer[2], outer_gains
    )
    datt, dqkv, back, o_first, dfirst = attention_backward(
        dsecond + join(back),
        o_unit,
        o_inverse,
        o_qkv,
        keep_seg[None],
        outer[0],
        outer[1],
        outer_gains,
        NSEG,
        NSEG,
        False,
    )
    dheads = dfirst + join(back)
    outer_norm_grad = jnp.concatenate([o_first[0, :2], o_second[0, :2]], axis=0).T
    dheads = dheads[:segs]
    places_grad = jnp.dot(dheads.T, one_hot, precision=highest, preferred_element_type=jnp.float32)

    dffn_in, dpre_in, dhid_in, few_sums = ffn_backward_firsts(
        flat_grad,
        dheads,
        unit_two,
        inverse_two,
        slope,
        inner[3],
        inner[2],
        inner_gains,
        main[:3],
    )
    wide_dp = dp_count > 4
    if not wide_dp:
        ffn_packed = ffn_grads(hid_in, dpre_in, active_in, dffn_in)
        dhid_in = after(dhid_in, ffn_packed[0])
    datt_in, dqkv_in, input_grad, first_sums = attention_backward(
        dhid_in,
        unit_one,
        inverse_one,
        qkv,
        keep_row,
        inner[0],
        inner[1],
        inner_gains,
        SEG,
        rows_tile,
        True,
    )
    if wide_dp:
        inner_grads = (
            first_grad(x_in, dqkv_in, 1),
            second_grad(mixed_in, datt_in, 2),
            first_grad(hid_in, jnp.split(dpre_in, col_count, 1), 1),
            second_grad(active_in, dffn_in, 2),
        )
        gate = None
    else:
        ffn_sums = first_swaps(ffn_packed)
        attention_packed = attention_grads(x_in, dqkv_in, mixed_in, datt_in, ffn_sums[0])
        ffn_pieces = second_swaps(ffn_sums)
        gate = attention_packed[0]
    shared = [halves(part, 1)[0] for part in (x_low, hid_low, datt, dffn)]
    own, over = zip(*([halves(part, 1) for part in (active, dpre, mixed)] + [tuple(dqkv)]))
    packed = jnp.concatenate(
        [
            jnp.concatenate(shared + list(own), axis=1),
            rows_over(jnp.concatenate(shared + list(over), axis=1)),
        ],
        axis=0,
    )
    if dp_count > 4:
        packed = lax.all_gather(packed, "dp", axis=0, tiled=True)
    else:
        got = [dp_shift(packed, step) for step in range(1, dp_count)]
        packed = jnp.concatenate([packed] + got, axis=0)
    late = (outer_out, grid, first_sums, main[3])
    if gate is not None:
        late = after(late, gate)
    late_outer, late_inner, late_first, late_main = late
    layer_out = (
        jnp.concatenate([late_outer[:segs, None], late_inner[:, 1:]], axis=1).reshape(tokens, width)
        * valid[:, None]
    )
    inner_norm_grad = jnp.concatenate(
        [jnp.sum(late_first, 0)[:2], jnp.sum(late_main, 0)[:2] + few_sums[0, :2]], axis=0
    ).T
    small_grad = jnp.concatenate([inner_norm_grad, 0.25 * outer_norm_grad, places_grad], axis=1)
    if gate is not None:
        small_grad = after(small_grad, gate)
    columns = small_grad.shape[1]
    blocks = small_grad.reshape(2, dp_count, col_count, -1, columns)
    blocks = jnp.where(row == 0, blocks, blocks[::-1]).transpose(1, 0, 2, 3, 4)
    blocks = lax.all_to_all(
        blocks.reshape(device_count, -1, columns), everyone, 0, 0, tiled=True
    )
    small_sum = jnp.sum(blocks, axis=0)
    if not wide_dp:
        attention_sums = first_swaps(attention_packed)
        ffn_total = dp_swaps(after(ffn_pieces, small_sum))
        attention_pieces = second_swaps(after(attention_sums, small_sum))
        attention_total = dp_swaps(attention_pieces)
        inner_grads = unpack_attention(attention_total, inner_expand.shape[0]) + unpack_ffn(
            ffn_total, inner_expand.shape[0]
        )
    ends = []
    for part in shared + list(own):
        ends.append((ends[-1] if ends else 0) + part.shape[1])
    x_all, hid_all, datt_all, dffn_all, active_all, dpre_all, mixed_all, dqkv_all = jnp.split(
        packed, ends[:-1], axis=1
    )

    def own_rows(product):
        return lax.dynamic_index_in_dim(
            product.reshape((dp_count, -1) + product.shape[1:]), dp, 0, False
        )

    outer_grads = (
        own_rows(dot_rows(x_all, dqkv_all)),
        own_rows(dot_rows(mixed_all, datt_all)),
        own_rows(dot_rows(hid_all, dpre_all)),
        own_rows(dot_rows(active_all, dffn_all)),
    )

    return (
        to_features(layer_out, row),
        to_features(input_grad, row),
        inner_grads[0],
        inner_grads[1],
        inner_grads[2],
        inner_grads[3],
        small_sum[:, 0:4],
        small_sum[:, 8:],
        outer_grads[0],
        outer_grads[1],
        outer_grads[2],
        outer_grads[3],
        small_sum[:, 4:8],
    )


def solution(mesh):
    tokens = P(("dp", "col"), "row")
    first = P(("row", "dp"), "col")
    second = P(("col", "dp"), "row")
    small = P(("row", "dp", "col"), None)
    weights = (first, second, first, second)
    return jax.shard_map(
        layer,
        mesh=mesh,
        in_specs=(tokens, P("dp")) + weights + (small, small) + weights + (small, tokens),
        out_specs=(tokens, tokens) + weights + (small, small) + weights + (small,),
        check_vma=False,
    )
```

```python
import jax
import jax.numpy as jnp
from jax import lax
from jax.experimental import pallas as pl
from jax.experimental.pallas import tpu as pltpu
from jax.sharding import PartitionSpec as P


HDIM = 64
SEG = 128
NSEG = 16
epsilon = 1e-06
highest = lax.Precision.HIGHEST
low_type = jnp.bfloat16


def dot(left, right):
    return jnp.dot(left, right, preferred_element_type=jnp.float32)


def dot_t(left, right):
    return lax.dot_general(
        left, right, (((1,), (1,)), ((), ())), preferred_element_type=jnp.float32
    )


def dot_rows(left, right):
    return lax.dot_general(
        left, right, (((0,), (0,)), ((), ())), preferred_element_type=jnp.float32
    )


def row_swap(value):
    return lax.ppermute(value, "row", [(0, 1), (1, 0)])


def col_swap(value, mask):
    return lax.ppermute(value, "col", [(i, i ^ mask) for i in range(lax.axis_size("col"))])


def dp_shift(value, step):
    count = lax.axis_size("dp")
    return lax.ppermute(value, "dp", [(i, (i + step) % count) for i in range(count)])


def after(value, earlier):
    return lax.optimization_barrier((value, earlier))[0]


def dp_pieces(value):
    count = lax.axis_size("dp")
    return [value] + [dp_shift(value, step) for step in range(1, count)]


def place_pieces(pieces, cut=None):
    count = len(pieces)
    height, width = pieces[0].shape
    bounds = (0, height) if cut is None else (0, cut, height)
    spans = list(zip(bounds[:-1], bounds[1:]))

    def kernel(place_ref, *refs):
        for step in range(count):
            at = lax.rem(place_ref[0] - step + count, count)
            for (low, high), out in zip(spans, refs[count:]):
                size = high - low
                out[pl.ds(pl.multiple_of(at * size, 16), size), :] = refs[step][low:high]

    whole = pl.BlockSpec(memory_space=pltpu.VMEM)
    outs = [
        jax.ShapeDtypeStruct((count * (high - low), width), pieces[0].dtype) for low, high in spans
    ]
    placed = pl.pallas_call(
        kernel,
        out_shape=outs,
        grid_spec=pltpu.PrefetchScalarGridSpec(
            num_scalar_prefetch=1,
            grid=(),
            in_specs=[whole] * count,
            out_specs=[whole] * len(outs),
        ),
        cost_estimate=pl.CostEstimate(
            flops=0, bytes_accessed=4 * count * height * width, transcendentals=0
        ),
        name="place_pieces",
    )(lax.axis_index("dp").reshape(1), *pieces)
    return placed[0] if cut is None else placed


def dp_scatter_sum(value):
    count = lax.axis_size("dp")
    if count > 4:
        return lax.psum_scatter(value, "dp", scatter_dimension=0, tiled=True)
    place = lax.axis_index("dp")
    parts = value.reshape((count, -1) + value.shape[1:])
    total = lax.dynamic_index_in_dim(parts, place, 0, False)
    for step in range(1, count):
        piece = lax.dynamic_index_in_dim(parts, (place + step) % count, 0, False)
        total = total + dp_shift(piece.astype(low_type), step).astype(jnp.float32)
    return total


def plane_blocks(own, through):
    side = col_swap(own, 1)
    over = col_swap(own, 2)
    far = col_swap(over, 1) if through == 1 else col_swap(side, 2)
    mine = (own, side, over, far)
    return (mine, tuple(row_swap(block) for block in mine))


def pair_blocks(own):
    mine = (own, col_swap(own, 2))
    return (mine, tuple(row_swap(block) for block in mine))


def gather_wide(inner_shards, outer_shards, first_use):
    inner_own, outer_own = (
        [lax.all_gather(shard, "dp", axis=0, tiled=True) for shard in group]
        for group in (inner_shards, outer_shards)
    )
    inner = [plane_blocks(own, through) for own, through in zip(inner_own, (1, 2, 1, 2))]
    outer = [pair_blocks(own) for own in outer_own]
    steps = (lambda gate: outer[0], lambda gate: (outer[1], outer[3]), lambda gate: outer[2])
    return inner, steps, first_use(inner[0])


def gather_weights(inner_shards, outer_shards, first_use, early):
    inner_shards = [shard.astype(low_type) for shard in inner_shards]
    outer_shards = [shard.astype(low_type) for shard in outer_shards]
    if lax.axis_size("dp") > 4:
        return gather_wide(inner_shards, outer_shards, first_use)
    pieces = dp_pieces(inner_shards[0])
    merge_pieces = dp_pieces(inner_shards[1])
    own = place_pieces(pieces)
    expand_pieces = dp_pieces(after(inner_shards[2], own))
    side, over, far_project = (col_swap(own, mask) for mask in (1, 2, 3))
    project = both_rows((own, side, over, far_project))
    own = place_pieces(after(merge_pieces, (side, early)))
    side, over, far_merge = (col_swap(own, mask) for mask in (1, 2, 3))
    merge = both_rows((own, side, over, far_merge))
    own = place_pieces(after(expand_pieces, far_project))
    shrink_pieces = dp_pieces(after(inner_shards[3], expand_pieces))
    side, over, far_expand = (col_swap(own, mask) for mask in (1, 2, 3))
    used = first_use(after(project, own))
    expand = both_rows((own, side, over, far_expand))
    own = place_pieces(after(shrink_pieces, (side, over, used[0])))
    side, over, far = (col_swap(own, mask) for mask in (1, 2, 3))
    shrink = both_rows((own, side, over, far))
    rows = jnp.concatenate([outer_shards[1], outer_shards[3]], axis=0)
    first = dp_pieces(after(outer_shards[0], shrink_pieces))
    second = dp_pieces(after(rows, first[1]))
    third = dp_pieces(after(outer_shards[2], second[1]))

    def outer_project(gate):
        return pair_blocks(place_pieces(after(first, gate)))

    def outer_rows(gate):
        merge, shrink = place_pieces(after(second, gate), outer_shards[1].shape[0])
        return pair_blocks(merge), pair_blocks(shrink)

    def outer_expand(gate):
        own = place_pieces(after(third, gate))
        return pair_blocks(own)

    return (project, merge, expand, shrink), (outer_project, outer_rows, outer_expand), used


def both_rows(mine):
    return (mine, tuple(row_swap(block) for block in mine))


def plane_sum(sums, through):
    other = 3 - through
    own = sums[0] + col_swap(sums[through].astype(low_type), through).astype(jnp.float32)
    onward = sums[other] + col_swap(sums[3].astype(low_type), through).astype(jnp.float32)
    return own + col_swap(onward.astype(low_type), other).astype(jnp.float32)


def scatter_grad(mine, theirs, through):
    sums = [
        block.astype(jnp.float32) + row_swap(sent).astype(jnp.float32)
        for block, sent in zip(mine, theirs)
    ]
    return dp_scatter_sum(plane_sum(sums, through))


def whole_spec(array):
    return pl.BlockSpec(
        array.shape, lambda i: (0,) * array.ndim, pipeline_mode=pl.Buffered(1)
    )


def flat(blocks):
    return [block for half in blocks for block in half]


def grouped(refs, cols):
    return (refs[:cols], refs[cols : 2 * cols])


def down(refs, cols):
    return lambda c: jnp.concatenate([refs[c][...], refs[cols + c][...]], axis=0)


def across(refs, cols):
    return lambda c: jnp.concatenate([refs[c][...], refs[cols + c][...]], axis=1)


def kernel_norm(value, gain, shift):
    average = jnp.mean(value, axis=1, keepdims=True)
    centred = value - average
    inverse = lax.rsqrt(jnp.mean(centred * centred, axis=1, keepdims=True) + epsilon)
    unit = centred * inverse
    return unit * gain + shift, unit, inverse


def kernel_norm_backward(upstream, unit, inverse, gain):
    scaled = upstream * gain
    centre = jnp.mean(scaled, axis=1, keepdims=True)
    slope = jnp.mean(scaled * unit, axis=1, keepdims=True)
    return inverse * (scaled - centre - unit * slope)


def gelu_and_slope(value):
    share = 0.5 + 0.5 * lax.erf(value * 0.7071067811865476)
    density = 0.3989422804014327 * jnp.exp(-0.5 * value * value)
    return (value * share).astype(low_type), (share + value * density).astype(low_type)


def softmax(pairs, allowed):
    scores = [dot_t(query, key_part) * HDIM ** (-0.5) for query, key_part in pairs]
    scores = [jnp.where(allowed, one, -1000000000.0) for one in scores]
    tops = [jnp.max(one, axis=1, keepdims=True) for one in scores]
    expos = [jnp.exp(one - top) for one, top in zip(scores, tops)]
    shares = [1.0 / jnp.sum(expo, axis=1, keepdims=True) for expo in expos]
    return [expo * share for expo, share in zip(expos, shares)]


def head_parts(qkv, head):
    start = head * 3 * HDIM
    return [qkv[:, start + k * HDIM : start + (k + 1) * HDIM] for k in range(3)]


def run(kernel, grid, ins, in_specs, outs, out_specs, flops, aliases=None):
    moved = sum(x.size * x.dtype.itemsize for x in list(ins) + list(outs))
    return pl.pallas_call(
        kernel,
        out_shape=outs,
        grid=grid,
        in_specs=in_specs,
        out_specs=out_specs,
        input_output_aliases=aliases or {},
        cost_estimate=pl.CostEstimate(flops=flops, bytes_accessed=moved, transcendentals=0),
    )(*ins)


def shape(*dims, kind=low_type):
    return jax.ShapeDtypeStruct(dims, kind)


def tile(rows, width):
    return pl.BlockSpec((rows, width), lambda i: (i, 0))


def stack_tile(cols, rows, width):
    return pl.BlockSpec((cols, rows, width), lambda i: (0, i, 0))


def project_attend(value, keep, project, merge, group, rows):
    tokens, width = value.shape
    cols = len(project[0])
    wide = project[0][0].shape[1]
    heads = wide // (3 * HDIM)
    out_width = cols * heads * HDIM
    merge_in = flat(merge) if merge else []

    def kernel(value_ref, keep_ref, *refs):
        weight = down(refs, cols)
        merge_refs = refs[2 * cols : 2 * cols + len(merge_in)]
        low_ref, qkv_ref, mixed_ref = refs[2 * cols + len(merge_in) :][:3]
        low = value_ref[...].astype(low_type)
        low_ref[...] = low
        qkvs = []
        for c in range(cols):
            qkvs.append(dot(low, weight(c)).astype(low_type))
            qkv_ref[c] = qkvs[c]
        for g in range(rows // group):
            span = slice(g * group, (g + 1) * group)
            allowed = keep_ref[:, span] > 0.5
            outs = []
            for c in range(cols):
                parts = [head_parts(qkvs[c][span], head) for head in range(heads)]
                probs = softmax([part[:2] for part in parts], allowed)
                outs += [
                    dot(some.astype(low_type), part[2]) for some, part in zip(probs, parts)
                ]
            mixed_ref[span] = jnp.concatenate(outs, axis=1).astype(low_type)
        if merge_in:
            mixed = mixed_ref[...]
            for r, half in enumerate(grouped(merge_refs, cols)):
                joined = jnp.concatenate([ref[...] for ref in half], axis=0)
                size = joined.shape[1]
                refs[-1][:, r * size : (r + 1) * size] = dot(mixed, joined)

    ins = [value, keep] + flat(project) + merge_in
    outs = [
        shape(tokens, width),
        shape(cols, tokens, wide),
        shape(tokens, out_width),
    ]
    out_specs = [tile(rows, width), stack_tile(cols, rows, wide), tile(rows, out_width)]
    if merge_in:
        outs.append(shape(tokens, width, kind=jnp.float32))
        out_specs.append(tile(rows, width))
    return run(
        kernel,
        (tokens // rows,),
        ins,
        [tile(rows, width), pl.BlockSpec((1, rows), lambda i: (0, i))]
        + [whole_spec(x) for x in ins[2:]],
        outs,
        out_specs,
        2 * tokens * width * cols * wide + 4 * tokens * group * out_width,
    )


def merge_values(mixed, merge_refs, cols):
    parts = [
        dot(mixed, jnp.concatenate([ref[...] for ref in half], axis=0))
        for half in grouped(merge_refs, cols)
    ]
    return jnp.concatenate(parts, axis=1)


def merge_expand(value, mixed, merge, expand, norms, rows):
    tokens, width = value.shape
    cols = len(expand[0])
    wide = expand[0][0].shape[1]

    def kernel(value_ref, mixed_ref, norm_ref, *refs):
        merge_refs, expand_refs = refs[: 2 * cols], refs[2 * cols : 4 * cols]
        unit_ref, inverse_ref, low_ref, active_ref, slope_ref = refs[4 * cols :]
        attended = merge_values(mixed_ref[...], merge_refs, cols)
        hid, unit, inverse = kernel_norm(
            value_ref[...] + attended, norm_ref[0:1], norm_ref[1:2]
        )
        low = hid.astype(low_type)
        unit_ref[...] = unit
        inverse_ref[...] = inverse
        low_ref[...] = low
        weight = down(expand_refs, cols)
        for c in range(cols):
            span = slice(c * wide, (c + 1) * wide)
            active_ref[:, span], slope_ref[:, span] = gelu_and_slope(dot(low, weight(c)))

    ins = [value, mixed, norms] + flat(merge) + flat(expand)
    return run(
        kernel,
        (tokens // rows,),
        ins,
        [tile(rows, width), tile(rows, width)] + [whole_spec(x) for x in ins[2:]],
        [
            shape(tokens, width, kind=jnp.float32),
            shape(tokens, 1, kind=jnp.float32),
            shape(tokens, width),
            shape(tokens, cols * wide),
            shape(tokens, cols * wide),
        ],
        [tile(rows, width), tile(rows, 1), tile(rows, width)] + [tile(rows, cols * wide)] * 2,
        2 * tokens * width * (width + cols * wide),
    )


def shrink_values(active, shrink_refs, cols):
    parts = [
        dot(active, jnp.concatenate([ref[...] for ref in half], axis=0))
        for half in grouped(shrink_refs, cols)
    ]
    return jnp.concatenate(parts, axis=1)


def shrink_norm(unit, active, shrink, norms, rows):
    tokens, width = unit.shape
    cols = len(shrink[0])

    def kernel(unit_ref, active_ref, norm_ref, *refs):
        out_ref, second_ref, inverse_ref = refs[2 * cols :]
        hid = unit_ref[...] * norm_ref[0:1] + norm_ref[1:2]
        ffn = shrink_values(active_ref[...], refs[: 2 * cols], cols)
        out_ref[...], second_ref[...], inverse_ref[...] = kernel_norm(
            hid + ffn, norm_ref[2:3], norm_ref[3:4]
        )

    ins = [unit, active, norms] + flat(shrink)
    return run(
        kernel,
        (tokens // rows,),
        ins,
        [tile(rows, width), tile(rows, active.shape[1])] + [whole_spec(x) for x in ins[2:]],
        [
            shape(tokens, width, kind=jnp.float32),
            shape(tokens, width, kind=jnp.float32),
            shape(tokens, 1, kind=jnp.float32),
        ],
        [tile(rows, width), tile(rows, width), tile(rows, 1)],
        2 * tokens * width * active.shape[1],
    )


def ffn_backward_values(upstream, unit, inverse, slope, gain, shrink_refs, expand_refs, cols, put):
    dsecond = kernel_norm_backward(upstream, unit, inverse, gain)
    dffn = dsecond.astype(low_type)
    back = None
    for c in range(cols):
        dactive = dot_t(dffn, across(shrink_refs, cols)(c))
        dpre = (dactive * slope(c).astype(jnp.float32)).astype(low_type)
        put(c, dpre)
        part = dot_t(dpre, down(expand_refs, cols)(c))
        back = part if back is None else back + part
    return dffn, dsecond, back


def put_sums(ref, first, second, width):
    ref[0] = jnp.concatenate([first, second, jnp.zeros((6, width), jnp.float32)], axis=0)


def column_sum(value):
    return jnp.sum(value, axis=0, keepdims=True)


def ffn_backward(grad, unit, inverse, slope, shrink, expand, norms, rows):
    tokens, width = grad.shape
    cols = len(shrink[0])
    wide = shrink[0][0].shape[0]

    def kernel(grad_ref, unit_ref, inverse_ref, slope_ref, norm_ref, *refs):
        dffn_ref, dpre_ref, dhid_ref, sum_ref = refs[4 * cols :]
        place = lax.broadcasted_iota(jnp.int32, (rows, 1), 0)
        upstream = jnp.where(place % SEG == 0, 0.0, grad_ref[...])
        unit = unit_ref[...]

        def put(c, value):
            dpre_ref[:, c * wide : (c + 1) * wide] = value

        dffn, dsecond, back = ffn_backward_values(
            upstream,
            unit,
            inverse_ref[...],
            lambda c: slope_ref[:, c * wide : (c + 1) * wide],
            norm_ref[2:3],
            refs[: 2 * cols],
            refs[2 * cols : 4 * cols],
            cols,
            put,
        )
        dffn_ref[...] = dffn
        dhid_ref[...] = dsecond + back
        put_sums(sum_ref, column_sum(upstream * unit), column_sum(upstream), width)

    ins = [grad, unit, inverse, slope, norms] + flat(shrink) + flat(expand)
    return run(
        kernel,
        (tokens // rows,),
        ins,
        [tile(rows, width), tile(rows, width), tile(rows, 1), tile(rows, cols * wide)]
        + [whole_spec(x) for x in ins[4:]],
        [
            shape(tokens, width),
            shape(tokens, cols * wide),
            shape(tokens, width, kind=jnp.float32),
            shape(tokens // rows, 8, width, kind=jnp.float32),
        ],
        [
            tile(rows, width),
            tile(rows, cols * wide),
            tile(rows, width),
            pl.BlockSpec((1, 8, width), lambda i: (i, 0, 0)),
        ],
        4 * tokens * width * cols * wide,
    )


def ffn_backward_firsts(grad, dheads, unit, inverse, slope, shrink, expand, norms, outs):
    tokens, width = grad.shape
    segs = tokens // SEG
    few = 16
    cols = len(shrink[0])
    wide = shrink[0][0].shape[0]
    by_seg = [x.reshape(segs, SEG, -1) for x in (grad, unit, inverse, slope)]
    outs = [x.reshape(segs, SEG, -1) for x in outs]
    upstream = jnp.concatenate([dheads[:, None], by_seg[0][:, 1:few]], axis=1)

    def kernel(up_ref, unit_ref, inverse_ref, slope_ref, norm_ref, *refs):
        dffn_ref, dpre_ref, dhid_ref, sum_ref = refs[4 * cols + 3 :]
        count = segs * few
        upstream = up_ref[...].reshape(count, width)
        unit = unit_ref[...].reshape(count, width)

        def put(c, value):
            dpre_ref[:, :, c * wide : (c + 1) * wide] = value.reshape(segs, few, wide)

        dffn, dsecond, back = ffn_backward_values(
            upstream,
            unit,
            inverse_ref[...].reshape(count, 1),
            lambda c: slope_ref[:, :, c * wide : (c + 1) * wide].reshape(count, wide),
            norm_ref[2:3],
            refs[: 2 * cols],
            refs[2 * cols : 4 * cols],
            cols,
            put,
        )
        dffn_ref[...] = dffn.reshape(segs, few, width)
        dhid_ref[...] = (dsecond + back).reshape(segs, few, width)
        place = lax.broadcasted_iota(jnp.int32, (count, 1), 0)
        only = jnp.where(place % few == 0, upstream, 0.0)
        put_sums(sum_ref, column_sum(only * unit), column_sum(only), width)

    ins = [upstream] + by_seg[1:] + [norms] + flat(shrink) + flat(expand) + outs
    front = [
        pl.BlockSpec((segs, few, x.shape[2]), lambda i: (0, 0, 0)) for x in [upstream] + by_seg[1:]
    ]
    back_specs = [pl.BlockSpec((segs, few, x.shape[2]), lambda i: (0, 0, 0)) for x in outs]
    first_out = len(ins) - 3
    dffn, dpre, dhid, sums = run(
        kernel,
        (1,),
        ins,
        front
        + [whole_spec(x) for x in ins[4:first_out]]
        + [pl.BlockSpec(memory_space=pl.ANY)] * 3,
        [shape(*x.shape, kind=x.dtype) for x in outs] + [shape(1, 8, width, kind=jnp.float32)],
        back_specs + [pl.BlockSpec((1, 8, width), lambda i: (0, 0, 0))],
        4 * segs * few * width * cols * wide,
        {first_out + k: k for k in range(3)},
    )
    return [x.reshape(tokens, -1) for x in (dffn, dpre, dhid)] + [sums]


def attention_backward(dhid, unit, inverse, qkv, keep, project, merge, norms, group, rows, whole):
    tokens, width = dhid.shape
    cols = len(project[0])
    wide = project[0][0].shape[1]
    heads = wide // (3 * HDIM)

    def kernel(dhid_ref, unit_ref, inverse_ref, qkv_ref, keep_ref, norm_ref, *refs):
        project_refs, merge_refs = refs[: 2 * cols], refs[2 * cols : 4 * cols]
        datt_ref, dqkv_ref, dx_ref, sum_ref = refs[4 * cols : 4 * cols + 4]
        upstream = dhid_ref[...]
        unit = unit_ref[...]
        dfirst = kernel_norm_backward(upstream, unit, inverse_ref[...], norm_ref[0:1])
        put_sums(sum_ref, column_sum(upstream * unit), column_sum(upstream), width)
        datt = dfirst.astype(low_type)
        datt_ref[...] = datt
        back = dfirst if whole else None
        if not whole:
            refs[-1][...] = dfirst
        for c in range(cols):
            dmixed = dot_t(datt, across(merge_refs, cols)(c)).astype(low_type)
            blocks = []
            for g in range(rows // group):
                span = slice(g * group, (g + 1) * group)
                allowed = keep_ref[:, span] > 0.5
                parts = [head_parts(qkv_ref[c, span], head) for head in range(heads)]
                incoming = [
                    dmixed[span, head * HDIM : (head + 1) * HDIM] for head in range(heads)
                ]
                dprobs = [dot_t(some, part[2]) for some, part in zip(incoming, parts)]
                probs = softmax([part[:2] for part in parts], allowed)
                centres = [
                    jnp.sum(left * right, axis=1, keepdims=True)
                    for left, right in zip(dprobs, probs)
                ]
                dscores = [
                    (some * (left - centre)).astype(low_type)
                    for some, left, centre in zip(probs, dprobs, centres)
                ]
                pieces = []
                for some, dscore, up, part in zip(probs, dscores, incoming, parts):
                    pieces.append(dot(dscore, part[1]) * HDIM ** (-0.5))
                    pieces.append(dot_rows(dscore, part[0]) * HDIM ** (-0.5))
                    pieces.append(dot_rows(some.astype(low_type), up))
                blocks.append(jnp.concatenate(pieces, axis=1).astype(low_type))
            dqkv = blocks[0] if len(blocks) == 1 else jnp.concatenate(blocks, axis=0)
            dqkv_ref[c] = dqkv
            part = dot_t(dqkv, down(project_refs, cols)(c))
            back = part if back is None else back + part
        dx_ref[...] = back

    ins = [dhid, unit, inverse, qkv, keep, norms] + flat(project) + flat(merge)
    outs = [
        shape(tokens, width),
        shape(cols, tokens, wide),
        shape(tokens, width, kind=jnp.float32),
        shape(tokens // rows, 8, width, kind=jnp.float32),
    ]
    out_specs = [
        tile(rows, width),
        stack_tile(cols, rows, wide),
        tile(rows, width),
        pl.BlockSpec((1, 8, width), lambda i: (i, 0, 0)),
    ]
    if not whole:
        outs.append(shape(tokens, width, kind=jnp.float32))
        out_specs.append(tile(rows, width))
    return run(
        kernel,
        (tokens // rows,),
        ins,
        [
            tile(rows, width),
            tile(rows, width),
            tile(rows, 1),
            stack_tile(cols, rows, wide),
            pl.BlockSpec((1, rows), lambda i: (0, i)),
        ]
        + [whole_spec(x) for x in ins[5:]],
        outs,
        out_specs,
        2 * tokens * width * cols * wide + 10 * tokens * group * cols * heads * HDIM,
    )


def outer_middle(value, attended, expand, shrink, norms):
    tokens, width = value.shape
    cols = len(expand[0])
    wide = expand[0][0].shape[1]

    def kernel(value_ref, attended_ref, norm_ref, *refs):
        unit_ref, inverse_ref, low_ref, active_ref, slope_ref, ffn_ref = refs[4 * cols :]
        hid, unit, inverse = kernel_norm(
            value_ref[...] + attended_ref[...], norm_ref[0:1], norm_ref[1:2]
        )
        low = hid.astype(low_type)
        unit_ref[...] = unit
        inverse_ref[...] = inverse
        low_ref[...] = low
        for c in range(cols):
            span = slice(c * wide, (c + 1) * wide)
            active_ref[:, span], slope_ref[:, span] = gelu_and_slope(
                dot(low, down(refs[: 2 * cols], cols)(c))
            )
        ffn_ref[...] = shrink_values(active_ref[...], refs[2 * cols : 4 * cols], cols)

    ins = [value, attended, norms] + flat(expand) + flat(shrink)
    outs = [
        shape(tokens, width, kind=jnp.float32),
        shape(tokens, 1, kind=jnp.float32),
        shape(tokens, width),
        shape(tokens, cols * wide),
        shape(tokens, cols * wide),
        shape(tokens, width, kind=jnp.float32),
    ]
    return run(
        kernel,
        (1,),
        ins,
        [whole_spec(x) for x in ins],
        outs,
        [whole_spec(x) for x in outs],
        4 * tokens * width * cols * wide,
    )


def outer_turn(unit, ffn, grad, slope, shrink, expand, norms):
    tokens, width = unit.shape
    cols = len(expand[0])
    wide = expand[0][0].shape[1]

    def kernel(unit_ref, ffn_ref, grad_ref, slope_ref, norm_ref, *refs):
        out_ref, dffn_ref, dpre_ref, dsecond_ref, back_ref, sum_ref = refs[4 * cols :]
        hid = unit_ref[...] * norm_ref[0:1] + norm_ref[1:2]
        result, second, inverse = kernel_norm(hid + ffn_ref[...], norm_ref[2:3], norm_ref[3:4])
        out_ref[...] = result
        upstream = grad_ref[...]

        def put(c, value):
            dpre_ref[:, c * wide : (c + 1) * wide] = value

        dffn_ref[...], dsecond_ref[...], back_ref[...] = ffn_backward_values(
            upstream,
            second,
            inverse,
            lambda c: slope_ref[:, c * wide : (c + 1) * wide],
            norm_ref[2:3],
            refs[: 2 * cols],
            refs[2 * cols : 4 * cols],
            cols,
            put,
        )
        put_sums(sum_ref, column_sum(upstream * second), column_sum(upstream), width)

    ins = [unit, ffn, grad, slope, norms] + flat(shrink) + flat(expand)
    outs = [
        shape(tokens, width, kind=jnp.float32),
        shape(tokens, width),
        shape(tokens, cols * wide),
        shape(tokens, width, kind=jnp.float32),
        shape(tokens, width, kind=jnp.float32),
        shape(1, 8, width, kind=jnp.float32),
    ]
    return run(
        kernel,
        (1,),
        ins,
        [whole_spec(x) for x in ins],
        outs,
        [whole_spec(x) for x in outs],
        4 * tokens * width * cols * wide,
    )


def ffn_grads(hid_low, dpre, active, dffn):
    dp_count, col_count = lax.axis_size("dp"), lax.axis_size("col")
    half = hid_low.shape[1] // 2
    theirs_first = dot_rows(hid_low[:, half:], dpre).astype(low_type)
    theirs_second = dot_rows(active, dffn[:, half:]).astype(low_type)
    mine_first = dot_rows(hid_low[:, :half], dpre).astype(low_type)
    mine_second = dot_rows(active, dffn[:, :half]).astype(low_type)
    wide = mine_first.shape[1] // col_count
    tall = mine_second.shape[0] // col_count
    low, high = half // dp_count, tall // dp_count
    got_first, got_second = row_swap(theirs_first), row_swap(theirs_second)

    def kernel(*refs):
        ins, outs = refs[:8], refs[8:]
        for k in range(2):
            first = add_low(ins[2 * k][...], ins[2 * k + 1][...])
            second = add_low(ins[4 + 2 * k][...], ins[5 + 2 * k][...])
            for place in range(dp_count):
                part = first[place * low : (place + 1) * low]
                outs[k][0, place, :low] = part[:, :half]
                outs[k][0, place, low:] = part[:, half:]
                outs[2 + k][0, place] = second[place * high : (place + 1) * high]

    specs = (
        [pl.BlockSpec((half, wide), lambda i: (0, 2 * i))] * 2
        + [pl.BlockSpec((half, wide), lambda i: (0, 2 * i + 1))] * 2
        + [pl.BlockSpec((tall, half), lambda i: (i, 0))] * 2
        + [pl.BlockSpec((tall, half), lambda i: (i + 2, 0))] * 2
    )
    return pack_call(
        kernel,
        [mine_first, got_first] * 2 + [mine_second, got_second] * 2,
        specs,
        dp_count,
        (2 * low, high),
        half,
    )


def add_low(left, right):
    return (left.astype(jnp.float32) + right.astype(jnp.float32)).astype(low_type)


def pack_call(kernel, ins, specs, dp_count, heights, width):
    heights = [heights[0], heights[0], heights[1], heights[1]]
    return run(
        kernel,
        (2,),
        ins,
        specs,
        [shape(2, dp_count, height, width) for height in heights],
        [
            pl.BlockSpec((1, dp_count, height, width), lambda i: (i, 0, 0, 0))
            for height in heights
        ],
        0,
    )


def first_swaps(packed):
    keep_a, send_a, keep_b, send_b = packed
    got_a, got_b = col_swap(send_a, 1), col_swap(send_b, 2)

    def kernel(*refs):
        for half in range(2):
            total = add_low(refs[2 * half][...], refs[2 * half + 1][...])
            refs[4 + 2 * half][...] = total[0]
            refs[5 + 2 * half][...] = total[1]

    ins = [keep_a, got_a, keep_b, got_b]
    outs = [shape(*x.shape[1:]) for x in (keep_a, keep_a, keep_b, keep_b)]

    def spec(array):
        front = array.ndim - 3
        return pl.BlockSpec(
            (2,) * front + (1,) + array.shape[front + 1 :],
            lambda i: (0,) * front + (i, 0, 0),
        )

    return run(
        kernel, (keep_a.shape[1],), ins, [spec(x) for x in ins], outs, [spec(x) for x in outs], 0
    )


def second_swaps(sums):
    own_a, on_a, own_b, on_b = sums
    got_a, got_b = col_swap(on_a, 2), col_swap(on_b, 1)
    count, high_a, width = own_a.shape
    high_b = own_b.shape[1]

    def kernel(place_ref, *refs):
        for step in range(count):
            at = lax.rem(place_ref[0] + step, count)
            refs[4 + step][:high_a] = add_low(refs[0][at], refs[1][at])
            refs[4 + step][high_a:] = add_low(refs[2][at], refs[3][at])

    ins = [own_a, got_a, own_b, got_b]
    whole = pl.BlockSpec(memory_space=pltpu.VMEM)
    return pl.pallas_call(
        kernel,
        out_shape=[jax.ShapeDtypeStruct((high_a + high_b, width), low_type)] * count,
        grid_spec=pltpu.PrefetchScalarGridSpec(
            num_scalar_prefetch=1, grid=(), in_specs=[whole] * 4, out_specs=[whole] * count
        ),
        cost_estimate=pl.CostEstimate(
            flops=0, bytes_accessed=6 * count * (high_a + high_b) * width, transcendentals=0
        ),
        name="add_second",
    )(lax.axis_index("dp").reshape(1), *ins)


def rows_over(value):
    return col_swap(value, 2)


def dp_swaps(pieces):
    return [pieces[0]] + [dp_shift(piece, step) for step, piece in enumerate(pieces) if step]


def add_pieces(pieces):
    total = pieces[0].astype(jnp.float32)
    for piece in pieces[1:]:
        total = total + piece.astype(jnp.float32)
    return total


def row_products(left, right, part):
    cols, tokens, wide = right.shape
    half = left.shape[1] // 2

    def kernel(left_ref, right_ref, out_ref):
        out_ref[0] = dot_rows(left_ref[...], right_ref[0]).astype(low_type)

    return run(
        kernel,
        (cols,),
        [left, right],
        [
            pl.BlockSpec((tokens, half), lambda c: (0, part)),
            pl.BlockSpec((1, tokens, wide), lambda c: (c, 0, 0)),
        ],
        [shape(cols, half, wide)],
        [pl.BlockSpec((1, half, wide), lambda c: (c, 0, 0))],
        2 * tokens * half * cols * wide,
    )[0]


def attention_grads(x_low, dqkv, mixed, datt, ready):
    dp_count, col_count = lax.axis_size("dp"), lax.axis_size("col")
    half = x_low.shape[1] // 2
    wide = dqkv.shape[2]
    theirs_second = dot_rows(mixed, datt[:, half:]).astype(low_type)
    theirs_first = row_products(x_low, dqkv, 1)
    x_low, mixed = after((x_low, mixed), ready)
    mine_first = row_products(x_low, dqkv, 0)
    mine_second = dot_rows(mixed, datt[:, :half]).astype(low_type)
    got_first, got_second = row_swap(theirs_first), row_swap(theirs_second)
    tall = mine_second.shape[0] // col_count
    low, high = half // dp_count, tall // dp_count
    end_rows = low // 2
    assert (wide - half) * 2 == half

    def kernel(*refs):
        ins, outs = refs[:12], refs[12:]
        for k in range(2):
            first = add_low(ins[2 * k][0, :, :half], ins[2 * k + 1][0, :, :half])
            other = ins[4 + 2 * k][0, :, half:].astype(jnp.float32)
            other = other + ins[5 + 2 * k][0, :, half:].astype(jnp.float32)
            second = add_low(ins[8 + 2 * k][...], ins[9 + 2 * k][...])
            for place in range(dp_count):
                outs[k][0, place] = first[place * low : (place + 1) * low]
                ends = other[place * low : (place + 1) * low]
                outs[2 + k][0, place, :end_rows] = jnp.concatenate(
                    [ends[:end_rows], ends[end_rows:]], axis=1
                ).astype(low_type)
                outs[2 + k][0, place, end_rows:] = second[place * high : (place + 1) * high]

    def blocks(index):
        return [pl.BlockSpec((1, half, wide), lambda i: (index(i), 0, 0))] * 2

    specs = (
        blocks(lambda i: 2 * i)
        + blocks(lambda i: 2 * i + 1)
        + blocks(lambda i: i)
        + blocks(lambda i: i + 2)
        + [pl.BlockSpec((tall, half), lambda i: (i, 0))] * 2
        + [pl.BlockSpec((tall, half), lambda i: (i + 2, 0))] * 2
    )
    return pack_call(
        kernel,
        [mine_first, got_first] * 4 + [mine_second, got_second] * 2,
        specs,
        dp_count,
        (low, end_rows + high),
        half,
    )


def unpack_ffn(packed, low):
    return jnp.concatenate([packed[:low], packed[low : 2 * low]], axis=1), packed[2 * low :]


def unpack_attention(packed, low):
    half = packed.shape[1] // 2
    ends = packed[low : low + low // 2]
    ends = jnp.concatenate([ends[:, :half], ends[:, half:]], axis=0)
    return jnp.concatenate([packed[:low], ends], axis=1), packed[low + low // 2 :]


def halves(value, axis):
    return jnp.split(value, 2, axis=axis)


def first_grad(left, right, through):
    mine_left, theirs_left = halves(left, 1)
    theirs = [dot_rows(theirs_left, block).astype(low_type) for block in right]
    mine = [dot_rows(mine_left, block).astype(low_type) for block in right]
    return scatter_grad(mine, theirs, through)


def second_grad(left, right, through):
    mine_right, theirs_right = halves(right, 1)
    count = lax.axis_size("col")
    theirs = dot_rows(left, theirs_right).astype(low_type)
    mine = dot_rows(left, mine_right).astype(low_type)
    got = row_swap(theirs)
    total = mine.astype(jnp.float32) + got.astype(jnp.float32)
    return dp_scatter_sum(plane_sum(jnp.split(total, count, 0), through))


def to_tokens(value, row):
    parts = value.reshape((2, -1) + value.shape[1:])
    mine = lax.dynamic_index_in_dim(parts, row, 0, False)
    theirs = lax.dynamic_index_in_dim(parts, 1 - row, 0, False)
    return jnp.concatenate([mine, row_swap(theirs)], axis=1)


def to_features(value, row):
    mine, theirs = halves(value, 1)
    got = row_swap(theirs)
    first = jnp.where(row == 0, mine, got)
    second = jnp.where(row == 0, got, mine)
    return jnp.concatenate([first, second], axis=0)


def swap_features(value):
    first, second = halves(value, 1)
    return jnp.concatenate([second, first], axis=1)


def swap_rows(value):
    first, second = halves(value, 0)
    return jnp.concatenate([second, first], axis=0)


def layer(
    hidden,
    lengths,
    inner_project,
    inner_merge,
    inner_expand,
    inner_shrink,
    inner_norms,
    outer_places,
    outer_project,
    outer_merge,
    outer_expand,
    outer_shrink,
    outer_norms,
    out_grad,
):
    dp_count, row_count, col_count = (lax.axis_size(name) for name in ("dp", "row", "col"))
    dp, row, col = (lax.axis_index(name) for name in ("dp", "row", "col"))
    everyone = ("dp", "row", "col")
    device_count = dp_count * row_count * col_count
    value = to_tokens(hidden, row)
    grad_in = to_tokens(out_grad, row)
    tokens, width = value.shape
    segs = tokens // SEG

    small = jnp.concatenate([inner_norms, outer_norms, outer_places], axis=1)
    small = lax.all_to_all(
        jnp.broadcast_to(small[None], (device_count,) + small.shape), everyone, 0, 0, tiled=True
    )
    small_got = small
    small = small.reshape((dp_count, row_count, -1) + small.shape[2:])
    small = jnp.concatenate(
        [
            lax.dynamic_index_in_dim(small, row, 1, False).reshape(-1, small.shape[-1]),
            lax.dynamic_index_in_dim(small, 1 - row, 1, False).reshape(-1, small.shape[-1]),
        ],
        axis=0,
    )
    vectors = small.T
    inner_gains = vectors[0:4]
    outer_gains = vectors[4:8]
    places = vectors[8:]

    length = lax.dynamic_index_in_dim(lengths, col // 2, 0, False)
    half = col % 2
    seg_own = (half * 2 + row) * segs + jnp.arange(segs, dtype=jnp.int32)
    spot = (seg_own[:, None] * SEG + jnp.arange(SEG, dtype=jnp.int32)[None]).reshape(tokens)
    valid = (spot < length).astype(jnp.float32)
    keep_tok = ((spot < length) | (spot % SEG == 0)).astype(jnp.float32)
    seg_all = jnp.concatenate(
        [
            (h * 2 + r) * segs + jnp.arange(segs, dtype=jnp.int32)
            for h in (half, 1 - half)
            for r in (row, 1 - row)
        ]
    )
    keep_seg = (seg_all * SEG < length).astype(jnp.float32)
    one_hot = (seg_own[:, None] == jnp.arange(NSEG, dtype=jnp.int32)[None]).astype(jnp.float32)

    keep_row = keep_tok[None]
    rows_tile = 2 * SEG
    inner, outer_steps, (x_in, qkv, mixed_in) = gather_weights(
        (inner_project, inner_merge, inner_expand, inner_shrink),
        (outer_project, outer_merge, outer_expand, outer_shrink),
        lambda project: project_attend(value, keep_row, project, None, SEG, rows_tile),
        small_got,
    )
    unit_one, inverse_one, hid_in, active_in, slope = merge_expand(
        value, mixed_in, inner[1], inner[2], inner_gains, rows_tile
    )
    outer_project = outer_steps[0](hid_in)
    inner_out, unit_two, inverse_two = shrink_norm(
        unit_one, active_in, inner[3], inner_gains, rows_tile
    )
    outer_merge, outer_shrink = outer_steps[1](inner_out)
    grid = inner_out.reshape(segs, SEG, width)
    masked_grad = (grad_in * valid[:, None]).reshape(segs, SEG, width)
    heads_in = grid[:, 0] + jnp.dot(
        one_hot, places, precision=highest, preferred_element_type=jnp.float32
    )
    rows = jnp.concatenate([heads_in, masked_grad[:, 0]], axis=0)
    rows = jnp.stack([rows, swap_features(row_swap(rows))]).reshape(2, 2, segs, width)
    rows = jnp.stack([rows, col_swap(rows, 1)])
    rows = rows.transpose(2, 0, 1, 3, 4).reshape(2, NSEG, width)

    def join(partial_sum):
        return partial_sum + swap_rows(col_swap(partial_sum, 1))

    flat_grad = masked_grad.reshape(tokens, width)
    main = ffn_backward(
        flat_grad, unit_two, inverse_two, slope, inner[3], inner[2], inner_gains, rows_tile
    )
    outer_expand = outer_steps[2](main[3])
    outer = (outer_project, outer_merge, outer_expand, outer_shrink)
    rows = after(rows, main[3])
    x_low, o_qkv, mixed, attended = project_attend(
        rows[0], keep_seg[None], outer[0], outer[1], NSEG, NSEG
    )
    o_unit, o_inverse, hid_low, active, o_slope, ffn = outer_middle(
        rows[0], join(attended), outer[2], outer[3], outer_gains
    )
    outer_out, dffn, dpre, dsecond, back, o_second = outer_turn(
        o_unit, join(ffn), rows[1], o_slope, outer[3], outer[2], outer_gains
    )
    datt, dqkv, back, o_first, dfirst = attention_backward(
        dsecond + join(back),
        o_unit,
        o_inverse,
        o_qkv,
        keep_seg[None],
        outer[0],
        outer[1],
        outer_gains,
        NSEG,
        NSEG,
        False,
    )
    dheads = dfirst + join(back)
    outer_norm_grad = jnp.concatenate([o_first[0, :2], o_second[0, :2]], axis=0).T
    dheads = dheads[:segs]
    places_grad = jnp.dot(dheads.T, one_hot, precision=highest, preferred_element_type=jnp.float32)

    dffn_in, dpre_in, dhid_in, few_sums = ffn_backward_firsts(
        flat_grad,
        dheads,
        unit_two,
        inverse_two,
        slope,
        inner[3],
        inner[2],
        inner_gains,
        main[:3],
    )
    wide_dp = dp_count > 4
    if not wide_dp:
        ffn_packed = ffn_grads(hid_in, dpre_in, active_in, dffn_in)
        dhid_in = after(dhid_in, ffn_packed[0])
    datt_in, dqkv_in, input_grad, first_sums = attention_backward(
        dhid_in,
        unit_one,
        inverse_one,
        qkv,
        keep_row,
        inner[0],
        inner[1],
        inner_gains,
        SEG,
        rows_tile,
        True,
    )
    if wide_dp:
        inner_grads = (
            first_grad(x_in, dqkv_in, 1),
            second_grad(mixed_in, datt_in, 2),
            first_grad(hid_in, jnp.split(dpre_in, col_count, 1), 1),
            second_grad(active_in, dffn_in, 2),
        )
        gate = None
    else:
        ffn_sums = first_swaps(ffn_packed)
        attention_packed = attention_grads(x_in, dqkv_in, mixed_in, datt_in, ffn_sums[0])
        ffn_pieces = second_swaps(ffn_sums)
        gate = attention_packed[0]
    shared = [halves(part, 1)[0] for part in (x_low, hid_low, datt, dffn)]
    own, over = zip(*([halves(part, 1) for part in (active, dpre, mixed)] + [tuple(dqkv)]))
    packed = jnp.concatenate(
        [
            jnp.concatenate(shared + list(own), axis=1),
            rows_over(jnp.concatenate(shared + list(over), axis=1)),
        ],
        axis=0,
    )
    if dp_count > 4:
        packed = lax.all_gather(packed, "dp", axis=0, tiled=True)
    else:
        got = [dp_shift(packed, step) for step in range(1, dp_count)]
        packed = [packed] + got
    late = (outer_out, grid, first_sums, main[3])
    if gate is not None:
        late = after(late, gate)
    late_outer, late_inner, late_first, late_main = late
    layer_out = (
        jnp.concatenate([late_outer[:segs, None], late_inner[:, 1:]], axis=1).reshape(tokens, width)
        * valid[:, None]
    )
    inner_norm_grad = jnp.concatenate(
        [jnp.sum(late_first, 0)[:2], jnp.sum(late_main, 0)[:2] + few_sums[0, :2]], axis=0
    ).T
    small_grad = jnp.concatenate([inner_norm_grad, 0.25 * outer_norm_grad, places_grad], axis=1)
    if gate is not None:
        small_grad = after(small_grad, gate)
    columns = small_grad.shape[1]
    blocks = small_grad.reshape(2, dp_count, col_count, -1, columns)
    blocks = jnp.where(row == 0, blocks, blocks[::-1]).transpose(1, 0, 2, 3, 4)
    blocks = lax.all_to_all(blocks.reshape(device_count, -1, columns), everyone, 0, 0, tiled=True)
    small_sum = jnp.sum(blocks, axis=0)
    if not wide_dp:
        attention_sums = first_swaps(attention_packed)
        ffn_got = dp_swaps(after(ffn_pieces, small_sum))
        attention_pieces = second_swaps(after(attention_sums, small_sum))
        attention_total = add_pieces(dp_swaps(attention_pieces))
        ffn_total = add_pieces(after(ffn_got, attention_pieces))
        inner_grads = unpack_attention(attention_total, inner_expand.shape[0]) + unpack_ffn(
            ffn_total, inner_expand.shape[0]
        )
    if not wide_dp:
        packed = jnp.concatenate(after(packed, attention_pieces), axis=0)
    ends = []
    for part in shared + list(own):
        ends.append((ends[-1] if ends else 0) + part.shape[1])
    x_all, hid_all, datt_all, dffn_all, active_all, dpre_all, mixed_all, dqkv_all = jnp.split(
        packed, ends[:-1], axis=1
    )

    def own_rows(product):
        return lax.dynamic_index_in_dim(
            product.reshape((dp_count, -1) + product.shape[1:]), dp, 0, False
        )

    outer_grads = (
        own_rows(dot_rows(x_all, dqkv_all)),
        own_rows(dot_rows(mixed_all, datt_all)),
        own_rows(dot_rows(hid_all, dpre_all)),
        own_rows(dot_rows(active_all, dffn_all)),
    )

    return (
        to_features(layer_out, row),
        to_features(input_grad, row),
        inner_grads[0],
        inner_grads[1],
        inner_grads[2],
        inner_grads[3],
        small_sum[:, 0:4],
        small_sum[:, 8:],
        outer_grads[0],
        outer_grads[1],
        outer_grads[2],
        outer_grads[3],
        small_sum[:, 4:8],
    )


def solution(mesh):
    tokens = P(("dp", "col"), "row")
    first = P(("row", "dp"), "col")
    second = P(("col", "dp"), "row")
    small = P(("row", "dp", "col"), None)
    weights = (first, second, first, second)
    return jax.shard_map(
        layer,
        mesh=mesh,
        in_specs=(tokens, P("dp")) + weights + (small, small) + weights + (small, tokens),
        out_specs=(tokens, tokens) + weights + (small, small) + weights + (small,),
        check_vma=False,
    )
```
